128 devices in a mesh: cuts: 8 (over x, core), tile: 16 (over z, y).
Axes of the slice: x: 4, y: 4, z: 4, core: 2. Of those that a mesh axis runs over, the one named last changes fastest.
Arguments:
- acquired: bfloat16 [2097152, 256], P(('cuts', 'tile')), may hold values from -6 to 6
- stencil: bfloat16 [4096, 1024], P('tile'), may hold values from -0.03125 to 0.03125
- send_slots: int32 [128, 16, 1280], P(('cuts', 'tile')), may hold values from 0 to 16383
- send_lines: int32 [128, 16, 1280], P(('cuts', 'tile')), may hold values from 0 to 2047
- send_counts: int32 [128, 16], P(('cuts', 'tile')), may hold values from 1 to 1280, as said below
- return_slots: int32 [128, 16, 128], P(('cuts', 'tile')), may hold values from 0 to 255
- return_counts: int32 [128, 16], P(('cuts', 'tile')), may hold values from 1 to 128, as said below
Outputs:
- field_out: bfloat16 [128, 256, 256], P(('cuts', 'tile'))
- returned: bfloat16 [2048, 128, 256], P(('cuts', 'tile'))
The draws below stay inside these ranges and needn't reach their ends.
Inputs may be any that keep to these rules, and one draw needn't show every extreme that they name: `send_counts`: some tile receives 1280 rows from every device. `return_counts`: some reader tile receives 128 lines from every owner.
All inputs are finite; a program needn't handle non-finite values.
Results may differ from the reference program's by a relative error of at most 0.00075.
Values may be sent and summed in bfloat16 or wider, within the bound.
No kernel may reach another device: no remote copies, remote signals or barrier semaphores. Data moves between devices by JAX's collectives and lax.ppermute only.
A program may use at most 192 MiB of HBM per device.

```python
import jax
import jax.numpy as jnp
from jax import lax

NX = 256
NY = 256
TAPS = 4
ITERS = 2
ZDEV = 1
ROWS_DEV = 16384
CAP = 1280
RCAP = 128
NZ = 128
ACQ = 2097152
N_CUTS = 8
N_TILE = 16


def skewed_counts(key, rows_total, cols_total, most):
    rank = jax.random.permutation(jax.random.fold_in(key, 11), cols_total)
    high = jnp.where(rank % 4 == 0, most, most // (1 + rank % 4)) + 1
    low = max(1, most // 8)
    drawn = jax.random.randint(jax.random.fold_in(key, 12), (rows_total, cols_total), low, high[None, :])
    return jnp.where(rank[None, :] == 0, most, drawn).astype(jnp.int32)


def draw_send_counts(key, part):
    return skewed_counts(key, N_CUTS * N_TILE, N_TILE, CAP)


def draw_return_counts(key, part):
    return skewed_counts(jax.random.fold_in(key, 5), N_CUTS * N_TILE, N_TILE, RCAP)


def plant(result, stream_key, low, top_value):
    spot = [jax.random.randint(jax.random.fold_in(stream_key, axis), (), 0, length) for axis, length in enumerate(result.shape)]
    main_axis = result.shape.index(max(result.shape))
    beside = spot[:main_axis] + [(spot[main_axis] + 1) % result.shape[main_axis]] + spot[main_axis + 1:]
    return result.at[tuple(spot)].set(low).at[tuple(beside)].set(top_value)


def level_of(own_key, dims, cuts, smallest, high):
    gain, own = 1.0, jax.random.fold_in(own_key, 6)
    for dim, shards_of in cuts:
        steps = jnp.exp(jax.random.uniform(jax.random.fold_in(own, dim), (shards_of,), jnp.float32, smallest / len(cuts), high / len(cuts)))
        gain = gain * jnp.repeat(steps, dims[dim] // shards_of).reshape([-1 if axis == dim else 1 for axis in range(len(dims))])
    return gain


def centred(stream_key, extent, width, limit, cuts=(), held_as=jnp.bfloat16):
    array = width * jax.random.normal(stream_key, extent, jnp.float32)
    if cuts:
        array = array * level_of(stream_key, extent, cuts, -0.22, 0.18)
    return jnp.clip(array, -limit, limit).astype(held_as)


def setup_inputs(seed: int = 0) -> dict:
    key_list = jax.random.split(jax.random.key(seed), 8)
    acquired = centred(key_list[0], (ACQ, NX), 1.0, 6.0, ((0, 128),))
    stencil = centred(key_list[1], (N_TILE * NX, TAPS * NX), (NX * N_TILE * CAP * 2 // (ZDEV * NY)) ** -0.5, 0.03125, ((0, 16),))
    send_slots = plant(jax.random.randint(key_list[2], (N_CUTS * N_TILE, N_TILE, CAP), 0, ROWS_DEV), jax.random.fold_in(key_list[2], 1), 0, ROWS_DEV - 1).astype(jnp.int32)
    send_lines = plant(jax.random.randint(key_list[3], (N_CUTS * N_TILE, N_TILE, CAP), 0, N_CUTS * ZDEV * NY), jax.random.fold_in(key_list[3], 1), 0, (N_CUTS * ZDEV * NY) - 1).astype(jnp.int32)
    send_counts = draw_send_counts(jax.random.fold_in(key_list[7], 71), 0)
    return_slots = plant(jax.random.randint(key_list[5], (N_CUTS * N_TILE, N_TILE, RCAP), 0, ZDEV * NY), jax.random.fold_in(key_list[5], 1), 0, (ZDEV * NY) - 1).astype(jnp.int32)
    return_counts = draw_return_counts(jax.random.fold_in(key_list[7], 71), 0)
    return dict(acquired=acquired, stencil=stencil, send_slots=send_slots, send_lines=send_lines, send_counts=send_counts, return_slots=return_slots, return_counts=return_counts)


def neighbour_sum(inner):
    zpad = jnp.pad(inner, ((1, 1), (0, 0), (0, 0)))
    ypad = jnp.pad(inner, ((0, 0), (1, 1), (0, 0)))
    xpad = jnp.pad(inner, ((0, 0), (0, 0), (1, 1)))
    return zpad[2:] + zpad[:-2] + ypad[:, 2:] + ypad[:, :-2] + xpad[:, :, 2:] + xpad[:, :, :-2]


def reference(acquired, stencil, send_slots, send_lines, send_counts, return_slots, return_counts):
    devices_all = N_CUTS * N_TILE
    rows_all = acquired.reshape(devices_all, ROWS_DEV, NX)
    stencils = stencil.reshape(N_TILE, NX, TAPS * NX).astype(jnp.float32)
    slot_index = jnp.arange(CAP, dtype=jnp.int32)
    tap_offsets = jnp.arange(TAPS, dtype=jnp.int32)
    tile_ids = jnp.arange(N_TILE, dtype=jnp.int32)

    def add_source(raw_field, source_item):
        src_rows, slots, line_ids, counts = source_item
        usable = slot_index[None, :] < counts[:, None]
        picked = src_rows[slots]
        picked = jnp.where(usable[:, :, None], picked, jnp.zeros_like(picked)).astype(jnp.float32)
        terms = jnp.einsum("tcr,trk->tck", picked, stencils, precision=lax.Precision.HIGHEST)
        cut_ids = line_ids // (ZDEV * NY)
        plane_ids = (line_ids // NY) % ZDEV
        row_in_plane = line_ids % NY
        depth = (cut_ids * N_TILE + tile_ids[:, None]) * ZDEV + plane_ids
        target = depth[:, :, None] * NY + (row_in_plane[:, :, None] + tap_offsets) % NY
        raw_field = raw_field.at[target.reshape(-1)].add(terms.reshape(-1, NX))
        return raw_field, None

    raw_field = jnp.zeros((NZ * NY, NX), jnp.float32)
    raw_field, _ = lax.scan(add_source, raw_field, (rows_all, send_slots, send_lines, send_counts))
    smooth_field = raw_field.reshape(NZ, NY, NX)
    for sweep in range(ITERS):
        smooth_field = smooth_field + 0.15 * (neighbour_sum(smooth_field) - 6.0 * smooth_field)
    field_out = smooth_field.astype(jnp.bfloat16)
    per_device = field_out.reshape(devices_all, ZDEV * NY, NX)
    fetched = jax.vmap(lambda dev_field, read_ids: dev_field[read_ids])(per_device, return_slots)
    read_index = jnp.arange(RCAP, dtype=jnp.int32)
    usable_back = read_index[None, None, :] < return_counts[:, :, None]
    fetched = jnp.where(usable_back[..., None], fetched, jnp.zeros_like(fetched))
    returned = fetched.reshape(N_CUTS, N_TILE, N_TILE, RCAP, NX).transpose(0, 2, 1, 3, 4)
    returned = returned.reshape(devices_all * N_TILE, RCAP, NX)
    return field_out, returned
```

```python
import functools
import math

import jax
import jax.numpy as jnp
from jax import lax
from jax.experimental import pallas as pl
from jax.experimental.pallas import tpu as pltpu
from jax.sharding import PartitionSpec as P

NX = 256
NY = 256
TAPS = 4
HALF = 128
ALPHA = math.log(2.0) / 64.0
TOP = 32700.0
CHUNK = 256


def params(mib):
    return pltpu.CompilerParams(
        vmem_limit_bytes=mib * 1024 * 1024, dimension_semantics=("arbitrary",)
    )


def encode(block):
    top = jnp.max(jnp.abs(block), axis=1, keepdims=True)
    code = jnp.ceil(jnp.log(jnp.maximum(top, 1e-33)) * (1.0 / ALPHA))
    values = block * (TOP / jnp.exp(code * ALPHA))
    values = jnp.round(values).astype(jnp.int32).astype(jnp.int16)
    return values, code


def eye(size):
    return lax.broadcasted_iota(jnp.int32, (size, size), 0) == lax.broadcasted_iota(
        jnp.int32, (size, size), 1
    )


def to_row(column):
    return jnp.sum(jnp.where(eye(HALF), column, 0.0), axis=0, keepdims=True)


def to_column(row):
    return jnp.sum(jnp.where(eye(HALF), row, 0.0), axis=1, keepdims=True)


def decode(values, code_row):
    scale = jnp.exp(code_row * ALPHA) * (1.0 / TOP)
    return values.astype(jnp.int32).astype(jnp.float32) * to_column(scale)


def code_block(rows):
    block = jnp.zeros((16, NX), jnp.float32)
    index = lax.broadcasted_iota(jnp.int32, (16, NX), 0)
    for i, row in enumerate(rows):
        block = jnp.where(index == i, row, block)
    return block.astype(jnp.int32).astype(jnp.int16)


def gather_kernel(slots_ref, counts_ref, acq_ref, out_ref, wide_ref, stage_ref):
    step = pl.program_id(0)
    rows = acq_ref.shape[0]

    @pl.when(step == 0)
    def _():
        def widen(i, carry):
            base = pl.multiple_of(i * 64, 64)
            x = acq_ref[pl.ds(base, 64), :].astype(jnp.float32)
            wide_ref[pl.ds(base, 64), 0, :] = x[:, :128]
            wide_ref[pl.ds(base, 64), 1, :] = x[:, 128:]
            return carry

        lax.fori_loop(0, rows // 64, widen, 0)
        stage_ref[...] = jnp.zeros(stage_ref.shape, jnp.float32)

    count = counts_ref[step]

    def pick(i, carry):
        base = i * 16
        for u in range(16):
            stage_ref[base + u] = wide_ref[slots_ref[step, base + u]]
        return carry

    lax.fori_loop(0, (count + 15) // 16, pick, 0)

    def narrow(i, carry):
        base = pl.multiple_of(i * CHUNK, CHUNK)
        out_ref[0, pl.ds(base, CHUNK), 0:128] = stage_ref[pl.ds(base, CHUNK), 0, :].astype(jnp.bfloat16)
        out_ref[0, pl.ds(base, CHUNK), 128:256] = stage_ref[pl.ds(base, CHUNK), 1, :].astype(jnp.bfloat16)
        return carry

    lax.fori_loop(0, (count + CHUNK - 1) // CHUNK, narrow, 0)


def gather_rows(acquired, slots, counts):
    tiles, cap = slots.shape
    return pl.pallas_call(
        gather_kernel,
        grid_spec=pltpu.PrefetchScalarGridSpec(
            num_scalar_prefetch=2,
            grid=(tiles,),
            in_specs=[pl.BlockSpec(acquired.shape, lambda t, s, c: (0, 0))],
            out_specs=pl.BlockSpec((1, cap, NX), lambda t, s, c: (t, 0, 0)),
            scratch_shapes=[
                pltpu.VMEM((acquired.shape[0], 2, 128), jnp.float32),
                pltpu.VMEM((cap, 2, 128), jnp.float32),
            ],
        ),
        out_shape=jax.ShapeDtypeStruct((tiles, cap, NX), jnp.bfloat16),
        compiler_params=params(48),
        name="gather_rows",
    )(slots, counts, acquired)


def lines_kernel(
    own_n, peer_n, own_ref, peer_ref, own_lines, peer_lines, alias_ref,
    a0_ref, a1_ref, a2_ref, a3_ref, b_ref, acc_ref, code_ref,
):
    step = pl.program_id(0)
    last = pl.num_programs(0) - 1
    acc_ref[...] = jnp.zeros(acc_ref.shape, jnp.float32)
    position = lax.broadcasted_iota(jnp.int32, (CHUNK, CHUNK), 0)

    def add(rows_ref, lines_ref):
        def body(i, carry):
            base = pl.multiple_of(i * CHUNK, CHUNK)
            rows = rows_ref[0, pl.ds(base, CHUNK), :]
            ids = lines_ref[0, pl.ds(i, 1), :]
            for m in range(acc_ref.shape[0] // CHUNK):
                hot = jnp.where(position + m * CHUNK == ids, 1.0, 0.0).astype(jnp.bfloat16)
                span = pl.ds(m * CHUNK, CHUNK)
                acc_ref[span, :] += jnp.dot(hot, rows, preferred_element_type=jnp.float32)
            return carry

        return body

    lax.fori_loop(0, (own_n[step] + CHUNK - 1) // CHUNK, add(own_ref, own_lines), 0)
    lax.fori_loop(0, (peer_n[step] + CHUNK - 1) // CHUNK, add(peer_ref, peer_lines), 0)

    outs = (a0_ref, a1_ref, a2_ref, a3_ref)
    tiles = a0_ref.shape[0] // HALF
    for k in range(4):
        values, code = encode(acc_ref[pl.ds(k * HALF, HALF), :])
        outs[k][pl.ds(pl.multiple_of(step * HALF, HALF), HALF), :] = values
        row = to_row(code)
        code_ref[k, pl.ds(step, 1), :] = row

    codes = []
    for k in range(4):
        values, code = encode(acc_ref[pl.ds(512 + k * HALF, HALF), :])
        b_ref[0, pl.ds(k * HALF, HALF), :] = values
        codes.append(to_row(code))
    b_ref[0, pl.ds(512, 16), :] = code_block(
        [jnp.concatenate(codes[0:2], axis=1), jnp.concatenate(codes[2:4], axis=1)]
    )

    @pl.when(step == last)
    def _():
        for k in range(4):
            first = code_ref[k]
            both = jnp.concatenate([first, jnp.zeros_like(first)], axis=1)
            both = jnp.concatenate([both, jnp.zeros_like(both)], axis=0)
            outs[k][pl.ds(last * HALF + HALF, 16), :] = both.astype(jnp.int32).astype(jnp.int16)


def line_blocks(own_rows, peer_rows, own_lines, peer_lines, own_n, peer_n, b_old, first, tiles_all):
    tiles, cap, _ = own_rows.shape
    span = cap // CHUNK
    row_spec = pl.BlockSpec((1, cap, NX), lambda t, *_: (t, 0, 0))
    line_spec = pl.BlockSpec((1, span, CHUNK), lambda t, *_: (t, 0, 0))
    a_shape = (tiles * HALF + 16, NX)
    args = [own_n, peer_n, own_rows, peer_rows, own_lines, peer_lines]
    aliases = {}
    if b_old is None:
        b_old = jnp.zeros((16, NX), jnp.int16)
    else:
        aliases = {6: 4}
    args.append(b_old)
    return pl.pallas_call(
        lines_kernel,
        grid_spec=pltpu.PrefetchScalarGridSpec(
            num_scalar_prefetch=2,
            grid=(tiles,),
            in_specs=[row_spec, row_spec, line_spec, line_spec, pl.BlockSpec(memory_space=pl.ANY)],
            out_specs=[pl.BlockSpec(a_shape, lambda t, *_: (0, 0))] * 4
            + [pl.BlockSpec((1, 4 * HALF + 16, NX), lambda t, *_: (t + first, 0, 0))],
            scratch_shapes=[
                pltpu.VMEM((8 * HALF, NX), jnp.float32),
                pltpu.VMEM((4, 8, HALF), jnp.float32),
            ],
        ),
        out_shape=[jax.ShapeDtypeStruct(a_shape, jnp.int16)] * 4
        + [jax.ShapeDtypeStruct((tiles_all, 4 * HALF + 16, NX), jnp.int16)],
        input_output_aliases=aliases,
        compiler_params=params(48),
        name="line_blocks",
    )(*args)


def sum_x_kernel(p0, p1, p2, p3, c0, c1, c2, c3, alias_ref, out_ref):
    step = pl.program_id(0)
    total = jnp.zeros((HALF, NX), jnp.float32)
    index = lax.broadcasted_iota(jnp.int32, (16, HALF), 0)
    for values, codes in ((p0, c0), (p1, c1), (p2, c2), (p3, c3)):
        table = codes[:, 0:HALF].astype(jnp.int32).astype(jnp.float32)
        row = jnp.sum(jnp.where(index == step, table, 0.0), axis=0, keepdims=True)
        total = total + decode(values[...], row)
    values, code = encode(total)
    out_ref[0, pl.ds(0, HALF), :] = values
    row = to_row(code)
    out_ref[0, pl.ds(HALF, 16), :] = code_block([jnp.concatenate([row, row], axis=1)])


def sum_x(parts, old, first, tiles_all):
    tiles = (parts[0].shape[0] - 16) // HALF
    aliases = {}
    if old is None:
        old = jnp.zeros((16, NX), jnp.int16)
    else:
        aliases = {8: 0}
    return pl.pallas_call(
        sum_x_kernel,
        grid=(tiles,),
        in_specs=[pl.BlockSpec((HALF, NX), lambda t: (t, 0))] * 4
        + [pl.BlockSpec((16, NX), lambda t: (tiles * HALF // 16, 0))] * 4
        + [pl.BlockSpec(memory_space=pl.ANY)],
        out_specs=pl.BlockSpec((1, HALF + 16, NX), lambda t: (t + first, 0, 0)),
        out_shape=jax.ShapeDtypeStruct((tiles_all, HALF + 16, NX), jnp.int16),
        input_output_aliases=aliases,
        compiler_params=params(32),
        name="sum_x",
    )(*parts, *parts, old)


def sum_tile_kernel(in_ref, o0, o1, o2, o3, acc_ref):
    step = pl.program_id(0)
    table = in_ref[0, pl.ds(4 * HALF, 16), :].astype(jnp.int32).astype(jnp.float32)
    for k in range(4):
        row = table[k // 2 : k // 2 + 1, (k % 2) * HALF : (k % 2) * HALF + HALF]
        part = decode(in_ref[0, pl.ds(k * HALF, HALF), :], row)
        old = jnp.where(step == 0, jnp.zeros_like(part), acc_ref[pl.ds(k * HALF, HALF), :])
        acc_ref[pl.ds(k * HALF, HALF), :] = old + part

    @pl.when(step == pl.num_programs(0) - 1)
    def _():
        for k, out in enumerate((o0, o1, o2, o3)):
            values, code = encode(acc_ref[pl.ds(k * HALF, HALF), :])
            out[pl.ds(0, HALF), :] = values
            row = to_row(code)
            out[pl.ds(HALF, 16), :] = code_block([jnp.concatenate([row, row], axis=1)])


def sum_tile(arrived):
    tiles, rows, _ = arrived.shape
    out_shape = (HALF + 16, NX)
    return pl.pallas_call(
        sum_tile_kernel,
        grid=(tiles,),
        in_specs=[pl.BlockSpec((1, rows, NX), lambda t: (t, 0, 0))],
        out_specs=[pl.BlockSpec(out_shape, lambda t: (0, 0))] * 4,
        out_shape=[jax.ShapeDtypeStruct(out_shape, jnp.int16)] * 4,
        scratch_shapes=[pltpu.VMEM((4 * HALF, NX), jnp.float32)],
        compiler_params=params(32),
        name="sum_tile",
    )(arrived)


def first_code(block):
    return block[0:1, 0:HALF].astype(jnp.int32).astype(jnp.float32)


def plane_kernel(a_ref, b0, b1, b2, b3, stencil_ref, plane_ref, send_ref, lines_ref):
    def body(i, carry):
        return carry + decode(a_ref[i, pl.ds(0, HALF), :], first_code(a_ref[i, pl.ds(HALF, 16), :]))

    lines_ref[pl.ds(0, HALF), :] = lax.fori_loop(
        0, a_ref.shape[0], body, jnp.zeros((HALF, NX), jnp.float32)
    )
    total = jnp.zeros((HALF, NX), jnp.float32)
    for b in (b0, b1, b2, b3):
        total = total + decode(b[pl.ds(0, HALF), :], first_code(b[pl.ds(HALF, 16), :]))
    lines_ref[pl.ds(HALF, HALF), :] = total

    lines = lines_ref[...]
    high = lines.astype(jnp.bfloat16)
    rest = lines - high.astype(jnp.float32)
    mid = rest.astype(jnp.bfloat16)
    low = (rest - mid.astype(jnp.float32)).astype(jnp.bfloat16)
    plane = jnp.zeros((NY, NX), jnp.float32)
    for k in range(TAPS):
        weights = stencil_ref[:, k * NX : (k + 1) * NX]
        product = jnp.dot(high, weights, preferred_element_type=jnp.float32)
        product += jnp.dot(mid, weights, preferred_element_type=jnp.float32)
        product += jnp.dot(low, weights, preferred_element_type=jnp.float32)
        if k:
            product = pltpu.roll(product, k, 0)
        plane = plane + product
    plane_ref[...] = plane
    rows = []
    for h in range(2):
        values, code = encode(plane[h * HALF : (h + 1) * HALF])
        send_ref[pl.ds(h * HALF, HALF), :] = values
        rows.append(to_row(code))
    send_ref[pl.ds(NY, 16), :] = code_block([jnp.concatenate(rows, axis=1)])


def own_plane(a, bs, stencil):
    return pl.pallas_call(
        plane_kernel,
        out_shape=[
            jax.ShapeDtypeStruct((NY, NX), jnp.float32),
            jax.ShapeDtypeStruct((NY + 16, NX), jnp.int16),
        ],
        scratch_shapes=[pltpu.VMEM((NY, NX), jnp.float32)],
        compiler_params=pltpu.CompilerParams(vmem_limit_bytes=32 * 1024 * 1024),
        name="own_plane",
    )(a, *bs, stencil)


def smooth_kernel(edge_ref, plane_ref, l1, l2, r1, r2, out_ref):
    def halo(ref):
        table = ref[pl.ds(NY, 16), :].astype(jnp.int32).astype(jnp.float32)
        parts = [
            decode(ref[pl.ds(h * HALF, HALF), :], table[0:1, h * HALF : (h + 1) * HALF])
            for h in range(2)
        ]
        return jnp.concatenate(parts, axis=0)

    row = lax.broadcasted_iota(jnp.int32, (NY, NX), 0)
    col = lax.broadcasted_iota(jnp.int32, (NY, NX), 1)

    def step(below, mid, above):
        near = jnp.where(row == 0, 0.0, pltpu.roll(mid, 1, 0))
        near += jnp.where(row == NY - 1, 0.0, pltpu.roll(mid, NY - 1, 0))
        near += jnp.where(col == 0, 0.0, pltpu.roll(mid, 1, 1))
        near += jnp.where(col == NX - 1, 0.0, pltpu.roll(mid, NX - 1, 1))
        return mid + 0.15 * (near + below + above - 6.0 * mid)

    plane = plane_ref[...]
    left, right = halo(l1), halo(r1)
    lower = step(halo(l2), left, plane)
    upper = step(plane, right, halo(r2))
    lower = jnp.where(edge_ref[0] > 0, lower, 0.0)
    upper = jnp.where(edge_ref[1] > 0, upper, 0.0)
    out_ref[...] = step(lower, step(left, plane, right), upper).astype(jnp.bfloat16)


def smooth(edges, plane, halos):
    vmem = pl.BlockSpec(memory_space=pltpu.VMEM)
    return pl.pallas_call(
        smooth_kernel,
        in_specs=[pl.BlockSpec(memory_space=pltpu.SMEM)] + [vmem] * 5,
        out_specs=vmem,
        out_shape=jax.ShapeDtypeStruct((NY, NX), jnp.bfloat16),
        compiler_params=pltpu.CompilerParams(vmem_limit_bytes=32 * 1024 * 1024),
        name="smooth",
    )(edges, plane, *halos)


def local(acquired, stencil, send_slots, send_lines, send_counts, return_slots, return_counts):
    tile_count = lax.axis_size("tile")
    cut_count = lax.axis_size("cuts")
    tile_half = tile_count // 2
    here = lax.axis_index("cuts")
    here_x = here // 2
    here_core = here % 2
    slots = send_slots[0]
    counts = send_counts[0]
    cap = slots.shape[1]
    slot_index = jnp.arange(cap, dtype=jnp.int32)
    usable = slot_index[None, :] < counts[:, None]
    masked = jnp.where(usable, send_lines[0], -1)
    tail = jnp.broadcast_to(counts[:, None], (tile_count, 128))
    sheet = jnp.concatenate([masked, tail], axis=1)
    swap = [(i, i ^ 1) for i in range(cut_count)]
    peer_sheet = lax.ppermute(sheet, "cuts", swap)
    peer_counts = peer_sheet[:, cap]

    def line_codes(ids):
        cut = ids // NY
        y = ids % NY
        mine = (ids >= 0) & (cut % 2 == here_core)
        ahead = (cut // 2 - here_x) % 4
        place = (y // HALF) * (4 * HALF) + ahead * HALF + y % HALF
        return jnp.where(mine, place, -1).reshape(tile_count, cap // CHUNK, CHUNK)

    own_codes = line_codes(masked)
    peer_codes = line_codes(peer_sheet[:, :cap])

    rows, peer_rows = [], []
    for h in range(2):
        part = slice(h * tile_half, (h + 1) * tile_half)
        rows.append(gather_rows(acquired, slots[part], counts[part]))
        peer_rows.append(lax.ppermute(rows[h], "cuts", swap))

    def x_send(block, k):
        return lax.ppermute(block, "cuts", [(i, (i + 2 * k) % cut_count) for i in range(cut_count)])

    b_blocks = None
    a_parts = []
    for h in range(2):
        part = slice(h * tile_half, (h + 1) * tile_half)
        *a_blocks, b_blocks = line_blocks(
            rows[h], peer_rows[h], own_codes[part], peer_codes[part],
            counts[part], peer_counts[part], b_blocks, h * tile_half, tile_count,
        )
        a_parts.append([a_blocks[0]] + [x_send(a_blocks[k], k) for k in (1, 2, 3)])
    b_arrived = lax.all_to_all(b_blocks, "tile", split_axis=0, concat_axis=0, tiled=True)
    a_sums = None
    for h in range(2):
        a_sums = sum_x(a_parts[h], a_sums, h * tile_half, tile_count)
    a_arrived = lax.all_to_all(a_sums, "tile", split_axis=0, concat_axis=0, tiled=True)
    b_sums = sum_tile(b_arrived)
    b_final = [b_sums[0]] + [x_send(b_sums[k], k) for k in (1, 2, 3)]
    plane, coded = own_plane(a_arrived, b_final, stencil)

    total = cut_count * tile_count

    def plane_send(k):
        pairs = [(i, i + k) for i in range(total) if 0 <= i + k < total]
        return lax.ppermute(coded, ("cuts", "tile"), pairs)

    halos = [plane_send(1), plane_send(2), plane_send(-1), plane_send(-2)]
    place = here * tile_count + lax.axis_index("tile")
    edges = jnp.stack([place > 0, place < total - 1]).astype(jnp.int32)
    field = smooth(edges, plane, halos)

    read_ids = return_slots[0]
    read_total = read_ids.shape[1]
    usable_back = jnp.arange(read_total, dtype=jnp.int32)[None, :] < return_counts[0][:, None]
    selector = jnp.where(usable_back, read_ids, -1).reshape(-1)[:, None] == jnp.arange(
        NY, dtype=jnp.int32
    )
    outgoing = jnp.dot(selector.astype(jnp.bfloat16), field, preferred_element_type=jnp.float32)
    outgoing = outgoing.astype(jnp.bfloat16).reshape(tile_count, read_total, NX)
    returned = lax.all_to_all(outgoing, "tile", split_axis=0, concat_axis=0, tiled=True)
    return field[None], returned


def solution(mesh):
    in_specs = (
        P(("cuts", "tile"), None),
        P("tile", None),
        P(("cuts", "tile"), None, None),
        P(("cuts", "tile"), None, None),
        P(("cuts", "tile"), None),
        P(("cuts", "tile"), None, None),
        P(("cuts", "tile"), None),
    )
    out_specs = (P(("cuts", "tile"), None, None), P(("cuts", "tile"), None, None))
    return jax.shard_map(local, mesh=mesh, in_specs=in_specs, out_specs=out_specs, check_vma=False)
```

```python
import functools
import math

import jax
import jax.numpy as jnp
from jax import lax
from jax.experimental import pallas as pl
from jax.experimental.pallas import tpu as pltpu
from jax.sharding import PartitionSpec as P

NX = 256
NY = 256
TAPS = 4
LA = 160
LB = NY - LA
ALPHA = math.log(2.0) / 64.0
TOP = 32700.0
CHUNK = 256
PICK = 32


def params(mib):
    return pltpu.CompilerParams(
        vmem_limit_bytes=mib * 1024 * 1024, dimension_semantics=("arbitrary",)
    )


def hbm(shape, dtype):
    return pltpu.HBM(shape, dtype)


def encode(block):
    top = to_row(jnp.max(jnp.abs(block), axis=1, keepdims=True))
    code = jnp.ceil(jnp.log(jnp.maximum(top, 1e-33)) * (1.0 / ALPHA))
    factor = to_column(TOP / jnp.exp(code * ALPHA))
    values = (block * factor + 12582912.0) - 12582912.0
    return values.astype(jnp.int32).astype(jnp.int16), code


def eye(size):
    return lax.broadcasted_iota(jnp.int32, (size, size), 0) == lax.broadcasted_iota(
        jnp.int32, (size, size), 1
    )


def to_row(column):
    return jnp.sum(jnp.where(eye(column.shape[0]), column, 0.0), axis=0, keepdims=True)


def to_column(row):
    return jnp.sum(jnp.where(eye(row.shape[1]), row, 0.0), axis=1, keepdims=True)


def decode(values, code_row):
    scale = jnp.exp(code_row * ALPHA) * (1.0 / TOP)
    return values.astype(jnp.int32).astype(jnp.float32) * to_column(scale)


def code_block(rows):
    block = jnp.zeros((16, NX), jnp.float32)
    index = lax.broadcasted_iota(jnp.int32, (16, NX), 0)
    for i, row in enumerate(rows):
        block = jnp.where(index == i, row, block)
    return block.astype(jnp.int32).astype(jnp.int16)


def gather_kernel(slots_ref, counts_ref, acq_ref, out_ref, wide_ref, half_ref, sem, *, first, cap):
    step = pl.program_id(0)
    pieces = sem.shape[0]
    piece = half_ref.shape[0] // pieces

    @pl.when(step == 0)
    def _():
        copies = []
        for k in range(pieces):
            span = pl.ds(k * piece, piece)
            copies.append(
                pltpu.make_async_copy(acq_ref.at[span, :], half_ref.at[span, :], sem.at[k])
            )
            copies[k].start()
        for k in range(pieces):
            copies[k].wait()

            def widen(i, carry):
                span = pl.ds(pl.multiple_of(k * piece + i * CHUNK, CHUNK), CHUNK)
                wide_ref[span, :] = half_ref[span, :].astype(jnp.float32)
                return carry

            lax.fori_loop(0, piece // CHUNK, widen, 0)

    count = counts_ref[first + step]
    start = (first + step) * cap

    def pick(i, carry):
        base = pl.multiple_of(i * PICK, PICK)
        rows = [wide_ref[pl.ds(slots_ref[start + base + u], 1), :] for u in range(PICK)]
        out_ref[0, pl.ds(base, PICK), :] = jnp.concatenate(rows, axis=0).astype(jnp.bfloat16)
        return carry

    def clear(i, carry):
        base = pl.multiple_of(i * PICK, PICK)
        out_ref[0, pl.ds(base, PICK), :] = jnp.zeros((PICK, NX), jnp.bfloat16)
        return carry

    picks = (count + PICK - 1) // PICK
    lax.fori_loop(0, picks, pick, 0)
    lax.fori_loop(picks, (count + CHUNK - 1) // CHUNK * (CHUNK // PICK), clear, 0)


def gather_rows(acquired, slots, counts, first, tiles, cap):
    body = functools.partial(gather_kernel, first=first, cap=cap)
    return pl.pallas_call(
        body,
        grid_spec=pltpu.PrefetchScalarGridSpec(
            num_scalar_prefetch=2,
            grid=(tiles,),
            in_specs=[pl.BlockSpec(memory_space=pl.ANY)],
            out_specs=pl.BlockSpec((1, cap, NX), lambda t, s, c: (t, 0, 0)),
            scratch_shapes=[
                pltpu.VMEM(acquired.shape, jnp.float32),
                pltpu.VMEM(acquired.shape, jnp.bfloat16),
                pltpu.SemaphoreType.DMA((8,)),
            ],
        ),
        out_shape=jax.ShapeDtypeStruct((tiles, cap, NX), jnp.bfloat16),
        compiler_params=params(48),
        cost_estimate=pl.CostEstimate(flops=0, transcendentals=0, bytes_accessed=40_000_000),
        name="gather_rows",
    )(slots, counts, acquired)


def lines_kernel(
    own_n, peer_n, own_ref, peer_ref, own_lines, peer_lines, alias_ref,
    a0_ref, a1_ref, a2_ref, a3_ref, b_ref, acc_ref, code_ref, *, first,
):
    step = pl.program_id(0)
    last = pl.num_programs(0) - 1
    acc_ref[...] = jnp.zeros(acc_ref.shape, jnp.float32)
    position = lax.broadcasted_iota(jnp.int32, (CHUNK, CHUNK), 0)

    def add(rows_ref, lines_ref):
        def body(i, carry):
            base = pl.multiple_of(i * CHUNK, CHUNK)
            rows = rows_ref[0, pl.ds(base, CHUNK), :]
            ids = lines_ref[0, pl.ds(i, 1), :]
            for m in range(acc_ref.shape[0] // CHUNK):
                hot = jnp.where(position + m * CHUNK == ids, 1.0, 0.0).astype(jnp.bfloat16)
                span = pl.ds(m * CHUNK, CHUNK)
                acc_ref[span, :] += jnp.dot(hot, rows, preferred_element_type=jnp.float32)
            return carry

        return body

    own_steps = (own_n[first + step] + CHUNK - 1) // CHUNK
    peer_steps = (peer_n[first + step] + CHUNK - 1) // CHUNK
    lax.fori_loop(0, own_steps, add(own_ref, own_lines), 0)
    lax.fori_loop(0, peer_steps, add(peer_ref, peer_lines), 0)

    outs = (a0_ref, a1_ref, a2_ref, a3_ref)
    for k in range(4):
        values, code = encode(acc_ref[pl.ds(k * LA, LA), :])
        outs[k][pl.ds(pl.multiple_of(step * LA, LA), LA), :] = values
        code_ref[k, pl.ds(step, 1), :] = pad_row(code)

    codes = []
    for k in range(4):
        values, code = encode(acc_ref[pl.ds(4 * LA + k * LB, LB), :])
        b_ref[0, pl.ds(k * LB, LB), :] = values
        codes.append(pad_row(code))
    b_ref[0, pl.ds(4 * LB, 16), :] = code_block(codes)

    @pl.when(step == last)
    def _():
        for k in range(4):
            table = code_ref[k]
            both = jnp.concatenate([table, jnp.zeros_like(table)], axis=0)
            outs[k][pl.ds((last + 1) * LA, 16), :] = both.astype(jnp.int32).astype(jnp.int16)


def pad_row(row):
    return jnp.concatenate([row, jnp.zeros((1, NX - row.shape[1]), jnp.float32)], axis=1)


def line_blocks(own_rows, peer_rows, own_lines, peer_lines, own_n, peer_n, b_old, first, tiles_all):
    tiles, cap, _ = own_rows.shape
    span = cap // CHUNK
    row_spec = pl.BlockSpec((1, cap, NX), lambda t, *_: (t, 0, 0))
    line_spec = pl.BlockSpec((1, span, CHUNK), lambda t, *_: (t + first, 0, 0))
    a_shape = (tiles * LA + 16, NX)
    args = [own_n, peer_n, own_rows, peer_rows, own_lines, peer_lines]
    aliases = {}
    if b_old is None:
        b_old = jnp.zeros((16, NX), jnp.int16)
    else:
        aliases = {6: 4}
    args.append(b_old)
    return pl.pallas_call(
        functools.partial(lines_kernel, first=first),
        grid_spec=pltpu.PrefetchScalarGridSpec(
            num_scalar_prefetch=2,
            grid=(tiles,),
            in_specs=[row_spec, row_spec, line_spec, line_spec, pl.BlockSpec(memory_space=pl.ANY)],
            out_specs=[pl.BlockSpec(a_shape, lambda t, *_: (0, 0))] * 4
            + [pl.BlockSpec((1, 4 * LB + 16, NX), lambda t, *_: (t + first, 0, 0))],
            scratch_shapes=[
                pltpu.VMEM((4 * NY, NX), jnp.float32),
                pltpu.VMEM((4, tiles, NX), jnp.float32),
            ],
        ),
        out_shape=[hbm(a_shape, jnp.int16)] * 4
        + [hbm((tiles_all, 4 * LB + 16, NX), jnp.int16)],
        input_output_aliases=aliases,
        compiler_params=params(48),
        cost_estimate=pl.CostEstimate(
            flops=2 * 1024 * 256 * 20480, transcendentals=0, bytes_accessed=40_000_000
        ),
        name="line_blocks",
    )(*args)


def code_row(block, index, length):
    table = block.astype(jnp.int32).astype(jnp.float32)
    rows = lax.broadcasted_iota(jnp.int32, table.shape, 0)
    row = jnp.sum(jnp.where(rows == index, table, 0.0), axis=0, keepdims=True)
    return row[:, 0:length]


def sum_x_kernel(p0, p1, p2, p3, c0, c1, c2, c3, alias_ref, out_ref):
    step = pl.program_id(0)
    total = jnp.zeros((LA, NX), jnp.float32)
    for values, codes in ((p0, c0), (p1, c1), (p2, c2), (p3, c3)):
        total = total + decode(values[...], code_row(codes[...], step, LA))
    values, code = encode(total)
    out_ref[0, pl.ds(0, LA), :] = values
    out_ref[0, pl.ds(LA, 16), :] = code_block([pad_row(code)])


def sum_x(parts, old, first, tiles_all):
    tiles = (parts[0].shape[0] - 16) // LA
    aliases = {}
    if old is None:
        old = jnp.zeros((16, NX), jnp.int16)
    else:
        aliases = {8: 0}
    return pl.pallas_call(
        sum_x_kernel,
        grid=(tiles,),
        in_specs=[pl.BlockSpec((LA, NX), lambda t: (t, 0))] * 4
        + [pl.BlockSpec((16, NX), lambda t: (tiles * LA // 16, 0))] * 4
        + [pl.BlockSpec(memory_space=pl.ANY)],
        out_specs=pl.BlockSpec((1, LA + 16, NX), lambda t: (t + first, 0, 0)),
        out_shape=hbm((tiles_all, LA + 16, NX), jnp.int16),
        input_output_aliases=aliases,
        compiler_params=params(32),
        name="sum_x",
    )(*parts, *parts, old)


def sum_tile_kernel(in_ref, o0, o1, o2, o3, acc_ref):
    step = pl.program_id(0)

    @pl.when(step == 0)
    def _():
        acc_ref[...] = jnp.zeros(acc_ref.shape, jnp.float32)

    table = in_ref[0, pl.ds(4 * LB, 16), :].astype(jnp.int32).astype(jnp.float32)
    for k in range(4):
        acc_ref[pl.ds(k * LB, LB), :] += decode(
            in_ref[0, pl.ds(k * LB, LB), :], table[k : k + 1, 0:LB]
        )

    @pl.when(step == pl.num_programs(0) - 1)
    def _():
        for k, out in enumerate((o0, o1, o2, o3)):
            values, code = encode(acc_ref[pl.ds(k * LB, LB), :])
            out[pl.ds(0, LB), :] = values
            out[pl.ds(LB, 16), :] = code_block([pad_row(code)])


def sum_tile(arrived):
    tiles, rows, _ = arrived.shape
    out_shape = (LB + 16, NX)
    return pl.pallas_call(
        sum_tile_kernel,
        grid=(tiles,),
        in_specs=[pl.BlockSpec((1, rows, NX), lambda t: (t, 0, 0))],
        out_specs=[pl.BlockSpec(out_shape, lambda t: (0, 0))] * 4,
        out_shape=[jax.ShapeDtypeStruct(out_shape, jnp.int16)] * 4,
        scratch_shapes=[pltpu.VMEM((4 * LB, NX), jnp.float32)],
        compiler_params=params(32),
        name="sum_tile",
    )(arrived)


def plane_kernel(a_ref, b0, b1, b2, b3, stencil_ref, plane_ref, send_ref, lines_ref):
    def body(i, carry):
        codes = code_row(a_ref[i, pl.ds(LA, 16), :], 0, LA)
        lines_ref[pl.ds(0, LA), :] += decode(a_ref[i, pl.ds(0, LA), :], codes)
        return carry

    lines_ref[pl.ds(0, LA), :] = jnp.zeros((LA, NX), jnp.float32)
    lax.fori_loop(0, a_ref.shape[0], body, 0)
    total = jnp.zeros((LB, NX), jnp.float32)
    for b in (b0, b1, b2, b3):
        total = total + decode(b[pl.ds(0, LB), :], code_row(b[pl.ds(LB, 16), :], 0, LB))
    lines_ref[pl.ds(LA, LB), :] = total

    lines = lines_ref[...]
    high = lines.astype(jnp.bfloat16)
    rest = lines - high.astype(jnp.float32)
    mid = rest.astype(jnp.bfloat16)
    low = (rest - mid.astype(jnp.float32)).astype(jnp.bfloat16)
    plane = jnp.zeros((NY, NX), jnp.float32)
    for k in range(TAPS):
        weights = stencil_ref[:, k * NX : (k + 1) * NX]
        product = jnp.dot(high, weights, preferred_element_type=jnp.float32)
        product += jnp.dot(mid, weights, preferred_element_type=jnp.float32)
        product += jnp.dot(low, weights, preferred_element_type=jnp.float32)
        if k:
            product = pltpu.roll(product, k, 0)
        plane = plane + product
    plane_ref[...] = plane
    rows = []
    for h in range(2):
        values, code = encode(plane[h * 128 : (h + 1) * 128])
        send_ref[pl.ds(h * 128, 128), :] = values
        rows.append(code)
    send_ref[pl.ds(NY, 16), :] = code_block([jnp.concatenate(rows, axis=1)])


def own_plane(a, bs, stencil):
    return pl.pallas_call(
        plane_kernel,
        out_shape=[
            jax.ShapeDtypeStruct((NY, NX), jnp.float32),
            jax.ShapeDtypeStruct((NY + 16, NX), jnp.int16),
        ],
        scratch_shapes=[pltpu.VMEM((NY, NX), jnp.float32)],
        compiler_params=pltpu.CompilerParams(vmem_limit_bytes=32 * 1024 * 1024),
        name="own_plane",
    )(a, *bs, stencil)


def smooth_kernel(edge_ref, plane_ref, l1, l2, r1, r2, out_ref):
    def halo(ref):
        table = ref[pl.ds(NY, 16), :].astype(jnp.int32).astype(jnp.float32)
        parts = [
            decode(ref[pl.ds(h * 128, 128), :], table[0:1, h * 128 : (h + 1) * 128])
            for h in range(2)
        ]
        return jnp.concatenate(parts, axis=0)

    row = lax.broadcasted_iota(jnp.int32, (NY, NX), 0)
    col = lax.broadcasted_iota(jnp.int32, (NY, NX), 1)

    def step(below, mid, above):
        near = jnp.where(row == 0, 0.0, pltpu.roll(mid, 1, 0))
        near += jnp.where(row == NY - 1, 0.0, pltpu.roll(mid, NY - 1, 0))
        near += jnp.where(col == 0, 0.0, pltpu.roll(mid, 1, 1))
        near += jnp.where(col == NX - 1, 0.0, pltpu.roll(mid, NX - 1, 1))
        return mid + 0.15 * (near + below + above - 6.0 * mid)

    plane = plane_ref[...]
    left, right = halo(l1), halo(r1)
    lower = step(halo(l2), left, plane)
    upper = step(plane, right, halo(r2))
    lower = jnp.where(edge_ref[0] > 0, lower, 0.0)
    upper = jnp.where(edge_ref[1] > 0, upper, 0.0)
    out_ref[...] = step(lower, step(left, plane, right), upper).astype(jnp.bfloat16)


def smooth(edges, plane, halos):
    vmem = pl.BlockSpec(memory_space=pltpu.VMEM)
    return pl.pallas_call(
        smooth_kernel,
        in_specs=[pl.BlockSpec(memory_space=pltpu.SMEM)] + [vmem] * 5,
        out_specs=vmem,
        out_shape=jax.ShapeDtypeStruct((NY, NX), jnp.bfloat16),
        compiler_params=pltpu.CompilerParams(vmem_limit_bytes=32 * 1024 * 1024),
        name="smooth",
    )(edges, plane, *halos)


def after_kernel(x_ref, *refs):
    del x_ref, refs


def after(x, others):
    anywhere = pl.BlockSpec(memory_space=pl.ANY)
    return pl.pallas_call(
        after_kernel,
        in_specs=[anywhere] * (1 + len(others)),
        out_specs=anywhere,
        out_shape=hbm(x.shape, x.dtype),
        input_output_aliases={0: 0},
        name="after",
    )(x, *others)


def local(acquired, stencil, send_slots, send_lines, send_counts, return_slots, return_counts):
    tile_count = lax.axis_size("tile")
    cut_count = lax.axis_size("cuts")
    tile_half = tile_count // 2
    here = lax.axis_index("cuts")
    here_x = here // 2
    here_core = here % 2
    slots = send_slots[0]
    counts = send_counts[0]
    cap = slots.shape[1]
    slot_index = jnp.arange(cap, dtype=jnp.int32)
    usable = slot_index[None, :] < counts[:, None]
    masked = jnp.where(usable, send_lines[0], -1)
    tail = jnp.broadcast_to(counts[:, None], (tile_count, 128))
    sheet = jnp.concatenate([masked, tail], axis=1)
    swap = [(i, i ^ 1) for i in range(cut_count)]
    flat_slots = slots.reshape(-1)

    def line_codes(ids):
        cut = ids // NY
        y = ids % NY
        mine = (ids >= 0) & (cut % 2 == here_core)
        ahead = (cut // 2 - here_x) % 4
        place = jnp.where(y < LA, ahead * LA + y, 4 * LA + ahead * LB + y - LA)
        return jnp.where(mine, place, -1).reshape(tile_count, cap // CHUNK, CHUNK)

    own_codes = line_codes(masked)

    counts, sheet = lax.optimization_barrier((counts, sheet))
    peer_sheet = lax.ppermute(sheet, "cuts", swap)
    rows, peer_rows = [], []
    for h in range(2):
        if h:
            counts, peer_sheet = lax.optimization_barrier((counts, peer_sheet))
        rows.append(gather_rows(acquired, flat_slots, counts, h * tile_half, tile_half, cap))
        peer_rows.append(lax.ppermute(rows[h], "cuts", swap))
    peer_counts = peer_sheet[:, cap]
    peer_codes = line_codes(peer_sheet[:, :cap])

    def x_send(block, k):
        return lax.ppermute(block, "cuts", [(i, (i + 2 * k) % cut_count) for i in range(cut_count)])

    b_blocks = None
    a_parts = []
    for h in range(2):
        *a_blocks, b_blocks = line_blocks(
            rows[h], peer_rows[h], own_codes, peer_codes,
            counts, peer_counts, b_blocks, h * tile_half, tile_count,
        )
        a_parts.append([a_blocks[0]] + [x_send(a_blocks[k], k) for k in (1, 2, 3)])
    near = (a_parts[0][1], a_parts[0][3])
    b_blocks = after(b_blocks, near)
    b_arrived = lax.all_to_all(b_blocks, "tile", split_axis=0, concat_axis=0, tiled=True)
    a_sums = None
    for h in range(2):
        a_sums = sum_x(a_parts[h], a_sums, h * tile_half, tile_count)
    a_arrived = lax.all_to_all(a_sums, "tile", split_axis=0, concat_axis=0, tiled=True)
    b_sums = sum_tile(b_arrived)
    b_final = [b_sums[0]] + [x_send(b_sums[k], k) for k in (1, 2, 3)]
    plane, coded = own_plane(a_arrived, b_final, stencil)

    total = cut_count * tile_count

    def plane_send(k):
        pairs = [(i, i + k) for i in range(total) if 0 <= i + k < total]
        return lax.ppermute(coded, ("cuts", "tile"), pairs)

    halos = [plane_send(1), plane_send(2), plane_send(-1), plane_send(-2)]
    place = here * tile_count + lax.axis_index("tile")
    edges = jnp.stack([place > 0, place < total - 1]).astype(jnp.int32)
    field = smooth(edges, plane, halos)

    read_ids = return_slots[0]
    read_total = read_ids.shape[1]
    usable_back = jnp.arange(read_total, dtype=jnp.int32)[None, :] < return_counts[0][:, None]
    selector = jnp.where(usable_back, read_ids, -1).reshape(-1)[:, None] == jnp.arange(
        NY, dtype=jnp.int32
    )
    outgoing = jnp.dot(selector.astype(jnp.bfloat16), field, preferred_element_type=jnp.float32)
    outgoing = outgoing.astype(jnp.bfloat16).reshape(tile_count, read_total, NX)
    returned = lax.all_to_all(outgoing, "tile", split_axis=0, concat_axis=0, tiled=True)
    return field[None], returned


def solution(mesh):
    in_specs = (
        P(("cuts", "tile"), None),
        P("tile", None),
        P(("cuts", "tile"), None, None),
        P(("cuts", "tile"), None, None),
        P(("cuts", "tile"), None),
        P(("cuts", "tile"), None, None),
        P(("cuts", "tile"), None),
    )
    out_specs = (P(("cuts", "tile"), None, None), P(("cuts", "tile"), None, None))
    return jax.shard_map(local, mesh=mesh, in_specs=in_specs, out_specs=out_specs, check_vma=False)
```

```python
import functools
import math

import jax
import jax.numpy as jnp
from jax import lax
from jax.experimental import pallas as pl
from jax.experimental.pallas import tpu as pltpu
from jax.sharding import PartitionSpec as P

NX = 256
NY = 256
TAPS = 4
LA = 144
LB = NY - LA
ALPHA = math.log(2.0) / 64.0
TOP = 32700.0
CHUNK = 256
PICK = 32


def params(mib):
    return pltpu.CompilerParams(
        vmem_limit_bytes=mib * 1024 * 1024, dimension_semantics=("arbitrary",)
    )


def hbm(shape, dtype):
    return pltpu.HBM(shape, dtype)


def encode(block):
    top = to_row(jnp.max(jnp.abs(block), axis=1, keepdims=True))
    code = jnp.ceil(jnp.log(jnp.maximum(top, 1e-33)) * (1.0 / ALPHA))
    factor = to_column(TOP / jnp.exp(code * ALPHA))
    values = (block * factor + 12582912.0) - 12582912.0
    return values.astype(jnp.int32).astype(jnp.int16), code


def eye(size):
    return lax.broadcasted_iota(jnp.int32, (size, size), 0) == lax.broadcasted_iota(
        jnp.int32, (size, size), 1
    )


def to_row(column):
    return jnp.sum(jnp.where(eye(column.shape[0]), column, 0.0), axis=0, keepdims=True)


def to_column(row):
    return jnp.sum(jnp.where(eye(row.shape[1]), row, 0.0), axis=1, keepdims=True)


def decode(values, code_row):
    scale = jnp.exp(code_row * ALPHA) * (1.0 / TOP)
    return values.astype(jnp.int32).astype(jnp.float32) * to_column(scale)


def code_block(rows):
    block = jnp.zeros((16, NX), jnp.float32)
    index = lax.broadcasted_iota(jnp.int32, (16, NX), 0)
    for i, row in enumerate(rows):
        block = jnp.where(index == i, row, block)
    return block.astype(jnp.int32).astype(jnp.int16)


def gather_kernel(
    slots_ref, counts_ref, acq_ref, lines_ref, out_ref, wide_ref, half_ref, sem, *, first, cap
):
    step = pl.program_id(0)
    pieces = sem.shape[0]
    piece = half_ref.shape[0] // pieces

    @pl.when(step == 0)
    def _():
        copies = []
        for k in range(pieces):
            span = pl.ds(k * piece, piece)
            copies.append(
                pltpu.make_async_copy(acq_ref.at[span, :], half_ref.at[span, :], sem.at[k])
            )
            copies[k].start()
        for k in range(pieces):
            copies[k].wait()

            def widen(i, carry):
                span = pl.ds(pl.multiple_of(k * piece + i * CHUNK, CHUNK), CHUNK)
                wide_ref[span, :] = half_ref[span, :].astype(jnp.float32)
                return carry

            lax.fori_loop(0, piece // CHUNK, widen, 0)

    count = counts_ref[first + step]
    start = (first + step) * cap

    def pick(i, carry):
        base = pl.multiple_of(i * PICK, PICK)
        rows = [wide_ref[pl.ds(slots_ref[start + base + u], 1), :] for u in range(PICK)]
        out_ref[0, pl.ds(base, PICK), :] = jnp.concatenate(rows, axis=0).astype(jnp.bfloat16)
        return carry

    def clear(i, carry):
        base = pl.multiple_of(i * PICK, PICK)
        out_ref[0, pl.ds(base, PICK), :] = jnp.zeros((PICK, NX), jnp.bfloat16)
        return carry

    picks = (count + PICK - 1) // PICK
    lax.fori_loop(0, picks, pick, 0)
    lax.fori_loop(picks, (count + CHUNK - 1) // CHUNK * (CHUNK // PICK), clear, 0)

    ids = lines_ref[pl.ds(first + step, 1), :]
    position = lax.broadcasted_iota(jnp.int32, ids.shape, 1)
    ids = jnp.where(position < count, ids + 1, 0)
    index = lax.broadcasted_iota(jnp.int32, (8, NX), 0)
    table = jnp.where(index == 7, count, 0)
    for i in range(cap // CHUNK):
        table = jnp.where(index == i, ids[:, i * CHUNK : (i + 1) * CHUNK], table)
    both = jnp.concatenate([table >> 6, table & 63], axis=0)
    out_ref[0, pl.ds(cap, 16), :] = both.astype(jnp.float32).astype(jnp.bfloat16)


def gather_rows(acquired, slots, counts, lines, first, tiles):
    cap = lines.shape[1]
    body = functools.partial(gather_kernel, first=first, cap=cap)
    return pl.pallas_call(
        body,
        grid_spec=pltpu.PrefetchScalarGridSpec(
            num_scalar_prefetch=2,
            grid=(tiles,),
            in_specs=[
                pl.BlockSpec(memory_space=pl.ANY),
                pl.BlockSpec(lines.shape, lambda t, s, c: (0, 0)),
            ],
            out_specs=pl.BlockSpec((1, cap + 16, NX), lambda t, s, c: (t, 0, 0)),
            scratch_shapes=[
                pltpu.VMEM(acquired.shape, jnp.float32),
                pltpu.VMEM(acquired.shape, jnp.bfloat16),
                pltpu.SemaphoreType.DMA((8,)),
            ],
        ),
        out_shape=hbm((tiles, cap + 16, NX), jnp.bfloat16),
        compiler_params=params(48),
        cost_estimate=pl.CostEstimate(flops=0, transcendentals=0, bytes_accessed=40_000_000),
        name="gather_rows",
    )(slots, counts, acquired, lines)


def lines_kernel(
    own_n, peer_n, place_ref, own_hbm, peer_hbm, alias_ref,
    a0_ref, a1_ref, a2_ref, a3_ref, b_ref,
    acc_ref, code_ref, rows_ref, ids_ref, sem, *, first, cap,
):
    step = pl.program_id(0)
    last = pl.num_programs(0) - 1
    most = cap // CHUNK

    def chunks(tile):
        return (own_n[first + tile] + CHUNK - 1) // CHUNK, (peer_n[tile] + CHUNK - 1) // CHUNK

    def for_copies(tile, act):
        slot = lax.rem(tile, 2)
        own, peer = chunks(tile)
        for j, (source, base, count) in enumerate(((own_hbm, 0, own), (peer_hbm, own, peer))):
            for i in range(most):
                copy = pltpu.make_async_copy(
                    source.at[tile, pl.ds(i * CHUNK, CHUNK), :],
                    rows_ref.at[slot, pl.ds(pl.multiple_of((base + i) * CHUNK, CHUNK), CHUNK), :],
                    sem.at[slot, j * (most + 1) + i],
                )

                @pl.when(i < count)
                def _():
                    act(copy)

            act(
                pltpu.make_async_copy(
                    source.at[tile, pl.ds(cap, 16), :],
                    ids_ref.at[slot, j],
                    sem.at[slot, j * (most + 1) + most],
                )
            )

    @pl.when(step == 0)
    def _():
        for_copies(0, lambda copy: copy.start())

    @pl.when(step < last)
    def _():
        for_copies(step + 1, lambda copy: copy.start())

    for_copies(step, lambda copy: copy.wait())

    slot = lax.rem(step, 2)
    own, peer = chunks(step)
    here_core, here_x = place_ref[0], place_ref[1]
    for j in range(2):
        pair = ids_ref[slot, j].astype(jnp.float32).astype(jnp.int32)
        line = pair[0:8] * 64 + pair[8:16] - 1
        cut = line >> 8
        y = line & (NY - 1)
        mine = (line >= 0) & ((cut & 1) == here_core)
        ahead = ((cut >> 1) - here_x) & 3
        target = jnp.where(y < LA, ahead * LA + y, 4 * LA + ahead * LB + y - LA)
        target = jnp.where(mine, target, -1)
        for i in range(most):
            spot = i if j == 0 else own + i
            code_ref[4, pl.ds(spot, 1), :] = target[i : i + 1].astype(jnp.float32)

    acc_ref[...] = jnp.zeros(acc_ref.shape, jnp.float32)
    position = lax.broadcasted_iota(jnp.int32, (CHUNK, CHUNK), 0).astype(jnp.float32)

    def add(start, width):
        rows = rows_ref[slot, pl.ds(pl.multiple_of(start * CHUNK, CHUNK), width * CHUNK), :]
        ids = [code_ref[4, pl.ds(start + i, 1), :] for i in range(width)]
        for m in range(acc_ref.shape[0] // CHUNK):
            hot = [
                jnp.where(position == row - m * CHUNK, 1.0, 0.0).astype(jnp.bfloat16) for row in ids
            ]
            hot = jnp.concatenate(hot, axis=1) if width > 1 else hot[0]
            span = pl.ds(m * CHUNK, CHUNK)
            acc_ref[span, :] += jnp.dot(hot, rows, preferred_element_type=jnp.float32)

    total = own + peer

    def four(i, carry):
        add(i * 4, 4)
        return carry

    lax.fori_loop(0, total // 4, four, 0)
    for width in (1, 2, 3):

        @pl.when(total % 4 == width)
        def _():
            add(total // 4 * 4, width)

    outs = (a0_ref, a1_ref, a2_ref, a3_ref)
    for k in range(4):
        values, code = encode(acc_ref[pl.ds(k * LA, LA), :])
        outs[k][pl.ds(pl.multiple_of(step * LA, LA), LA), :] = values
        code_ref[k, pl.ds(step, 1), :] = pad_row(code)

    codes = []
    for k in range(4):
        values, code = encode(acc_ref[pl.ds(4 * LA + k * LB, LB), :])
        b_ref[0, pl.ds(k * LB, LB), :] = values
        codes.append(pad_row(code))
    b_ref[0, pl.ds(4 * LB, 16), :] = code_block(codes)

    @pl.when(step == last)
    def _():
        for k in range(4):
            outs[k][pl.ds((last + 1) * LA, 16), :] = code_ref[k].astype(jnp.int32).astype(jnp.int16)


def pad_row(row):
    return jnp.concatenate([row, jnp.zeros((1, NX - row.shape[1]), jnp.float32)], axis=1)


def line_blocks(own_rows, peer_rows, own_n, peer_n, place, b_old, first, tiles_all):
    tiles, cap, _ = own_rows.shape
    cap -= 16
    a_shape = (tiles * LA + 16, NX)
    own_rows = pltpu.with_memory_space_constraint(own_rows, pltpu.HBM)
    peer_rows = pltpu.with_memory_space_constraint(peer_rows, pltpu.HBM)
    args = [own_n, peer_n, place, own_rows, peer_rows]
    aliases = {}
    if b_old is None:
        b_old = jnp.zeros((16, NX), jnp.int16)
    else:
        aliases = {5: 4}
    args.append(b_old)
    return pl.pallas_call(
        functools.partial(lines_kernel, first=first, cap=cap),
        grid_spec=pltpu.PrefetchScalarGridSpec(
            num_scalar_prefetch=3,
            grid=(tiles,),
            in_specs=[pl.BlockSpec(memory_space=pltpu.HBM)] * 2
            + [pl.BlockSpec(memory_space=pl.ANY)],
            out_specs=[pl.BlockSpec(a_shape, lambda t, *_: (0, 0))] * 4
            + [pl.BlockSpec((1, 4 * LB + 16, NX), lambda t, *_: (t + first, 0, 0))],
            scratch_shapes=[
                pltpu.VMEM((4 * NY, NX), jnp.float32),
                pltpu.VMEM((5, 16, NX), jnp.float32),
                pltpu.VMEM((2, 2 * cap, NX), jnp.bfloat16),
                pltpu.VMEM((2, 2, 16, NX), jnp.bfloat16),
                pltpu.SemaphoreType.DMA((2, 2 * (cap // CHUNK + 1))),
            ],
        ),
        out_shape=[hbm(a_shape, jnp.int16)] * 4
        + [hbm((tiles_all, 4 * LB + 16, NX), jnp.int16)],
        input_output_aliases=aliases,
        compiler_params=params(48),
        cost_estimate=pl.CostEstimate(
            flops=2 * 1024 * 256 * 20480, transcendentals=0, bytes_accessed=40_000_000
        ),
        name="line_blocks",
    )(*args)


def code_row(block, index, length):
    table = block.astype(jnp.int32).astype(jnp.float32)
    rows = lax.broadcasted_iota(jnp.int32, table.shape, 0)
    row = jnp.sum(jnp.where(rows == index, table, 0.0), axis=0, keepdims=True)
    return row[:, 0:length]


def sum_x_kernel(p0, p1, p2, p3, alias_ref, out_ref, sum_ref, sem, *, first):
    tiles = sum_ref.shape[0]

    def copy_out(i):
        return pltpu.make_async_copy(sum_ref.at[i], out_ref.at[first + i], sem.at[i])

    for i in range(tiles):
        total = jnp.zeros((LA, NX), jnp.float32)
        for part in (p0, p1, p2, p3):
            codes = code_row(part[pl.ds(tiles * LA, 16), :], i, LA)
            total = total + decode(part[pl.ds(i * LA, LA), :], codes)
        values, code = encode(total)
        sum_ref[i, pl.ds(0, LA), :] = values
        sum_ref[i, pl.ds(LA, 16), :] = code_block([pad_row(code)])
        copy_out(i).start()
    for i in range(tiles):
        copy_out(i).wait()


def sum_x(parts, old, first, tiles_all):
    tiles = (parts[0].shape[0] - 16) // LA
    aliases = {}
    if old is None:
        old = jnp.zeros((16, NX), jnp.int16)
    else:
        aliases = {4: 0}
    return pl.pallas_call(
        functools.partial(sum_x_kernel, first=first),
        in_specs=[pl.BlockSpec(memory_space=pltpu.VMEM)] * 4 + [pl.BlockSpec(memory_space=pl.ANY)],
        out_specs=pl.BlockSpec(memory_space=pltpu.HBM),
        out_shape=hbm((tiles_all, LA + 16, NX), jnp.int16),
        scratch_shapes=[
            pltpu.VMEM((tiles, LA + 16, NX), jnp.int16),
            pltpu.SemaphoreType.DMA((tiles,)),
        ],
        input_output_aliases=aliases,
        compiler_params=pltpu.CompilerParams(vmem_limit_bytes=32 * 1024 * 1024),
        name="sum_x",
    )(*parts, old)


def sum_tile_kernel(in_ref, o0, o1, o2, o3, acc_ref):
    step = pl.program_id(0)

    @pl.when(step == 0)
    def _():
        acc_ref[...] = jnp.zeros(acc_ref.shape, jnp.float32)

    table = in_ref[0, pl.ds(4 * LB, 16), :].astype(jnp.int32).astype(jnp.float32)
    for k in range(4):
        acc_ref[pl.ds(k * LB, LB), :] += decode(
            in_ref[0, pl.ds(k * LB, LB), :], table[k : k + 1, 0:LB]
        )

    @pl.when(step == pl.num_programs(0) - 1)
    def _():
        for k, out in enumerate((o0, o1, o2, o3)):
            values, code = encode(acc_ref[pl.ds(k * LB, LB), :])
            out[pl.ds(0, LB), :] = values
            out[pl.ds(LB, 16), :] = code_block([pad_row(code)])


def sum_tile(arrived):
    tiles, rows, _ = arrived.shape
    out_shape = (LB + 16, NX)
    return pl.pallas_call(
        sum_tile_kernel,
        grid=(tiles,),
        in_specs=[pl.BlockSpec((1, rows, NX), lambda t: (t, 0, 0))],
        out_specs=[pl.BlockSpec(out_shape, lambda t: (0, 0))] * 4,
        out_shape=[jax.ShapeDtypeStruct(out_shape, jnp.int16)] * 4,
        scratch_shapes=[pltpu.VMEM((4 * LB, NX), jnp.float32)],
        compiler_params=params(32),
        name="sum_tile",
    )(arrived)


def plane_kernel(a_ref, b0, b1, b2, b3, stencil_ref, plane_ref, send_ref, lines_ref):
    def body(i, carry):
        codes = code_row(a_ref[i, pl.ds(LA, 16), :], 0, LA)
        lines_ref[pl.ds(0, LA), :] += decode(a_ref[i, pl.ds(0, LA), :], codes)
        return carry

    lines_ref[pl.ds(0, LA), :] = jnp.zeros((LA, NX), jnp.float32)
    lax.fori_loop(0, a_ref.shape[0], body, 0)
    total = jnp.zeros((LB, NX), jnp.float32)
    for b in (b0, b1, b2, b3):
        total = total + decode(b[pl.ds(0, LB), :], code_row(b[pl.ds(LB, 16), :], 0, LB))
    lines_ref[pl.ds(LA, LB), :] = total

    lines = lines_ref[...]
    high = lines.astype(jnp.bfloat16)
    rest = lines - high.astype(jnp.float32)
    mid = rest.astype(jnp.bfloat16)
    low = (rest - mid.astype(jnp.float32)).astype(jnp.bfloat16)
    plane = jnp.zeros((NY, NX), jnp.float32)
    for k in range(TAPS):
        weights = stencil_ref[:, k * NX : (k + 1) * NX]
        product = jnp.dot(high, weights, preferred_element_type=jnp.float32)
        product += jnp.dot(mid, weights, preferred_element_type=jnp.float32)
        product += jnp.dot(low, weights, preferred_element_type=jnp.float32)
        if k:
            product = pltpu.roll(product, k, 0)
        plane = plane + product
    plane_ref[...] = plane
    rows = []
    for h in range(2):
        values, code = encode(plane[h * 128 : (h + 1) * 128])
        send_ref[pl.ds(h * 128, 128), :] = values
        rows.append(code)
    send_ref[pl.ds(NY, 16), :] = code_block([jnp.concatenate(rows, axis=1)])


def own_plane(a, bs, stencil):
    return pl.pallas_call(
        plane_kernel,
        out_shape=[
            jax.ShapeDtypeStruct((NY, NX), jnp.float32),
            jax.ShapeDtypeStruct((NY + 16, NX), jnp.int16),
        ],
        scratch_shapes=[pltpu.VMEM((NY, NX), jnp.float32)],
        compiler_params=pltpu.CompilerParams(vmem_limit_bytes=32 * 1024 * 1024),
        name="own_plane",
    )(a, *bs, stencil)


def smooth_kernel(edge_ref, counts_ref, plane_ref, l1, l2, r1, r2, reads_ref, out_ref, back_ref):
    def halo(ref):
        table = ref[pl.ds(NY, 16), :].astype(jnp.int32).astype(jnp.float32)
        parts = [
            decode(ref[pl.ds(h * 128, 128), :], table[0:1, h * 128 : (h + 1) * 128])
            for h in range(2)
        ]
        return jnp.concatenate(parts, axis=0)

    row = lax.broadcasted_iota(jnp.int32, (NY, NX), 0)
    col = lax.broadcasted_iota(jnp.int32, (NY, NX), 1)

    def step(below, mid, above):
        near = jnp.where(row == 0, 0.0, pltpu.roll(mid, 1, 0))
        near += jnp.where(row == NY - 1, 0.0, pltpu.roll(mid, NY - 1, 0))
        near += jnp.where(col == 0, 0.0, pltpu.roll(mid, 1, 1))
        near += jnp.where(col == NX - 1, 0.0, pltpu.roll(mid, NX - 1, 1))
        return mid + 0.15 * (near + below + above - 6.0 * mid)

    plane = plane_ref[...]
    left, right = halo(l1), halo(r1)
    lower = step(halo(l2), left, plane)
    upper = step(plane, right, halo(r2))
    lower = jnp.where(edge_ref[0] > 0, lower, 0.0)
    upper = jnp.where(edge_ref[1] > 0, upper, 0.0)
    field = step(lower, step(left, plane, right), upper).astype(jnp.bfloat16)
    out_ref[...] = field

    readers, most = reads_ref.shape
    lane = lax.broadcasted_iota(jnp.int32, (1, most), 1)
    columns = lax.broadcasted_iota(jnp.int32, (most, NY), 1).astype(jnp.float32)
    for t in range(readers):
        ids = jnp.where(lane < counts_ref[t], reads_ref[pl.ds(t, 1), :], -1)
        hot = jnp.where(columns == to_column(ids.astype(jnp.float32)), 1.0, 0.0)
        lines = jnp.dot(hot.astype(jnp.bfloat16), field, preferred_element_type=jnp.float32)
        back_ref[t] = lines.astype(jnp.bfloat16)


def smooth(edges, counts, plane, halos, reads):
    vmem = pl.BlockSpec(memory_space=pltpu.VMEM)
    smem = pl.BlockSpec(memory_space=pltpu.SMEM)
    readers, most = reads.shape
    return pl.pallas_call(
        smooth_kernel,
        in_specs=[smem, smem] + [vmem] * 6,
        out_specs=[vmem, vmem],
        out_shape=[
            jax.ShapeDtypeStruct((NY, NX), jnp.bfloat16),
            jax.ShapeDtypeStruct((readers, most, NX), jnp.bfloat16),
        ],
        compiler_params=pltpu.CompilerParams(vmem_limit_bytes=32 * 1024 * 1024),
        name="smooth",
    )(edges, counts, plane, *halos, reads)


def after_kernel(x_ref, *refs):
    del x_ref, refs


def after(x, others):
    anywhere = pl.BlockSpec(memory_space=pl.ANY)
    return pl.pallas_call(
        after_kernel,
        in_specs=[anywhere] * (1 + len(others)),
        out_specs=anywhere,
        out_shape=hbm(x.shape, x.dtype),
        input_output_aliases={0: 0},
        name="after",
    )(x, *others)


def local(acquired, stencil, send_slots, send_lines, send_counts, return_slots, return_counts):
    tile_count = lax.axis_size("tile")
    cut_count = lax.axis_size("cuts")
    tile_half = tile_count // 2
    here = lax.axis_index("cuts")
    here_x = here // 2
    here_core = here % 2
    place = jnp.stack([here_core, here_x]).astype(jnp.int32)
    counts = send_counts[0]
    flat_slots = send_slots.reshape(-1)
    swap = [(i, i ^ 1) for i in range(cut_count)]

    rows, peer_rows = [], []
    for h in range(2):
        rows.append(
            gather_rows(acquired, flat_slots, counts, send_lines[0], h * tile_half, tile_half)
        )
        peer_rows.append(lax.ppermute(rows[h], "cuts", swap))
    cap = send_slots.shape[2]
    peer_counts = [
        (part[:, cap + 7, 0].astype(jnp.float32) * 64 + part[:, cap + 15, 0].astype(jnp.float32))
        .astype(jnp.int32)
        for part in peer_rows
    ]

    def x_send(block, k):
        return lax.ppermute(block, "cuts", [(i, (i + 2 * k) % cut_count) for i in range(cut_count)])

    b_blocks = None
    a_parts = []
    for h in range(2):
        *a_blocks, b_blocks = line_blocks(
            rows[h], peer_rows[h], counts, peer_counts[h], place,
            b_blocks, h * tile_half, tile_count,
        )
        a_parts.append([a_blocks[0]] + [x_send(a_blocks[k], k) for k in (1, 2, 3)])
    near = (a_parts[0][1][:16], a_parts[0][3][:16])
    b_blocks = after(b_blocks, near)
    b_arrived = lax.all_to_all(b_blocks, "tile", split_axis=0, concat_axis=0, tiled=True)
    a_sums = None
    for h in range(2):
        a_sums = sum_x(a_parts[h], a_sums, h * tile_half, tile_count)
    a_arrived = lax.all_to_all(a_sums, "tile", split_axis=0, concat_axis=0, tiled=True)
    b_sums = sum_tile(b_arrived)
    b_final = [b_sums[0]] + [x_send(b_sums[k], k) for k in (1, 2, 3)]
    plane, coded = own_plane(a_arrived, b_final, stencil)

    total = cut_count * tile_count

    def plane_send(k):
        pairs = [(i, i + k) for i in range(total) if 0 <= i + k < total]
        return lax.ppermute(coded, ("cuts", "tile"), pairs)

    halos = [plane_send(1), plane_send(2), plane_send(-1), plane_send(-2)]
    spot = here * tile_count + lax.axis_index("tile")
    edges = jnp.stack([spot > 0, spot < total - 1]).astype(jnp.int32)
    field, outgoing = smooth(edges, return_counts[0], plane, halos, return_slots[0])
    returned = lax.all_to_all(outgoing, "tile", split_axis=0, concat_axis=0, tiled=True)
    return field[None], returned


def solution(mesh):
    in_specs = (
        P(("cuts", "tile"), None),
        P("tile", None),
        P(("cuts", "tile"), None, None),
        P(("cuts", "tile"), None, None),
        P(("cuts", "tile"), None),
        P(("cuts", "tile"), None, None),
        P(("cuts", "tile"), None),
    )
    out_specs = (P(("cuts", "tile"), None, None), P(("cuts", "tile"), None, None))
    return jax.shard_map(local, mesh=mesh, in_specs=in_specs, out_specs=out_specs, check_vma=False)
```

```python
import functools
import math

import jax
import jax.numpy as jnp
from jax import lax
from jax.experimental import pallas as pl
from jax.experimental.pallas import tpu as pltpu
from jax.sharding import PartitionSpec as P

NX = 256
NY = 256
TAPS = 4
LA = 112
LB = NY - LA
ALPHA = math.log(2.0) / 64.0
TOP = 32700.0
CHUNK = 256
PICK = 32


def params(mib):
    return pltpu.CompilerParams(
        vmem_limit_bytes=mib * 1024 * 1024, dimension_semantics=("arbitrary",)
    )


def hbm(shape, dtype):
    return pltpu.HBM(shape, dtype)


def encode(block):
    top = to_row(jnp.max(jnp.abs(block), axis=1, keepdims=True))
    code = jnp.ceil(jnp.log(jnp.maximum(top, 1e-33)) * (1.0 / ALPHA))
    factor = to_column(TOP / jnp.exp(code * ALPHA))
    values = (block * factor + 12582912.0) - 12582912.0
    return values.astype(jnp.int32).astype(jnp.int16), code


def eye(size):
    return lax.broadcasted_iota(jnp.int32, (size, size), 0) == lax.broadcasted_iota(
        jnp.int32, (size, size), 1
    )


def to_row(column):
    return jnp.sum(jnp.where(eye(column.shape[0]), column, 0.0), axis=0, keepdims=True)


def to_column(row):
    return jnp.sum(jnp.where(eye(row.shape[1]), row, 0.0), axis=1, keepdims=True)


def decode(values, code_row):
    scale = jnp.exp(code_row * ALPHA) * (1.0 / TOP)
    return values.astype(jnp.int32).astype(jnp.float32) * to_column(scale)


def code_block(rows):
    block = jnp.zeros((16, NX), jnp.float32)
    index = lax.broadcasted_iota(jnp.int32, (16, NX), 0)
    for i, row in enumerate(rows):
        block = jnp.where(index == i, row, block)
    return block.astype(jnp.int32).astype(jnp.int16)


def gather_kernel(
    slots_ref, counts_ref, acq_ref, lines_ref, out_ref, wide_ref, half_ref, sem, *, first, cap
):
    step = pl.program_id(0)
    pieces = sem.shape[0]
    piece = half_ref.shape[0] // pieces

    @pl.when(step == 0)
    def _():
        copies = []
        for k in range(pieces):
            span = pl.ds(k * piece, piece)
            copies.append(
                pltpu.make_async_copy(acq_ref.at[span, :], half_ref.at[span, :], sem.at[k])
            )
            copies[k].start()
        for k in range(pieces):
            copies[k].wait()

            def widen(i, carry):
                span = pl.ds(pl.multiple_of(k * piece + i * CHUNK, CHUNK), CHUNK)
                wide_ref[span, :] = half_ref[span, :].astype(jnp.float32)
                return carry

            lax.fori_loop(0, piece // CHUNK, widen, 0)

    count = counts_ref[first + step]
    start = (first + step) * cap

    def pick(i, carry):
        base = pl.multiple_of(i * PICK, PICK)
        rows = [wide_ref[pl.ds(slots_ref[start + base + u], 1), :] for u in range(PICK)]
        out_ref[0, pl.ds(base, PICK), :] = jnp.concatenate(rows, axis=0).astype(jnp.bfloat16)
        return carry

    def clear(i, carry):
        base = pl.multiple_of(i * PICK, PICK)
        out_ref[0, pl.ds(base, PICK), :] = jnp.zeros((PICK, NX), jnp.bfloat16)
        return carry

    picks = (count + PICK - 1) // PICK
    lax.fori_loop(0, picks, pick, 0)
    lax.fori_loop(picks, (count + CHUNK - 1) // CHUNK * (CHUNK // PICK), clear, 0)

    ids = lines_ref[pl.ds(first + step, 1), :]
    position = lax.broadcasted_iota(jnp.int32, ids.shape, 1)
    ids = jnp.where(position < count, ids + 1, 0)
    index = lax.broadcasted_iota(jnp.int32, (8, NX), 0)
    table = jnp.where(index == 7, count, 0)
    for i in range(cap // CHUNK):
        table = jnp.where(index == i, ids[:, i * CHUNK : (i + 1) * CHUNK], table)
    both = jnp.concatenate([table >> 6, table & 63], axis=0)
    out_ref[0, pl.ds(cap, 16), :] = both.astype(jnp.float32).astype(jnp.bfloat16)


def gather_rows(acquired, slots, counts, lines, first, tiles):
    cap = lines.shape[1]
    body = functools.partial(gather_kernel, first=first, cap=cap)
    return pl.pallas_call(
        body,
        grid_spec=pltpu.PrefetchScalarGridSpec(
            num_scalar_prefetch=2,
            grid=(tiles,),
            in_specs=[
                pl.BlockSpec(memory_space=pl.ANY),
                pl.BlockSpec(lines.shape, lambda t, s, c: (0, 0)),
            ],
            out_specs=pl.BlockSpec((1, cap + 16, NX), lambda t, s, c: (t, 0, 0)),
            scratch_shapes=[
                pltpu.VMEM(acquired.shape, jnp.float32),
                pltpu.VMEM(acquired.shape, jnp.bfloat16),
                pltpu.SemaphoreType.DMA((8,)),
            ],
        ),
        out_shape=hbm((tiles, cap + 16, NX), jnp.bfloat16),
        compiler_params=params(48),
        cost_estimate=pl.CostEstimate(flops=0, transcendentals=0, bytes_accessed=40_000_000),
        name="gather_rows",
    )(slots, counts, acquired, lines)


def sum_lines(
    own_n, peer_n, place_ref, own_hbm, peer_hbm, acc_ref, spot_ref, rows_ref, ids_ref, sem,
    *, first, cap, low, length,
):
    step = pl.program_id(0)
    last = pl.num_programs(0) - 1
    most = cap // CHUNK

    def chunks(tile):
        return (own_n[first + tile] + CHUNK - 1) // CHUNK, (peer_n[tile] + CHUNK - 1) // CHUNK

    def for_copies(tile, act):
        slot = lax.rem(tile, 2)
        own, peer = chunks(tile)
        for j, (source, base, count) in enumerate(((own_hbm, 0, own), (peer_hbm, own, peer))):
            for i in range(most):
                copy = pltpu.make_async_copy(
                    source.at[tile, pl.ds(i * CHUNK, CHUNK), :],
                    rows_ref.at[slot, pl.ds(pl.multiple_of((base + i) * CHUNK, CHUNK), CHUNK), :],
                    sem.at[slot, j * (most + 1) + i],
                )

                @pl.when(i < count)
                def _():
                    act(copy)

            act(
                pltpu.make_async_copy(
                    source.at[tile, pl.ds(cap, 16), :],
                    ids_ref.at[slot, j],
                    sem.at[slot, j * (most + 1) + most],
                )
            )

    @pl.when(step == 0)
    def _():
        for_copies(0, lambda copy: copy.start())

    @pl.when(step < last)
    def _():
        for_copies(step + 1, lambda copy: copy.start())

    for_copies(step, lambda copy: copy.wait())

    slot = lax.rem(step, 2)
    own, peer = chunks(step)
    here_core, here_x = place_ref[0], place_ref[1]
    for j in range(2):
        pair = ids_ref[slot, j].astype(jnp.float32).astype(jnp.int32)
        line = pair[0:8] * 64 + pair[8:16] - 1
        cut = line >> 8
        y = (line & (NY - 1)) - low
        mine = (line >= 0) & ((cut & 1) == here_core) & (y >= 0) & (y < length)
        ahead = ((cut >> 1) - here_x) & 3
        target = jnp.where(mine, ahead * length + y, -1)
        for i in range(most):
            spot = i if j == 0 else own + i
            spot_ref[pl.ds(spot, 1), :] = target[i : i + 1].astype(jnp.float32)

    acc_ref[...] = jnp.zeros(acc_ref.shape, jnp.float32)
    block = 2 * length
    position = lax.broadcasted_iota(jnp.int32, (block, CHUNK), 0).astype(jnp.float32)

    def add(start, width):
        rows = rows_ref[slot, pl.ds(pl.multiple_of(start * CHUNK, CHUNK), width * CHUNK), :]
        ids = [spot_ref[pl.ds(start + i, 1), :] for i in range(width)]
        for m in range(2):
            hot = [
                jnp.where(position == row - m * block, 1.0, 0.0).astype(jnp.bfloat16) for row in ids
            ]
            hot = jnp.concatenate(hot, axis=1) if width > 1 else hot[0]
            span = pl.ds(m * block, block)
            acc_ref[span, :] += jnp.dot(hot, rows, preferred_element_type=jnp.float32)

    total = own + peer

    def four(i, carry):
        add(i * 4, 4)
        return carry

    lax.fori_loop(0, total // 4, four, 0)
    for width in (1, 2, 3):

        @pl.when(total % 4 == width)
        def _():
            add(total // 4 * 4, width)

    return [encode(acc_ref[pl.ds(k * length, length), :]) for k in range(4)]


def tile_kernel(own_n, peer_n, place_ref, own_hbm, peer_hbm, alias_ref, b_ref, *scratch, **sizes):
    blocks = sum_lines(own_n, peer_n, place_ref, own_hbm, peer_hbm, *scratch, **sizes)
    for k, (values, _) in enumerate(blocks):
        b_ref[0, pl.ds(k * LB, LB), :] = values
    b_ref[0, pl.ds(4 * LB, 16), :] = code_block([pad_row(code) for _, code in blocks])


def x_kernel(
    own_n, peer_n, place_ref, own_hbm, peer_hbm, a0, a1, a2, a3, code_ref, *scratch, **sizes
):
    step = pl.program_id(0)
    last = pl.num_programs(0) - 1
    blocks = sum_lines(own_n, peer_n, place_ref, own_hbm, peer_hbm, *scratch, **sizes)
    outs = (a0, a1, a2, a3)
    for k, (values, code) in enumerate(blocks):
        outs[k][pl.ds(pl.multiple_of(step * LA, LA), LA), :] = values
        code_ref[k, pl.ds(step, 1), :] = pad_row(code)

    @pl.when(step == last)
    def _():
        for k in range(4):
            outs[k][pl.ds((last + 1) * LA, 16), :] = code_ref[k].astype(jnp.int32).astype(jnp.int16)


def pad_row(row):
    return jnp.concatenate([row, jnp.zeros((1, NX - row.shape[1]), jnp.float32)], axis=1)


def lines_call(body, name, ins, grid_tiles, cap, length, out_specs, out_shape, scratch, aliases):
    return pl.pallas_call(
        body,
        grid_spec=pltpu.PrefetchScalarGridSpec(
            num_scalar_prefetch=3,
            grid=(grid_tiles,),
            in_specs=[pl.BlockSpec(memory_space=pltpu.HBM)] * 2
            + [pl.BlockSpec(memory_space=pl.ANY)] * (len(ins) - 5),
            out_specs=out_specs,
            scratch_shapes=scratch
            + [
                pltpu.VMEM((4 * length, NX), jnp.float32),
                pltpu.VMEM((16, NX), jnp.float32),
                pltpu.VMEM((2, 2 * cap, NX), jnp.bfloat16),
                pltpu.VMEM((2, 2, 16, NX), jnp.bfloat16),
                pltpu.SemaphoreType.DMA((2, 2 * (cap // CHUNK + 1))),
            ],
        ),
        out_shape=out_shape,
        input_output_aliases=aliases,
        compiler_params=params(48),
        cost_estimate=pl.CostEstimate(
            flops=2 * 4 * length * 256 * 20480, transcendentals=0, bytes_accessed=20_000_000
        ),
        name=name,
    )(*ins)


def in_hbm(x):
    return pltpu.with_memory_space_constraint(x, pltpu.HBM)


def tile_blocks(own_rows, peer_rows, own_n, peer_n, place, b_old, first, tiles_all):
    tiles, cap, _ = own_rows.shape
    cap -= 16
    if b_old is None:
        b_old, aliases = jnp.zeros((16, NX), jnp.int16), {}
    else:
        aliases = {5: 0}
    return lines_call(
        functools.partial(tile_kernel, first=first, cap=cap, low=LA, length=LB),
        "tile_blocks",
        [own_n, peer_n, place, in_hbm(own_rows), in_hbm(peer_rows), b_old],
        tiles, cap, LB,
        pl.BlockSpec((1, 4 * LB + 16, NX), lambda t, *_: (t + first, 0, 0)),
        hbm((tiles_all, 4 * LB + 16, NX), jnp.int16),
        [], aliases,
    )


def x_blocks(own_rows, peer_rows, own_n, peer_n, place, first):
    tiles, cap, _ = own_rows.shape
    cap -= 16
    shape = (tiles * LA + 16, NX)
    return lines_call(
        functools.partial(x_kernel, first=first, cap=cap, low=0, length=LA),
        "x_blocks",
        [own_n, peer_n, place, in_hbm(own_rows), in_hbm(peer_rows)],
        tiles, cap, LA,
        [pl.BlockSpec(shape, lambda t, *_: (0, 0))] * 4,
        [hbm(shape, jnp.int16)] * 4,
        [pltpu.VMEM((4, 16, NX), jnp.float32)], {},
    )


def code_row(block, index, length):
    table = block.astype(jnp.int32).astype(jnp.float32)
    rows = lax.broadcasted_iota(jnp.int32, table.shape, 0)
    row = jnp.sum(jnp.where(rows == index, table, 0.0), axis=0, keepdims=True)
    return row[:, 0:length]


def sum_x_kernel(p0, p1, p2, p3, alias_ref, out_ref, sum_ref, sem, *, first):
    tiles = sum_ref.shape[0]

    def copy_out(i):
        return pltpu.make_async_copy(sum_ref.at[i], out_ref.at[first + i], sem.at[i])

    for i in range(tiles):
        total = jnp.zeros((LA, NX), jnp.float32)
        for part in (p0, p1, p2, p3):
            codes = code_row(part[pl.ds(tiles * LA, 16), :], i, LA)
            total = total + decode(part[pl.ds(i * LA, LA), :], codes)
        values, code = encode(total)
        sum_ref[i, pl.ds(0, LA), :] = values
        sum_ref[i, pl.ds(LA, 16), :] = code_block([pad_row(code)])
        copy_out(i).start()
    for i in range(tiles):
        copy_out(i).wait()


def sum_x(parts, old, first, tiles_all):
    tiles = (parts[0].shape[0] - 16) // LA
    aliases = {}
    if old is None:
        old = jnp.zeros((16, NX), jnp.int16)
    else:
        aliases = {4: 0}
    return pl.pallas_call(
        functools.partial(sum_x_kernel, first=first),
        in_specs=[pl.BlockSpec(memory_space=pltpu.VMEM)] * 4 + [pl.BlockSpec(memory_space=pl.ANY)],
        out_specs=pl.BlockSpec(memory_space=pltpu.HBM),
        out_shape=hbm((tiles_all, LA + 16, NX), jnp.int16),
        scratch_shapes=[
            pltpu.VMEM((tiles, LA + 16, NX), jnp.int16),
            pltpu.SemaphoreType.DMA((tiles,)),
        ],
        input_output_aliases=aliases,
        compiler_params=pltpu.CompilerParams(vmem_limit_bytes=32 * 1024 * 1024),
        name="sum_x",
    )(*parts, old)


def sum_tile_kernel(in_ref, o0, o1, o2, o3, acc_ref):
    acc_ref[...] = jnp.zeros(acc_ref.shape, jnp.float32)

    def body(t, carry):
        table = in_ref[t, pl.ds(4 * LB, 16), :].astype(jnp.int32).astype(jnp.float32)
        for k in range(4):
            acc_ref[pl.ds(k * LB, LB), :] += decode(
                in_ref[t, pl.ds(k * LB, LB), :], table[k : k + 1, 0:LB]
            )
        return carry

    lax.fori_loop(0, in_ref.shape[0], body, 0)
    for k, out in enumerate((o0, o1, o2, o3)):
        values, code = encode(acc_ref[pl.ds(k * LB, LB), :])
        out[pl.ds(0, LB), :] = values
        out[pl.ds(LB, 16), :] = code_block([pad_row(code)])


def sum_tile(arrived):
    out_shape = (LB + 16, NX)
    return pl.pallas_call(
        sum_tile_kernel,
        out_shape=[jax.ShapeDtypeStruct(out_shape, jnp.int16)] * 4,
        scratch_shapes=[pltpu.VMEM((4 * LB, NX), jnp.float32)],
        compiler_params=pltpu.CompilerParams(vmem_limit_bytes=32 * 1024 * 1024),
        name="sum_tile",
    )(arrived)


def plane_kernel(a_ref, b0, b1, b2, b3, stencil_ref, plane_ref, send_ref, lines_ref):
    def body(i, carry):
        codes = code_row(a_ref[i, pl.ds(LA, 16), :], 0, LA)
        lines_ref[pl.ds(0, LA), :] += decode(a_ref[i, pl.ds(0, LA), :], codes)
        return carry

    lines_ref[pl.ds(0, LA), :] = jnp.zeros((LA, NX), jnp.float32)
    lax.fori_loop(0, a_ref.shape[0], body, 0)
    total = jnp.zeros((LB, NX), jnp.float32)
    for b in (b0, b1, b2, b3):
        total = total + decode(b[pl.ds(0, LB), :], code_row(b[pl.ds(LB, 16), :], 0, LB))
    lines_ref[pl.ds(LA, LB), :] = total

    lines = lines_ref[...]
    high = lines.astype(jnp.bfloat16)
    rest = lines - high.astype(jnp.float32)
    mid = rest.astype(jnp.bfloat16)
    low = (rest - mid.astype(jnp.float32)).astype(jnp.bfloat16)
    plane = jnp.zeros((NY, NX), jnp.float32)
    for k in range(TAPS):
        weights = stencil_ref[:, k * NX : (k + 1) * NX]
        product = jnp.dot(high, weights, preferred_element_type=jnp.float32)
        product += jnp.dot(mid, weights, preferred_element_type=jnp.float32)
        product += jnp.dot(low, weights, preferred_element_type=jnp.float32)
        if k:
            product = pltpu.roll(product, k, 0)
        plane = plane + product
    plane_ref[...] = plane
    rows = []
    for h in range(2):
        values, code = encode(plane[h * 128 : (h + 1) * 128])
        send_ref[pl.ds(h * 128, 128), :] = values
        rows.append(code)
    send_ref[pl.ds(NY, 16), :] = code_block([jnp.concatenate(rows, axis=1)])


def own_plane(a, bs, stencil):
    return pl.pallas_call(
        plane_kernel,
        out_shape=[
            jax.ShapeDtypeStruct((NY, NX), jnp.float32),
            jax.ShapeDtypeStruct((NY + 16, NX), jnp.int16),
        ],
        scratch_shapes=[pltpu.VMEM((NY, NX), jnp.float32)],
        compiler_params=pltpu.CompilerParams(vmem_limit_bytes=32 * 1024 * 1024),
        name="own_plane",
    )(a, *bs, stencil)


def smooth_kernel(edge_ref, counts_ref, plane_ref, l1, l2, r1, r2, reads_ref, out_ref, back_ref):
    def halo(ref):
        table = ref[pl.ds(NY, 16), :].astype(jnp.int32).astype(jnp.float32)
        parts = [
            decode(ref[pl.ds(h * 128, 128), :], table[0:1, h * 128 : (h + 1) * 128])
            for h in range(2)
        ]
        return jnp.concatenate(parts, axis=0)

    row = lax.broadcasted_iota(jnp.int32, (NY, NX), 0)
    col = lax.broadcasted_iota(jnp.int32, (NY, NX), 1)

    def step(below, mid, above):
        near = jnp.where(row == 0, 0.0, pltpu.roll(mid, 1, 0))
        near += jnp.where(row == NY - 1, 0.0, pltpu.roll(mid, NY - 1, 0))
        near += jnp.where(col == 0, 0.0, pltpu.roll(mid, 1, 1))
        near += jnp.where(col == NX - 1, 0.0, pltpu.roll(mid, NX - 1, 1))
        return mid + 0.15 * (near + below + above - 6.0 * mid)

    plane = plane_ref[...]
    left, right = halo(l1), halo(r1)
    lower = step(halo(l2), left, plane)
    upper = step(plane, right, halo(r2))
    lower = jnp.where(edge_ref[0] > 0, lower, 0.0)
    upper = jnp.where(edge_ref[1] > 0, upper, 0.0)
    field = step(lower, step(left, plane, right), upper).astype(jnp.bfloat16)
    out_ref[...] = field

    readers, most = reads_ref.shape
    lane = lax.broadcasted_iota(jnp.int32, (1, most), 1)
    columns = lax.broadcasted_iota(jnp.int32, (most, NY), 1).astype(jnp.float32)
    for t in range(readers):
        ids = jnp.where(lane < counts_ref[t], reads_ref[pl.ds(t, 1), :], -1)
        hot = jnp.where(columns == to_column(ids.astype(jnp.float32)), 1.0, 0.0)
        lines = jnp.dot(hot.astype(jnp.bfloat16), field, preferred_element_type=jnp.float32)
        back_ref[t] = lines.astype(jnp.bfloat16)


def smooth(edges, counts, plane, halos, reads):
    vmem = pl.BlockSpec(memory_space=pltpu.VMEM)
    smem = pl.BlockSpec(memory_space=pltpu.SMEM)
    readers, most = reads.shape
    return pl.pallas_call(
        smooth_kernel,
        in_specs=[smem, smem] + [vmem] * 6,
        out_specs=[vmem, vmem],
        out_shape=[
            jax.ShapeDtypeStruct((NY, NX), jnp.bfloat16),
            jax.ShapeDtypeStruct((readers, most, NX), jnp.bfloat16),
        ],
        compiler_params=pltpu.CompilerParams(vmem_limit_bytes=32 * 1024 * 1024),
        name="smooth",
    )(edges, counts, plane, *halos, reads)


def local(acquired, stencil, send_slots, send_lines, send_counts, return_slots, return_counts):
    tile_count = lax.axis_size("tile")
    cut_count = lax.axis_size("cuts")
    tile_half = tile_count // 2
    here = lax.axis_index("cuts")
    here_x = here // 2
    here_core = here % 2
    place = jnp.stack([here_core, here_x]).astype(jnp.int32)
    counts = send_counts[0]
    flat_slots = send_slots.reshape(-1)
    swap = [(i, i ^ 1) for i in range(cut_count)]

    rows, peer_rows = [], []
    for h in range(2):
        rows.append(
            gather_rows(acquired, flat_slots, counts, send_lines[0], h * tile_half, tile_half)
        )
        peer_rows.append(lax.ppermute(rows[h], "cuts", swap))
    cap = send_slots.shape[2]
    peer_counts = [
        (part[:, cap + 7, 0].astype(jnp.float32) * 64 + part[:, cap + 15, 0].astype(jnp.float32))
        .astype(jnp.int32)
        for part in peer_rows
    ]

    def x_send(block, k):
        return lax.ppermute(block, "cuts", [(i, (i + 2 * k) % cut_count) for i in range(cut_count)])

    b_blocks = None
    for h in range(2):
        b_blocks = tile_blocks(
            rows[h], peer_rows[h], counts, peer_counts[h], place, b_blocks, h * tile_half, tile_count
        )
    b_arrived = lax.all_to_all(b_blocks, "tile", split_axis=0, concat_axis=0, tiled=True)
    a_sums = None
    for h in range(2):
        a_blocks = x_blocks(rows[h], peer_rows[h], counts, peer_counts[h], place, h * tile_half)
        parts = [a_blocks[0]] + [x_send(a_blocks[k], k) for k in (1, 2, 3)]
        a_sums = sum_x(parts, a_sums, h * tile_half, tile_count)
    a_arrived = lax.all_to_all(a_sums, "tile", split_axis=0, concat_axis=0, tiled=True)
    b_sums = sum_tile(b_arrived)
    b_final = [b_sums[0]] + [x_send(b_sums[k], k) for k in (1, 2, 3)]
    plane, coded = own_plane(a_arrived, b_final, stencil)

    total = cut_count * tile_count

    def plane_send(k):
        pairs = [(i, i + k) for i in range(total) if 0 <= i + k < total]
        return lax.ppermute(coded, ("cuts", "tile"), pairs)

    halos = [plane_send(1), plane_send(2), plane_send(-1), plane_send(-2)]
    spot = here * tile_count + lax.axis_index("tile")
    edges = jnp.stack([spot > 0, spot < total - 1]).astype(jnp.int32)
    field, outgoing = smooth(edges, return_counts[0], plane, halos, return_slots[0])
    returned = lax.all_to_all(outgoing, "tile", split_axis=0, concat_axis=0, tiled=True)
    return field[None], returned


def solution(mesh):
    in_specs = (
        P(("cuts", "tile"), None),
        P("tile", None),
        P(("cuts", "tile"), None, None),
        P(("cuts", "tile"), None, None),
        P(("cuts", "tile"), None),
        P(("cuts", "tile"), None, None),
        P(("cuts", "tile"), None),
    )
    out_specs = (P(("cuts", "tile"), None, None), P(("cuts", "tile"), None, None))
    return jax.shard_map(local, mesh=mesh, in_specs=in_specs, out_specs=out_specs, check_vma=False)
```

```python
import functools
import math

import jax
import jax.numpy as jnp
from jax import lax
from jax.experimental import pallas as pl
from jax.experimental.pallas import tpu as pltpu
from jax.sharding import PartitionSpec as P

NX = 256
NY = 256
TAPS = 4
LA = 160
LB = NY - LA
ALPHA = math.log(2.0) / 64.0
TOP = 32700.0
CHUNK = 256
PICK = 32


def params(mib):
    return pltpu.CompilerParams(
        vmem_limit_bytes=mib * 1024 * 1024, dimension_semantics=("arbitrary",)
    )


def hbm(shape, dtype):
    return pltpu.HBM(shape, dtype)


def in_hbm(x):
    return pltpu.with_memory_space_constraint(x, pltpu.HBM)


def encode(block):
    top = to_row(jnp.max(jnp.abs(block), axis=1, keepdims=True))
    code = jnp.ceil(jnp.log(jnp.maximum(top, 1e-33)) * (1.0 / ALPHA))
    factor = to_column(TOP / jnp.exp(code * ALPHA))
    values = (block * factor + 12582912.0) - 12582912.0
    return values.astype(jnp.int32).astype(jnp.int16), code


def eye(size):
    return lax.broadcasted_iota(jnp.int32, (size, size), 0) == lax.broadcasted_iota(
        jnp.int32, (size, size), 1
    )


def to_row(column):
    return jnp.sum(jnp.where(eye(column.shape[0]), column, 0.0), axis=0, keepdims=True)


def to_column(row):
    return jnp.sum(jnp.where(eye(row.shape[1]), row, 0.0), axis=1, keepdims=True)


def decode(values, code_row):
    scale = jnp.exp(code_row * ALPHA) * (1.0 / TOP)
    return values.astype(jnp.int32).astype(jnp.float32) * to_column(scale)


def code_block(rows):
    block = jnp.zeros((16, NX), jnp.float32)
    index = lax.broadcasted_iota(jnp.int32, (16, NX), 0)
    for i, row in enumerate(rows):
        block = jnp.where(index == i, row, block)
    return block.astype(jnp.int32).astype(jnp.int16)


def widen_kernel(acq_ref, wide_ref, half_ref, sem):
    pieces = sem.shape[0]
    piece = half_ref.shape[0] // pieces
    copies = []
    for k in range(pieces):
        span = pl.ds(k * piece, piece)
        copies.append(pltpu.make_async_copy(acq_ref.at[span, :], half_ref.at[span, :], sem.at[k]))
        copies[k].start()
    for k in range(pieces):
        copies[k].wait()

        def widen(i, carry):
            span = pl.ds(pl.multiple_of(k * piece + i * CHUNK, CHUNK), CHUNK)
            wide_ref[span, :] = half_ref[span, :].astype(jnp.float32)
            return carry

        lax.fori_loop(0, piece // CHUNK, widen, 0)


def first_gather_kernel(
    slots_ref, counts_ref, acq_ref, lines_hbm, out_ref, wide_ref, lines_ref, half_ref, sem, line_sem,
    **sizes,
):
    fetch = pltpu.make_async_copy(lines_hbm, lines_ref, line_sem)

    @pl.when(pl.program_id(0) == 0)
    def _():
        fetch.start()
        widen_kernel(acq_ref, wide_ref, half_ref, sem)
        fetch.wait()

    gather_tile(slots_ref, counts_ref, lines_ref, out_ref, wide_ref, **sizes)


def next_gather_kernel(
    slots_ref, counts_ref, wide_ref, lines_hbm, out_ref, lines_ref, line_sem, **sizes
):
    fetch = pltpu.make_async_copy(lines_hbm, lines_ref, line_sem)

    @pl.when(pl.program_id(0) == 0)
    def _():
        fetch.start()
        fetch.wait()

    gather_tile(slots_ref, counts_ref, lines_ref, out_ref, wide_ref, **sizes)


def gather_tile(slots_ref, counts_ref, lines_ref, out_ref, wide_ref, *, first, cap):
    step = pl.program_id(0)
    count = counts_ref[first + step]
    start = (first + step) * cap

    def pick(i, carry):
        base = pl.multiple_of(i * PICK, PICK)
        rows = [wide_ref[pl.ds(slots_ref[start + base + u], 1), :] for u in range(PICK)]
        out_ref[0, pl.ds(base, PICK), :] = jnp.concatenate(rows, axis=0).astype(jnp.bfloat16)
        return carry

    def clear(i, carry):
        base = pl.multiple_of(i * PICK, PICK)
        out_ref[0, pl.ds(base, PICK), :] = jnp.zeros((PICK, NX), jnp.bfloat16)
        return carry

    picks = (count + PICK - 1) // PICK
    lax.fori_loop(0, picks, pick, 0)
    lax.fori_loop(picks, (count + CHUNK - 1) // CHUNK * (CHUNK // PICK), clear, 0)

    ids = lines_ref[pl.ds(first + step, 1), :]
    position = lax.broadcasted_iota(jnp.int32, ids.shape, 1)
    ids = jnp.where(position < count, ids + 1, 0)
    index = lax.broadcasted_iota(jnp.int32, (8, NX), 0)
    table = jnp.where(index == 7, count, 0)
    for i in range(cap // CHUNK):
        table = jnp.where(index == i, ids[:, i * CHUNK : (i + 1) * CHUNK], table)
    both = jnp.concatenate([table >> 6, table & 63], axis=0)
    out_ref[0, pl.ds(cap, 16), :] = both.astype(jnp.float32).astype(jnp.bfloat16)


def gather_rows(source, slots, counts, lines, first, tiles):
    cap = lines.shape[1]
    rows_spec = pl.BlockSpec((1, cap + 16, NX), lambda t, s, c: (t, 0, 0))
    rows_shape = hbm((tiles, cap + 16, NX), jnp.bfloat16)
    line_scratch = [pltpu.VMEM(lines.shape, jnp.int32)]
    line_sem = [pltpu.SemaphoreType.DMA]
    whole = pl.BlockSpec(memory_space=pltpu.VMEM)
    if first:
        body = next_gather_kernel
        source = pltpu.with_memory_space_constraint(source, pltpu.VMEM)
        source_spec = whole
        out_specs, out_shape = rows_spec, rows_shape
        scratch = line_scratch + line_sem
    else:
        body = first_gather_kernel
        source = pltpu.with_memory_space_constraint(source, pltpu.HBM)
        source_spec = pl.BlockSpec(memory_space=pltpu.HBM)
        out_specs = [rows_spec, whole]
        out_shape = [rows_shape, pltpu.VMEM(source.shape, jnp.float32)]
        scratch = (
            line_scratch
            + [pltpu.VMEM(source.shape, jnp.bfloat16), pltpu.SemaphoreType.DMA((8,))]
            + line_sem
        )
    return pl.pallas_call(
        functools.partial(body, first=first, cap=cap),
        grid_spec=pltpu.PrefetchScalarGridSpec(
            num_scalar_prefetch=2,
            grid=(tiles,),
            in_specs=[source_spec, pl.BlockSpec(memory_space=pltpu.HBM)],
            out_specs=out_specs,
            scratch_shapes=scratch,
        ),
        out_shape=out_shape,
        compiler_params=params(14),
        cost_estimate=pl.CostEstimate(flops=0, transcendentals=0, bytes_accessed=40_000_000),
        name="gather_rows",
    )(slots, counts, source, pltpu.with_memory_space_constraint(lines, pltpu.HBM))


def lines_kernel(
    own_n, peer_n, place_ref, own_hbm, peer_hbm, alias_ref,
    a0_ref, a1_ref, a2_ref, a3_ref, b_ref,
    acc_ref, code_ref, rows_ref, ids_ref, sem, *, first, cap,
):
    step = pl.program_id(0)
    last = pl.num_programs(0) - 1
    most = cap // CHUNK

    def chunks(tile):
        return (own_n[first + tile] + CHUNK - 1) // CHUNK, (peer_n[tile] + CHUNK - 1) // CHUNK

    def for_copies(tile, act):
        slot = lax.rem(tile, 2)
        own, peer = chunks(tile)
        for j, (source, base, count) in enumerate(((own_hbm, 0, own), (peer_hbm, own, peer))):
            for i in range(most):
                copy = pltpu.make_async_copy(
                    source.at[tile, pl.ds(i * CHUNK, CHUNK), :],
                    rows_ref.at[slot, pl.ds(pl.multiple_of((base + i) * CHUNK, CHUNK), CHUNK), :],
                    sem.at[slot, j * (most + 1) + i],
                )

                @pl.when(i < count)
                def _():
                    act(copy)

            act(
                pltpu.make_async_copy(
                    source.at[tile, pl.ds(cap, 16), :],
                    ids_ref.at[slot, j],
                    sem.at[slot, j * (most + 1) + most],
                )
            )

    @pl.when(step == 0)
    def _():
        for_copies(0, lambda copy: copy.start())

    @pl.when(step < last)
    def _():
        for_copies(step + 1, lambda copy: copy.start())

    for_copies(step, lambda copy: copy.wait())

    slot = lax.rem(step, 2)
    own, peer = chunks(step)
    here_core, here_x = place_ref[0], place_ref[1]
    for j in range(2):
        pair = ids_ref[slot, j].astype(jnp.float32).astype(jnp.int32)
        line = pair[0:8] * 64 + pair[8:16] - 1
        cut = line >> 8
        y = line & (NY - 1)
        mine = (line >= 0) & ((cut & 1) == here_core)
        ahead = ((cut >> 1) - here_x) & 3
        target = jnp.where(y < LA, ahead * LA + y, 4 * LA + ahead * LB + y - LA)
        target = jnp.where(mine, target, -1)
        for i in range(most):
            spot = i if j == 0 else own + i
            code_ref[4, pl.ds(spot, 1), :] = target[i : i + 1].astype(jnp.float32)

    acc_ref[...] = jnp.zeros(acc_ref.shape, jnp.float32)
    position = lax.broadcasted_iota(jnp.int32, (CHUNK, CHUNK), 0).astype(jnp.float32)

    def add(start, width):
        rows = rows_ref[slot, pl.ds(pl.multiple_of(start * CHUNK, CHUNK), width * CHUNK), :]
        ids = [code_ref[4, pl.ds(start + i, 1), :] for i in range(width)]
        for m in range(acc_ref.shape[0] // CHUNK):
            hot = [
                jnp.where(position == row - m * CHUNK, 1.0, 0.0).astype(jnp.bfloat16) for row in ids
            ]
            hot = jnp.concatenate(hot, axis=1) if width > 1 else hot[0]
            span = pl.ds(m * CHUNK, CHUNK)
            acc_ref[span, :] += jnp.dot(hot, rows, preferred_element_type=jnp.float32)

    total = own + peer

    def four(i, carry):
        add(i * 4, 4)
        return carry

    lax.fori_loop(0, total // 4, four, 0)
    for width in (1, 2, 3):

        @pl.when(total % 4 == width)
        def _():
            add(total // 4 * 4, width)

    outs = (a0_ref, a1_ref, a2_ref, a3_ref)
    for k in range(4):
        values, code = encode(acc_ref[pl.ds(k * LA, LA), :])
        outs[k][pl.ds(pl.multiple_of(step * LA, LA), LA), :] = values
        code_ref[k, pl.ds(step, 1), :] = pad_row(code)

    codes = []
    for k in range(4):
        values, code = encode(acc_ref[pl.ds(4 * LA + k * LB, LB), :])
        b_ref[0, pl.ds(k * LB, LB), :] = values
        codes.append(pad_row(code))
    b_ref[0, pl.ds(4 * LB, 16), :] = code_block(codes)

    @pl.when(step == last)
    def _():
        for k in range(4):
            outs[k][pl.ds((last + 1) * LA, 16), :] = code_ref[k].astype(jnp.int32).astype(jnp.int16)


def pad_row(row):
    return jnp.concatenate([row, jnp.zeros((1, NX - row.shape[1]), jnp.float32)], axis=1)


def line_blocks(own_rows, peer_rows, own_n, peer_n, place, b_old, first, tiles_all):
    tiles, cap, _ = own_rows.shape
    cap -= 16
    a_shape = (tiles * LA + 16, NX)
    own_rows = pltpu.with_memory_space_constraint(own_rows, pltpu.HBM)
    peer_rows = pltpu.with_memory_space_constraint(peer_rows, pltpu.HBM)
    args = [own_n, peer_n, place, own_rows, peer_rows]
    aliases = {}
    if b_old is None:
        b_old = jnp.zeros((16, NX), jnp.int16)
    else:
        aliases = {5: 4}
    args.append(b_old)
    return pl.pallas_call(
        functools.partial(lines_kernel, first=first, cap=cap),
        grid_spec=pltpu.PrefetchScalarGridSpec(
            num_scalar_prefetch=3,
            grid=(tiles,),
            in_specs=[pl.BlockSpec(memory_space=pltpu.HBM)] * 2
            + [pl.BlockSpec(memory_space=pl.ANY)],
            out_specs=[pl.BlockSpec(a_shape, lambda t, *_: (0, 0))] * 4
            + [pl.BlockSpec((1, 4 * LB + 16, NX), lambda t, *_: (t + first, 0, 0))],
            scratch_shapes=[
                pltpu.VMEM((4 * NY, NX), jnp.float32),
                pltpu.VMEM((5, 16, NX), jnp.float32),
                pltpu.VMEM((2, 2 * cap, NX), jnp.bfloat16),
                pltpu.VMEM((2, 2, 16, NX), jnp.bfloat16),
                pltpu.SemaphoreType.DMA((2, 2 * (cap // CHUNK + 1))),
            ],
        ),
        out_shape=[hbm(a_shape, jnp.int16)] * 4
        + [hbm((tiles_all, 4 * LB + 16, NX), jnp.int16)],
        input_output_aliases=aliases,
        compiler_params=params(16),
        cost_estimate=pl.CostEstimate(
            flops=2 * 1024 * 256 * 20480, transcendentals=0, bytes_accessed=40_000_000
        ),
        name="line_blocks",
    )(*args)


def code_row(block, index, length):
    table = block.astype(jnp.int32).astype(jnp.float32)
    rows = lax.broadcasted_iota(jnp.int32, table.shape, 0)
    row = jnp.sum(jnp.where(rows == index, table, 0.0), axis=0, keepdims=True)
    return row[:, 0:length]


def sum_x_kernel(p0, p1, p2, p3, alias_ref, out_ref, sum_ref, sem, *, first):
    tiles = sum_ref.shape[0]

    def copy_out(i):
        return pltpu.make_async_copy(sum_ref.at[i], out_ref.at[first + i], sem.at[i])

    for i in range(tiles):
        total = jnp.zeros((LA, NX), jnp.float32)
        for part in (p0, p1, p2, p3):
            codes = code_row(part[pl.ds(tiles * LA, 16), :], i, LA)
            total = total + decode(part[pl.ds(i * LA, LA), :], codes)
        values, code = encode(total)
        sum_ref[i, pl.ds(0, LA), :] = values
        sum_ref[i, pl.ds(LA, 16), :] = code_block([pad_row(code)])
        copy_out(i).start()
    for i in range(tiles):
        copy_out(i).wait()


def sum_x(parts, old, first, tiles_all):
    tiles = (parts[0].shape[0] - 16) // LA
    aliases = {}
    if old is None:
        old = jnp.zeros((16, NX), jnp.int16)
    else:
        aliases = {4: 0}
    return pl.pallas_call(
        functools.partial(sum_x_kernel, first=first),
        in_specs=[pl.BlockSpec(memory_space=pltpu.VMEM)] * 4 + [pl.BlockSpec(memory_space=pl.ANY)],
        out_specs=pl.BlockSpec(memory_space=pltpu.HBM),
        out_shape=hbm((tiles_all, LA + 16, NX), jnp.int16),
        scratch_shapes=[
            pltpu.VMEM((tiles, LA + 16, NX), jnp.int16),
            pltpu.SemaphoreType.DMA((tiles,)),
        ],
        input_output_aliases=aliases,
        compiler_params=pltpu.CompilerParams(vmem_limit_bytes=12 * 1024 * 1024),
        name="sum_x",
    )(*parts, old)


def sum_tile_kernel(in_hbm_ref, o0, o1, o2, o3, acc_ref, in_ref, sem):
    tiles = in_ref.shape[0]

    def fetch(t):
        return pltpu.make_async_copy(in_hbm_ref.at[t], in_ref.at[t], sem.at[t])

    for t in range(tiles):
        fetch(t).start()
    acc_ref[...] = jnp.zeros(acc_ref.shape, jnp.float32)

    def body(t, carry):
        fetch(t).wait()
        table = in_ref[t, pl.ds(4 * LB, 16), :].astype(jnp.int32).astype(jnp.float32)
        for k in range(4):
            acc_ref[pl.ds(k * LB, LB), :] += decode(
                in_ref[t, pl.ds(k * LB, LB), :], table[k : k + 1, 0:LB]
            )
        return carry

    lax.fori_loop(0, tiles, body, 0)
    for k, out in enumerate((o0, o1, o2, o3)):
        values, code = encode(acc_ref[pl.ds(k * LB, LB), :])
        out[pl.ds(0, LB), :] = values
        out[pl.ds(LB, 16), :] = code_block([pad_row(code)])


def sum_tile(arrived):
    out_shape = (LB + 16, NX)
    return pl.pallas_call(
        sum_tile_kernel,
        in_specs=[pl.BlockSpec(memory_space=pltpu.HBM)],
        out_shape=[jax.ShapeDtypeStruct(out_shape, jnp.int16)] * 4,
        scratch_shapes=[
            pltpu.VMEM((4 * LB, NX), jnp.float32),
            pltpu.VMEM(arrived.shape, jnp.int16),
            pltpu.SemaphoreType.DMA(arrived.shape[:1]),
        ],
        compiler_params=pltpu.CompilerParams(vmem_limit_bytes=12 * 1024 * 1024),
        name="sum_tile",
    )(in_hbm(arrived))


def plane_kernel(a_ref, b0, b1, b2, b3, stencil_ref, plane_ref, send_ref, lines_ref):
    def body(i, carry):
        codes = code_row(a_ref[i, pl.ds(LA, 16), :], 0, LA)
        lines_ref[pl.ds(0, LA), :] += decode(a_ref[i, pl.ds(0, LA), :], codes)
        return carry

    lines_ref[pl.ds(0, LA), :] = jnp.zeros((LA, NX), jnp.float32)
    lax.fori_loop(0, a_ref.shape[0], body, 0)
    total = jnp.zeros((LB, NX), jnp.float32)
    for b in (b0, b1, b2, b3):
        total = total + decode(b[pl.ds(0, LB), :], code_row(b[pl.ds(LB, 16), :], 0, LB))
    lines_ref[pl.ds(LA, LB), :] = total

    lines = lines_ref[...]
    high = lines.astype(jnp.bfloat16)
    rest = lines - high.astype(jnp.float32)
    mid = rest.astype(jnp.bfloat16)
    low = (rest - mid.astype(jnp.float32)).astype(jnp.bfloat16)
    plane = jnp.zeros((NY, NX), jnp.float32)
    for k in range(TAPS):
        weights = stencil_ref[:, k * NX : (k + 1) * NX]
        product = jnp.dot(high, weights, preferred_element_type=jnp.float32)
        product += jnp.dot(mid, weights, preferred_element_type=jnp.float32)
        product += jnp.dot(low, weights, preferred_element_type=jnp.float32)
        if k:
            product = pltpu.roll(product, k, 0)
        plane = plane + product
    plane_ref[...] = plane
    rows = []
    for h in range(2):
        values, code = encode(plane[h * 128 : (h + 1) * 128])
        send_ref[pl.ds(h * 128, 128), :] = values
        rows.append(code)
    send_ref[pl.ds(NY, 16), :] = code_block([jnp.concatenate(rows, axis=1)])


def own_plane(a, bs, stencil):
    return pl.pallas_call(
        plane_kernel,
        out_shape=[
            jax.ShapeDtypeStruct((NY, NX), jnp.float32),
            jax.ShapeDtypeStruct((NY + 16, NX), jnp.int16),
        ],
        scratch_shapes=[pltpu.VMEM((NY, NX), jnp.float32)],
        compiler_params=pltpu.CompilerParams(vmem_limit_bytes=12 * 1024 * 1024),
        name="own_plane",
    )(a, *bs, stencil)


def smooth_kernel(edge_ref, counts_ref, plane_ref, l1, l2, r1, r2, reads_ref, out_ref, back_ref):
    def halo(ref):
        table = ref[pl.ds(NY, 16), :].astype(jnp.int32).astype(jnp.float32)
        parts = [
            decode(ref[pl.ds(h * 128, 128), :], table[0:1, h * 128 : (h + 1) * 128])
            for h in range(2)
        ]
        return jnp.concatenate(parts, axis=0)

    row = lax.broadcasted_iota(jnp.int32, (NY, NX), 0)
    col = lax.broadcasted_iota(jnp.int32, (NY, NX), 1)

    def step(below, mid, above):
        near = jnp.where(row == 0, 0.0, pltpu.roll(mid, 1, 0))
        near += jnp.where(row == NY - 1, 0.0, pltpu.roll(mid, NY - 1, 0))
        near += jnp.where(col == 0, 0.0, pltpu.roll(mid, 1, 1))
        near += jnp.where(col == NX - 1, 0.0, pltpu.roll(mid, NX - 1, 1))
        return mid + 0.15 * (near + below + above - 6.0 * mid)

    plane = plane_ref[...]
    left, right = halo(l1), halo(r1)
    lower = step(halo(l2), left, plane)
    upper = step(plane, right, halo(r2))
    lower = jnp.where(edge_ref[0] > 0, lower, 0.0)
    upper = jnp.where(edge_ref[1] > 0, upper, 0.0)
    field = step(lower, step(left, plane, right), upper).astype(jnp.bfloat16)
    out_ref[...] = field

    readers, most = reads_ref.shape
    lane = lax.broadcasted_iota(jnp.int32, (1, most), 1)
    columns = lax.broadcasted_iota(jnp.int32, (most, NY), 1).astype(jnp.float32)
    for t in range(readers):
        ids = jnp.where(lane < counts_ref[t], reads_ref[pl.ds(t, 1), :], -1)
        hot = jnp.where(columns == to_column(ids.astype(jnp.float32)), 1.0, 0.0)
        lines = jnp.dot(hot.astype(jnp.bfloat16), field, preferred_element_type=jnp.float32)
        back_ref[t] = lines.astype(jnp.bfloat16)


def smooth(edges, counts, plane, halos, reads):
    vmem = pl.BlockSpec(memory_space=pltpu.VMEM)
    smem = pl.BlockSpec(memory_space=pltpu.SMEM)
    readers, most = reads.shape
    return pl.pallas_call(
        smooth_kernel,
        in_specs=[smem, smem] + [vmem] * 6,
        out_specs=[vmem, vmem],
        out_shape=[
            jax.ShapeDtypeStruct((NY, NX), jnp.bfloat16),
            jax.ShapeDtypeStruct((readers, most, NX), jnp.bfloat16),
        ],
        compiler_params=pltpu.CompilerParams(vmem_limit_bytes=12 * 1024 * 1024),
        name="smooth",
    )(edges, counts, plane, *halos, reads)


def after_kernel(x_ref, *refs):
    del x_ref, refs


def after(x, others):
    anywhere = pl.BlockSpec(memory_space=pl.ANY)
    return pl.pallas_call(
        after_kernel,
        in_specs=[anywhere] * (1 + len(others)),
        out_specs=anywhere,
        out_shape=hbm(x.shape, x.dtype),
        input_output_aliases={0: 0},
        name="after",
    )(x, *others)


def local(acquired, stencil, send_slots, send_lines, send_counts, return_slots, return_counts):
    tile_count = lax.axis_size("tile")
    cut_count = lax.axis_size("cuts")
    tile_half = tile_count // 2
    here = lax.axis_index("cuts")
    here_x = here // 2
    here_core = here % 2
    place = jnp.stack([here_core, here_x]).astype(jnp.int32)
    counts = send_counts[0]
    flat_slots = send_slots.reshape(-1)
    swap = [(i, i ^ 1) for i in range(cut_count)]

    rows, peer_rows = [], []
    for h in range(2):
        source = wide if h else acquired
        made = gather_rows(source, flat_slots, counts, send_lines[0], h * tile_half, tile_half)
        if not h:
            made, wide = made
        rows.append(made)
        peer_rows.append(lax.ppermute(rows[h], "cuts", swap))
    cap = send_slots.shape[2]
    peer_counts = [
        (part[:, cap + 7, 0].astype(jnp.float32) * 64 + part[:, cap + 15, 0].astype(jnp.float32))
        .astype(jnp.int32)
        for part in peer_rows
    ]

    def x_send(block, k):
        return lax.ppermute(block, "cuts", [(i, (i + 2 * k) % cut_count) for i in range(cut_count)])

    b_blocks = None
    a_parts = []
    for h in range(2):
        *a_blocks, b_blocks = line_blocks(
            rows[h], peer_rows[h], counts, peer_counts[h], place,
            b_blocks, h * tile_half, tile_count,
        )
        a_parts.append([a_blocks[0]] + [x_send(a_blocks[k], k) for k in (1, 2, 3)])
    near = (a_parts[0][1][:16], a_parts[0][3][:16])
    b_blocks = after(b_blocks, near)
    b_arrived = lax.all_to_all(b_blocks, "tile", split_axis=0, concat_axis=0, tiled=True)
    a_sums = None
    for h in range(2):
        a_sums = sum_x(a_parts[h], a_sums, h * tile_half, tile_count)
    a_arrived = lax.all_to_all(a_sums, "tile", split_axis=0, concat_axis=0, tiled=True)
    b_sums = sum_tile(b_arrived)
    b_final = [b_sums[0]] + [x_send(b_sums[k], k) for k in (1, 2, 3)]
    plane, coded = own_plane(a_arrived, b_final, stencil)

    total = cut_count * tile_count

    def plane_send(k):
        pairs = [(i, i + k) for i in range(total) if 0 <= i + k < total]
        return lax.ppermute(coded, ("cuts", "tile"), pairs)

    halos = [plane_send(1), plane_send(2), plane_send(-1), plane_send(-2)]
    spot = here * tile_count + lax.axis_index("tile")
    edges = jnp.stack([spot > 0, spot < total - 1]).astype(jnp.int32)
    field, outgoing = smooth(edges, return_counts[0], plane, halos, return_slots[0])
    returned = lax.all_to_all(outgoing, "tile", split_axis=0, concat_axis=0, tiled=True)
    return field[None], pltpu.with_memory_space_constraint(returned, pltpu.HBM)


def solution(mesh):
    in_specs = (
        P(("cuts", "tile"), None),
        P("tile", None),
        P(("cuts", "tile"), None, None),
        P(("cuts", "tile"), None, None),
        P(("cuts", "tile"), None),
        P(("cuts", "tile"), None, None),
        P(("cuts", "tile"), None),
    )
    out_specs = (P(("cuts", "tile"), None, None), P(("cuts", "tile"), None, None))
    return jax.shard_map(local, mesh=mesh, in_specs=in_specs, out_specs=out_specs, check_vma=False)
```

```python
import functools
import math

import jax
import jax.numpy as jnp
from jax import lax
from jax.experimental import pallas as pl
from jax.experimental.pallas import tpu as pltpu
from jax.sharding import PartitionSpec as P

NX = 256
NY = 256
TAPS = 4
SPLIT = 6
LA = 160
LB = NY - LA
ALPHA = math.log(2.0) / 64.0
TOP = 32700.0
CHUNK = 256
PICK = 32


def params(mib):
    return pltpu.CompilerParams(
        vmem_limit_bytes=mib * 1024 * 1024, dimension_semantics=("arbitrary",)
    )


def hbm(shape, dtype):
    return pltpu.HBM(shape, dtype)


def in_hbm(x):
    return pltpu.with_memory_space_constraint(x, pltpu.HBM)


def encode(block):
    top = to_row(jnp.max(jnp.abs(block), axis=1, keepdims=True))
    code = jnp.ceil(jnp.log(jnp.maximum(top, 1e-33)) * (1.0 / ALPHA))
    factor = to_column(TOP / jnp.exp(code * ALPHA))
    values = (block * factor + 12582912.0) - 12582912.0
    return values.astype(jnp.int32).astype(jnp.int16), code


def eye(size):
    return lax.broadcasted_iota(jnp.int32, (size, size), 0) == lax.broadcasted_iota(
        jnp.int32, (size, size), 1
    )


def to_row(column):
    return jnp.sum(jnp.where(eye(column.shape[0]), column, 0.0), axis=0, keepdims=True)


def to_column(row):
    return jnp.sum(jnp.where(eye(row.shape[1]), row, 0.0), axis=1, keepdims=True)


def decode(values, code_row):
    scale = jnp.exp(code_row * ALPHA) * (1.0 / TOP)
    return values.astype(jnp.int32).astype(jnp.float32) * to_column(scale)


def code_block(rows):
    block = jnp.zeros((16, NX), jnp.float32)
    index = lax.broadcasted_iota(jnp.int32, (16, NX), 0)
    for i, row in enumerate(rows):
        block = jnp.where(index == i, row, block)
    return block.astype(jnp.int32).astype(jnp.int16)


def widen_kernel(acq_ref, wide_ref, half_ref, sem):
    pieces = sem.shape[0]
    piece = half_ref.shape[0] // pieces
    copies = []
    for k in range(pieces):
        span = pl.ds(k * piece, piece)
        copies.append(pltpu.make_async_copy(acq_ref.at[span, :], half_ref.at[span, :], sem.at[k]))
        copies[k].start()
    for k in range(pieces):
        copies[k].wait()

        def widen(i, carry):
            span = pl.ds(pl.multiple_of(k * piece + i * CHUNK, CHUNK), CHUNK)
            wide_ref[span, :] = half_ref[span, :].astype(jnp.float32)
            return carry

        lax.fori_loop(0, piece // CHUNK, widen, 0)


def first_gather_kernel(
    slots_ref, counts_ref, acq_ref, lines_hbm, out_ref, wide_ref, lines_ref, half_ref, sem, line_sem,
    **sizes,
):
    fetch = pltpu.make_async_copy(lines_hbm, lines_ref, line_sem)

    @pl.when(pl.program_id(0) == 0)
    def _():
        fetch.start()
        widen_kernel(acq_ref, wide_ref, half_ref, sem)
        fetch.wait()

    gather_tile(slots_ref, counts_ref, lines_ref, out_ref, wide_ref, **sizes)


def next_gather_kernel(
    slots_ref, counts_ref, wide_ref, lines_hbm, out_ref, lines_ref, line_sem, **sizes
):
    fetch = pltpu.make_async_copy(lines_hbm, lines_ref, line_sem)

    @pl.when(pl.program_id(0) == 0)
    def _():
        fetch.start()
        fetch.wait()

    gather_tile(slots_ref, counts_ref, lines_ref, out_ref, wide_ref, **sizes)


def gather_tile(slots_ref, counts_ref, lines_ref, out_ref, wide_ref, *, first, cap):
    step = pl.program_id(0)
    count = counts_ref[first + step]
    start = (first + step) * cap

    def pick(i, carry):
        base = pl.multiple_of(i * PICK, PICK)
        rows = [wide_ref[pl.ds(slots_ref[start + base + u], 1), :] for u in range(PICK)]
        out_ref[0, pl.ds(base, PICK), :] = jnp.concatenate(rows, axis=0).astype(jnp.bfloat16)
        return carry

    def clear(i, carry):
        base = pl.multiple_of(i * PICK, PICK)
        out_ref[0, pl.ds(base, PICK), :] = jnp.zeros((PICK, NX), jnp.bfloat16)
        return carry

    picks = (count + PICK - 1) // PICK
    lax.fori_loop(0, picks, pick, 0)
    lax.fori_loop(picks, (count + CHUNK - 1) // CHUNK * (CHUNK // PICK), clear, 0)

    ids = lines_ref[pl.ds(first + step, 1), :]
    position = lax.broadcasted_iota(jnp.int32, ids.shape, 1)
    ids = jnp.where(position < count, ids + 1, 0)
    index = lax.broadcasted_iota(jnp.int32, (8, NX), 0)
    table = jnp.where(index == 7, count, 0)
    for i in range(cap // CHUNK):
        table = jnp.where(index == i, ids[:, i * CHUNK : (i + 1) * CHUNK], table)
    both = jnp.concatenate([table >> 6, table & 63], axis=0)
    out_ref[0, pl.ds(cap, 16), :] = both.astype(jnp.float32).astype(jnp.bfloat16)


def gather_rows(source, slots, counts, lines, first, tiles):
    cap = lines.shape[1]
    rows_spec = pl.BlockSpec((1, cap + 16, NX), lambda t, s, c: (t, 0, 0))
    rows_shape = hbm((tiles, cap + 16, NX), jnp.bfloat16)
    line_scratch = [pltpu.VMEM(lines.shape, jnp.int32)]
    line_sem = [pltpu.SemaphoreType.DMA]
    whole = pl.BlockSpec(memory_space=pltpu.VMEM)
    if first:
        body = next_gather_kernel
        source = pltpu.with_memory_space_constraint(source, pltpu.VMEM)
        source_spec = whole
        out_specs, out_shape = rows_spec, rows_shape
        scratch = line_scratch + line_sem
    else:
        body = first_gather_kernel
        source = pltpu.with_memory_space_constraint(source, pltpu.HBM)
        source_spec = pl.BlockSpec(memory_space=pltpu.HBM)
        out_specs = [rows_spec, whole]
        out_shape = [rows_shape, pltpu.VMEM(source.shape, jnp.float32)]
        scratch = (
            line_scratch
            + [pltpu.VMEM(source.shape, jnp.bfloat16), pltpu.SemaphoreType.DMA((8,))]
            + line_sem
        )
    return pl.pallas_call(
        functools.partial(body, first=first, cap=cap),
        grid_spec=pltpu.PrefetchScalarGridSpec(
            num_scalar_prefetch=2,
            grid=(tiles,),
            in_specs=[source_spec, pl.BlockSpec(memory_space=pltpu.HBM)],
            out_specs=out_specs,
            scratch_shapes=scratch,
        ),
        out_shape=out_shape,
        compiler_params=params(14),
        cost_estimate=pl.CostEstimate(flops=0, transcendentals=0, bytes_accessed=40_000_000),
        name="gather_rows",
    )(slots, counts, source, pltpu.with_memory_space_constraint(lines, pltpu.HBM))


def lines_kernel(own_n, peer_n, place_ref, *refs, first, cap, sources):
    own_refs, peer_refs = refs[:sources], refs[sources : 2 * sources]
    a0_ref, a1_ref, a2_ref, a3_ref, b_ref = refs[2 * sources + 1 : 2 * sources + 6]
    acc_ref, code_ref, rows_ref, ids_ref, sem = refs[2 * sources + 6 :]
    held = own_refs[0].shape[0]
    step = pl.program_id(0)
    last = pl.num_programs(0) - 1
    most = cap // CHUNK

    def chunks(tile):
        return (own_n[first + tile] + CHUNK - 1) // CHUNK, (
            peer_n[first + tile] + CHUNK - 1
        ) // CHUNK

    def for_copies(tile, own_ref, peer_ref, row, act):
        slot = lax.rem(tile, 2)
        own, peer = chunks(tile)
        for j, (source, base, count) in enumerate(((own_ref, 0, own), (peer_ref, own, peer))):
            for i in range(most):

                @pl.when(i < count)
                def _():
                    act(
                        pltpu.make_async_copy(
                            source.at[row, pl.ds(i * CHUNK, CHUNK), :],
                            rows_ref.at[
                                slot, pl.ds(pl.multiple_of((base + i) * CHUNK, CHUNK), CHUNK), :
                            ],
                            sem.at[slot, j * (most + 1) + i],
                        )
                    )

            act(
                pltpu.make_async_copy(
                    source.at[row, pl.ds(cap, 16), :],
                    ids_ref.at[slot, j],
                    sem.at[slot, j * (most + 1) + most],
                )
            )

    def start(tile):
        for k in range(sources):

            @pl.when((first + tile) // held == k)
            def _():
                row = first + tile - k * held
                for_copies(tile, own_refs[k], peer_refs[k], row, lambda copy: copy.start())

    @pl.when(step == 0)
    def _():
        start(step)

    @pl.when(step < last)
    def _():
        start(step + 1)

    for_copies(step, own_refs[0], peer_refs[0], 0, lambda copy: copy.wait())

    slot = lax.rem(step, 2)
    own, peer = chunks(step)
    here_core, here_x = place_ref[0], place_ref[1]
    for j in range(2):
        pair = ids_ref[slot, j].astype(jnp.float32).astype(jnp.int32)
        line = pair[0:8] * 64 + pair[8:16] - 1
        cut = line >> 8
        y = line & (NY - 1)
        mine = (line >= 0) & ((cut & 1) == here_core)
        ahead = ((cut >> 1) - here_x) & 3
        target = jnp.where(y < LA, ahead * LA + y, 4 * LA + ahead * LB + y - LA)
        target = jnp.where(mine, target, -1)
        for i in range(most):
            spot = i if j == 0 else own + i
            code_ref[4, pl.ds(spot, 1), :] = target[i : i + 1].astype(jnp.float32)

    acc_ref[...] = jnp.zeros(acc_ref.shape, jnp.float32)
    position = lax.broadcasted_iota(jnp.int32, (CHUNK, CHUNK), 0).astype(jnp.float32)

    def add(start, width):
        rows = rows_ref[slot, pl.ds(pl.multiple_of(start * CHUNK, CHUNK), width * CHUNK), :]
        ids = [code_ref[4, pl.ds(start + i, 1), :] for i in range(width)]
        for m in range(acc_ref.shape[0] // CHUNK):
            hot = [
                jnp.where(position == row - m * CHUNK, 1.0, 0.0).astype(jnp.bfloat16) for row in ids
            ]
            hot = jnp.concatenate(hot, axis=1) if width > 1 else hot[0]
            span = pl.ds(m * CHUNK, CHUNK)
            acc_ref[span, :] += jnp.dot(hot, rows, preferred_element_type=jnp.float32)

    total = own + peer

    def four(i, carry):
        add(i * 4, 4)
        return carry

    lax.fori_loop(0, total // 4, four, 0)
    for width in (1, 2, 3):

        @pl.when(total % 4 == width)
        def _():
            add(total // 4 * 4, width)

    outs = (a0_ref, a1_ref, a2_ref, a3_ref)
    for k in range(4):
        values, code = encode(acc_ref[pl.ds(k * LA, LA), :])
        outs[k][pl.ds(pl.multiple_of(step * LA, LA), LA), :] = values
        code_ref[k, pl.ds(step, 1), :] = pad_row(code)

    codes = []
    for k in range(4):
        values, code = encode(acc_ref[pl.ds(4 * LA + k * LB, LB), :])
        b_ref[0, pl.ds(k * LB, LB), :] = values
        codes.append(pad_row(code))
    b_ref[0, pl.ds(4 * LB, 16), :] = code_block(codes)

    @pl.when(step == last)
    def _():
        for k in range(4):
            outs[k][pl.ds((last + 1) * LA, 16), :] = code_ref[k].astype(jnp.int32).astype(jnp.int16)


def pad_row(row):
    return jnp.concatenate([row, jnp.zeros((1, NX - row.shape[1]), jnp.float32)], axis=1)


def line_blocks(own_rows, peer_rows, own_n, peer_n, place, b_old, first, tiles, tiles_all):
    cap = own_rows[0].shape[1] - 16
    sources = len(own_rows)
    a_shape = (tiles * LA + 16, NX)
    args = [own_n, peer_n, place] + [in_hbm(rows) for rows in own_rows + peer_rows]
    aliases = {}
    if b_old is None:
        b_old = jnp.zeros((16, NX), jnp.int16)
    else:
        aliases = {len(args): 4}
    args.append(b_old)
    return pl.pallas_call(
        functools.partial(lines_kernel, first=first, cap=cap, sources=sources),
        grid_spec=pltpu.PrefetchScalarGridSpec(
            num_scalar_prefetch=3,
            grid=(tiles,),
            in_specs=[pl.BlockSpec(memory_space=pltpu.HBM)] * (2 * sources)
            + [pl.BlockSpec(memory_space=pl.ANY)],
            out_specs=[pl.BlockSpec(a_shape, lambda t, *_: (0, 0))] * 4
            + [pl.BlockSpec((1, 4 * LB + 16, NX), lambda t, *_: (t + first, 0, 0))],
            scratch_shapes=[
                pltpu.VMEM((4 * NY, NX), jnp.float32),
                pltpu.VMEM((5, 16, NX), jnp.float32),
                pltpu.VMEM((2, 2 * cap, NX), jnp.bfloat16),
                pltpu.VMEM((2, 2, 16, NX), jnp.bfloat16),
                pltpu.SemaphoreType.DMA((2, 2 * (cap // CHUNK + 1))),
            ],
        ),
        out_shape=[hbm(a_shape, jnp.int16)] * 4
        + [hbm((tiles_all, 4 * LB + 16, NX), jnp.int16)],
        input_output_aliases=aliases,
        compiler_params=params(16),
        name="line_blocks",
    )(*args)


def code_row(block, index, length):
    table = block.astype(jnp.int32).astype(jnp.float32)
    rows = lax.broadcasted_iota(jnp.int32, table.shape, 0)
    row = jnp.sum(jnp.where(rows == index, table, 0.0), axis=0, keepdims=True)
    return row[:, 0:length]


def sum_x_kernel(p0, p1, p2, p3, alias_ref, wait_ref, out_ref, token_ref, sum_ref, sem, *, first):
    tiles = sum_ref.shape[0]

    def copy_out(i):
        return pltpu.make_async_copy(sum_ref.at[i], out_ref.at[first + i], sem.at[i])

    for i in range(tiles):
        total = jnp.zeros((LA, NX), jnp.float32)
        for part in (p0, p1, p2, p3):
            codes = code_row(part[pl.ds(tiles * LA, 16), :], i, LA)
            total = total + decode(part[pl.ds(i * LA, LA), :], codes)
        values, code = encode(total)
        sum_ref[i, pl.ds(0, LA), :] = values
        sum_ref[i, pl.ds(LA, 16), :] = code_block([pad_row(code)])
        copy_out(i).start()
    token_ref[...] = jnp.zeros(token_ref.shape, jnp.float32)
    for i in range(tiles):
        copy_out(i).wait()


def sum_x(parts, old, later, first, tiles_all):
    tiles = (parts[0].shape[0] - 16) // LA
    aliases = {4: 0} if first else {}
    return pl.pallas_call(
        functools.partial(sum_x_kernel, first=first),
        in_specs=[pl.BlockSpec(memory_space=pltpu.VMEM)] * 4
        + [pl.BlockSpec(memory_space=pl.ANY)] * 2,
        out_specs=[pl.BlockSpec(memory_space=pltpu.HBM), pl.BlockSpec(memory_space=pltpu.VMEM)],
        out_shape=[
            hbm((tiles_all, LA + 16, NX), jnp.int16),
            jax.ShapeDtypeStruct((8, 128), jnp.float32),
        ],
        scratch_shapes=[
            pltpu.VMEM((tiles, LA + 16, NX), jnp.int16),
            pltpu.SemaphoreType.DMA((tiles,)),
        ],
        input_output_aliases=aliases,
        compiler_params=pltpu.CompilerParams(vmem_limit_bytes=12 * 1024 * 1024),
        name="sum_x",
    )(*parts, old, later)


def sum_tile_kernel(in_hbm_ref, o0, o1, o2, o3, acc_ref, in_ref, sem):
    tiles = in_ref.shape[0]

    def fetch(t):
        return pltpu.make_async_copy(in_hbm_ref.at[t], in_ref.at[t], sem.at[t])

    for t in range(tiles):
        fetch(t).start()
    acc_ref[...] = jnp.zeros(acc_ref.shape, jnp.float32)

    def body(t, carry):
        fetch(t).wait()
        table = in_ref[t, pl.ds(4 * LB, 16), :].astype(jnp.int32).astype(jnp.float32)
        for k in range(4):
            acc_ref[pl.ds(k * LB, LB), :] += decode(
                in_ref[t, pl.ds(k * LB, LB), :], table[k : k + 1, 0:LB]
            )
        return carry

    lax.fori_loop(0, tiles, body, 0)
    for k, out in enumerate((o0, o1, o2, o3)):
        values, code = encode(acc_ref[pl.ds(k * LB, LB), :])
        out[pl.ds(0, LB), :] = values
        out[pl.ds(LB, 16), :] = code_block([pad_row(code)])


def sum_tile(arrived):
    out_shape = (LB + 16, NX)
    return pl.pallas_call(
        sum_tile_kernel,
        in_specs=[pl.BlockSpec(memory_space=pltpu.HBM)],
        out_shape=[jax.ShapeDtypeStruct(out_shape, jnp.int16)] * 4,
        scratch_shapes=[
            pltpu.VMEM((4 * LB, NX), jnp.float32),
            pltpu.VMEM(arrived.shape, jnp.int16),
            pltpu.SemaphoreType.DMA(arrived.shape[:1]),
        ],
        compiler_params=pltpu.CompilerParams(vmem_limit_bytes=12 * 1024 * 1024),
        name="sum_tile",
    )(in_hbm(arrived))


def plane_kernel(a_ref, b0, b1, b2, b3, stencil_ref, plane_ref, send_ref, lines_ref):
    def body(i, carry):
        codes = code_row(a_ref[i, pl.ds(LA, 16), :], 0, LA)
        lines_ref[pl.ds(0, LA), :] += decode(a_ref[i, pl.ds(0, LA), :], codes)
        return carry

    lines_ref[pl.ds(0, LA), :] = jnp.zeros((LA, NX), jnp.float32)
    lax.fori_loop(0, a_ref.shape[0], body, 0)
    total = jnp.zeros((LB, NX), jnp.float32)
    for b in (b0, b1, b2, b3):
        total = total + decode(b[pl.ds(0, LB), :], code_row(b[pl.ds(LB, 16), :], 0, LB))
    lines_ref[pl.ds(LA, LB), :] = total

    lines = lines_ref[...]
    high = lines.astype(jnp.bfloat16)
    rest = lines - high.astype(jnp.float32)
    mid = rest.astype(jnp.bfloat16)
    low = (rest - mid.astype(jnp.float32)).astype(jnp.bfloat16)
    plane = jnp.zeros((NY, NX), jnp.float32)
    for k in range(TAPS):
        weights = stencil_ref[:, k * NX : (k + 1) * NX]
        product = jnp.dot(high, weights, preferred_element_type=jnp.float32)
        product += jnp.dot(mid, weights, preferred_element_type=jnp.float32)
        product += jnp.dot(low, weights, preferred_element_type=jnp.float32)
        if k:
            product = pltpu.roll(product, k, 0)
        plane = plane + product
    plane_ref[...] = plane
    rows = []
    for h in range(2):
        values, code = encode(plane[h * 128 : (h + 1) * 128])
        send_ref[pl.ds(h * 128, 128), :] = values
        rows.append(code)
    send_ref[pl.ds(NY, 16), :] = code_block([jnp.concatenate(rows, axis=1)])


def own_plane(a, bs, stencil):
    return pl.pallas_call(
        plane_kernel,
        out_shape=[
            jax.ShapeDtypeStruct((NY, NX), jnp.float32),
            jax.ShapeDtypeStruct((NY + 16, NX), jnp.int16),
        ],
        scratch_shapes=[pltpu.VMEM((NY, NX), jnp.float32)],
        compiler_params=pltpu.CompilerParams(vmem_limit_bytes=12 * 1024 * 1024),
        name="own_plane",
    )(a, *bs, stencil)


def smooth_kernel(edge_ref, counts_ref, plane_ref, l1, l2, r1, r2, reads_ref, out_ref, back_ref):
    def halo(ref):
        table = ref[pl.ds(NY, 16), :].astype(jnp.int32).astype(jnp.float32)
        parts = [
            decode(ref[pl.ds(h * 128, 128), :], table[0:1, h * 128 : (h + 1) * 128])
            for h in range(2)
        ]
        return jnp.concatenate(parts, axis=0)

    row = lax.broadcasted_iota(jnp.int32, (NY, NX), 0)
    col = lax.broadcasted_iota(jnp.int32, (NY, NX), 1)

    def step(below, mid, above):
        near = jnp.where(row == 0, 0.0, pltpu.roll(mid, 1, 0))
        near += jnp.where(row == NY - 1, 0.0, pltpu.roll(mid, NY - 1, 0))
        near += jnp.where(col == 0, 0.0, pltpu.roll(mid, 1, 1))
        near += jnp.where(col == NX - 1, 0.0, pltpu.roll(mid, NX - 1, 1))
        return mid + 0.15 * (near + below + above - 6.0 * mid)

    plane = plane_ref[...]
    left, right = halo(l1), halo(r1)
    lower = step(halo(l2), left, plane)
    upper = step(plane, right, halo(r2))
    lower = jnp.where(edge_ref[0] > 0, lower, 0.0)
    upper = jnp.where(edge_ref[1] > 0, upper, 0.0)
    field = step(lower, step(left, plane, right), upper).astype(jnp.bfloat16)
    out_ref[...] = field

    readers, most = reads_ref.shape
    lane = lax.broadcasted_iota(jnp.int32, (1, most), 1)
    columns = lax.broadcasted_iota(jnp.int32, (most, NY), 1).astype(jnp.float32)
    for t in range(readers):
        ids = jnp.where(lane < counts_ref[t], reads_ref[pl.ds(t, 1), :], -1)
        hot = jnp.where(columns == to_column(ids.astype(jnp.float32)), 1.0, 0.0)
        lines = jnp.dot(hot.astype(jnp.bfloat16), field, preferred_element_type=jnp.float32)
        back_ref[t] = lines.astype(jnp.bfloat16)


def smooth(edges, counts, plane, halos, reads):
    vmem = pl.BlockSpec(memory_space=pltpu.VMEM)
    smem = pl.BlockSpec(memory_space=pltpu.SMEM)
    readers, most = reads.shape
    return pl.pallas_call(
        smooth_kernel,
        in_specs=[smem, smem] + [vmem] * 6,
        out_specs=[vmem, vmem],
        out_shape=[
            jax.ShapeDtypeStruct((NY, NX), jnp.bfloat16),
            jax.ShapeDtypeStruct((readers, most, NX), jnp.bfloat16),
        ],
        compiler_params=pltpu.CompilerParams(vmem_limit_bytes=12 * 1024 * 1024),
        name="smooth",
    )(edges, counts, plane, *halos, reads)


def after_kernel(x_ref, *refs):
    del x_ref, refs


def after(x, others):
    anywhere = pl.BlockSpec(memory_space=pl.ANY)
    return pl.pallas_call(
        after_kernel,
        in_specs=[anywhere] + [pl.BlockSpec(memory_space=pltpu.VMEM)] * len(others),
        out_specs=anywhere,
        out_shape=hbm(x.shape, x.dtype),
        input_output_aliases={0: 0},
        name="after",
    )(x, *others)


def local(acquired, stencil, send_slots, send_lines, send_counts, return_slots, return_counts):
    tile_count = lax.axis_size("tile")
    cut_count = lax.axis_size("cuts")
    first_tiles = tile_count * SPLIT // 16
    tile_half = tile_count // 2
    here = lax.axis_index("cuts")
    here_x = here // 2
    here_core = here % 2
    place = jnp.stack([here_core, here_x]).astype(jnp.int32)
    counts = send_counts[0]
    flat_slots = send_slots.reshape(-1)
    swap = [(i, i ^ 1) for i in range(cut_count)]

    rows, peer_rows = [], []
    for h in range(2):
        source = wide if h else acquired
        made = gather_rows(source, flat_slots, counts, send_lines[0], h * tile_half, tile_half)
        if not h:
            made, wide = made
        rows.append(made)
        peer_rows.append(lax.ppermute(rows[h], "cuts", swap))
    cap = send_slots.shape[2]
    peer_counts = [
        (part[:, cap + 7, 0].astype(jnp.float32) * 64 + part[:, cap + 15, 0].astype(jnp.float32))
        .astype(jnp.int32)
        for part in peer_rows
    ]
    peer_counts[1] = jnp.concatenate(peer_counts)

    def x_send(block, k):
        return lax.ppermute(block, "cuts", [(i, (i + 2 * k) % cut_count) for i in range(cut_count)])

    b_blocks = None
    a_parts = []
    for first, last in ((0, first_tiles), (first_tiles, tile_count)):
        used = 2 if first else 1
        *a_blocks, b_blocks = line_blocks(
            rows[:used], peer_rows[:used], counts, peer_counts[used - 1], place,
            b_blocks, first, last - first, tile_count,
        )
        a_parts.append([a_blocks[0]] + [x_send(a_blocks[k], k) for k in (1, 2, 3)])
    a_sums, token = sum_x(
        a_parts[0], jnp.zeros((16, NX), jnp.int16), in_hbm(a_parts[1][0]), 0, tile_count
    )
    b_blocks = after(b_blocks, [token])
    b_arrived = lax.all_to_all(b_blocks, "tile", split_axis=0, concat_axis=0, tiled=True)
    a_sums, _ = sum_x(a_parts[1], a_sums, in_hbm(a_parts[1][0]), first_tiles, tile_count)
    a_arrived = lax.all_to_all(a_sums, "tile", split_axis=0, concat_axis=0, tiled=True)
    b_sums = sum_tile(b_arrived)
    b_final = [b_sums[0]] + [x_send(b_sums[k], k) for k in (1, 2, 3)]
    plane, coded = own_plane(a_arrived, b_final, stencil)

    total = cut_count * tile_count

    def plane_send(k):
        pairs = [(i, i + k) for i in range(total) if 0 <= i + k < total]
        return lax.ppermute(coded, ("cuts", "tile"), pairs)

    halos = [plane_send(1), plane_send(2), plane_send(-1), plane_send(-2)]
    spot = here * tile_count + lax.axis_index("tile")
    edges = jnp.stack([spot > 0, spot < total - 1]).astype(jnp.int32)
    field, outgoing = smooth(edges, return_counts[0], plane, halos, return_slots[0])
    returned = lax.all_to_all(outgoing, "tile", split_axis=0, concat_axis=0, tiled=True)
    return field[None], pltpu.with_memory_space_constraint(returned, pltpu.HBM)


def solution(mesh):
    in_specs = (
        P(("cuts", "tile"), None),
        P("tile", None),
        P(("cuts", "tile"), None, None),
        P(("cuts", "tile"), None, None),
        P(("cuts", "tile"), None),
        P(("cuts", "tile"), None, None),
        P(("cuts", "tile"), None),
    )
    out_specs = (P(("cuts", "tile"), None, None), P(("cuts", "tile"), None, None))
    return jax.shard_map(local, mesh=mesh, in_specs=in_specs, out_specs=out_specs, check_vma=False)
```

```python
import functools
import math

import jax
import jax.numpy as jnp
from jax import lax
from jax.experimental import pallas as pl
from jax.experimental.pallas import tpu as pltpu
from jax.sharding import PartitionSpec as P

NX = 256
NY = 256
TAPS = 4
LA = 160
LB = NY - LA
ALPHA = math.log(2.0) / 64.0
TOP = 32700.0
CHUNK = 256
PICK = 32
PAD = 8


def params(mib):
    return pltpu.CompilerParams(
        vmem_limit_bytes=mib * 1024 * 1024, dimension_semantics=("arbitrary",)
    )


def hbm(shape, dtype):
    return pltpu.HBM(shape, dtype)


def in_hbm(x):
    return pltpu.with_memory_space_constraint(x, pltpu.HBM)


def encode(block):
    top = to_row(jnp.max(jnp.abs(block), axis=1, keepdims=True))
    code = jnp.ceil(jnp.log(jnp.maximum(top, 1e-33)) * (1.0 / ALPHA))
    factor = to_column(TOP / jnp.exp(code * ALPHA))
    values = (block * factor + 12582912.0) - 12582912.0
    return values.astype(jnp.int32).astype(jnp.int16), code


def eye(size):
    return lax.broadcasted_iota(jnp.int32, (size, size), 0) == lax.broadcasted_iota(
        jnp.int32, (size, size), 1
    )


def to_row(column):
    return jnp.sum(jnp.where(eye(column.shape[0]), column, 0.0), axis=0, keepdims=True)


def to_column(row):
    return jnp.sum(jnp.where(eye(row.shape[1]), row, 0.0), axis=1, keepdims=True)


def decode(values, code_row):
    scale = jnp.exp(code_row * ALPHA) * (1.0 / TOP)
    return values.astype(jnp.int32).astype(jnp.float32) * to_column(scale)


def code_block(rows):
    block = jnp.zeros((PAD, NX), jnp.float32)
    index = lax.broadcasted_iota(jnp.int32, (PAD, NX), 0)
    for i, row in enumerate(rows):
        block = jnp.where(index == i, row, block)
    return block.astype(jnp.int32).astype(jnp.int16)


def widen_kernel(acq_ref, wide_ref, half_ref, sem):
    pieces = sem.shape[0]
    piece = half_ref.shape[0] // pieces
    copies = []
    for k in range(pieces):
        span = pl.ds(k * piece, piece)
        copies.append(pltpu.make_async_copy(acq_ref.at[span, :], half_ref.at[span, :], sem.at[k]))
        copies[k].start()
    for k in range(pieces):
        copies[k].wait()

        def widen(i, carry):
            span = pl.ds(pl.multiple_of(k * piece + i * CHUNK, CHUNK), CHUNK)
            x = half_ref[span, :].astype(jnp.float32)
            for g in range(CHUNK // 8):
                for c in range(2):
                    place = pl.multiple_of((k * piece + i * CHUNK) * 2 + (2 * g + c) * 8, 8)
                    wide_ref[pl.ds(place, 8), :] = x[g * 8 : g * 8 + 8, c * 128 : c * 128 + 128]
            return carry

        lax.fori_loop(0, piece // CHUNK, widen, 0)


def first_gather_kernel(
    counts_ref, acq_ref, lines_hbm, slots_hbm, out_ref, wide_ref, lines_ref, half_ref, sem, line_sem,
    slots_ref, slot_sem, **sizes,
):
    fetch = pltpu.make_async_copy(lines_hbm, lines_ref, line_sem)

    @pl.when(pl.program_id(0) == 0)
    def _():
        fetch.start()
        slots_of(slots_hbm, slots_ref, slot_sem, 0, **sizes).start()
        widen_kernel(acq_ref, wide_ref, half_ref, sem)
        fetch.wait()

    gather_tile(slots_hbm, slots_ref, slot_sem, counts_ref, lines_ref, out_ref, wide_ref, **sizes)


def next_gather_kernel(
    counts_ref, wide_ref, lines_hbm, slots_hbm, out_ref, lines_ref, line_sem, slots_ref, slot_sem,
    **sizes,
):
    fetch = pltpu.make_async_copy(lines_hbm, lines_ref, line_sem)

    @pl.when(pl.program_id(0) == 0)
    def _():
        fetch.start()
        slots_of(slots_hbm, slots_ref, slot_sem, 0, **sizes).start()
        fetch.wait()

    gather_tile(slots_hbm, slots_ref, slot_sem, counts_ref, lines_ref, out_ref, wide_ref, **sizes)


def slots_of(slots_hbm, slots_ref, slot_sem, tile, *, first, cap):
    side = lax.rem(tile, 2)
    return pltpu.make_async_copy(
        slots_hbm.at[first + tile], slots_ref.at[pl.ds(side * cap, cap)], slot_sem.at[side]
    )


def gather_tile(
    slots_hbm, slots_ref, slot_sem, counts_ref, lines_ref, out_ref, wide_ref, *, first, cap
):
    step = pl.program_id(0)

    @pl.when(step + 1 < pl.num_programs(0))
    def _():
        slots_of(slots_hbm, slots_ref, slot_sem, step + 1, first=first, cap=cap).start()

    slots_of(slots_hbm, slots_ref, slot_sem, step, first=first, cap=cap).wait()
    count = counts_ref[first + step]
    start = lax.rem(step, 2) * cap

    def pick(i, carry):
        base = pl.multiple_of(i * PICK, PICK)
        places = [slots_ref[start + base + u] for u in range(PICK)]
        for c in range(2):
            rows = [wide_ref[pl.ds(place + 8 * c, 1), :] for place in places]
            rows = jnp.concatenate(rows, axis=0).astype(jnp.bfloat16)
            out_ref[0, pl.ds(base, PICK), c * 128 : c * 128 + 128] = rows
        return carry

    def clear(i, carry):
        base = pl.multiple_of(i * PICK, PICK)
        out_ref[0, pl.ds(base, PICK), :] = jnp.zeros((PICK, NX), jnp.bfloat16)
        return carry

    picks = (count + PICK - 1) // PICK
    lax.fori_loop(0, picks, pick, 0)
    lax.fori_loop(picks, (count + CHUNK - 1) // CHUNK * (CHUNK // PICK), clear, 0)

    ids = lines_ref[pl.ds(first + step, 1), :]
    position = lax.broadcasted_iota(jnp.int32, ids.shape, 1)
    ids = jnp.where(position < count, ids + 1, 0)
    index = lax.broadcasted_iota(jnp.int32, (8, NX), 0)
    table = jnp.where(index == 7, count, 0)
    for i in range(cap // CHUNK):
        table = jnp.where(index == i, ids[:, i * CHUNK : (i + 1) * CHUNK], table)
    both = jnp.concatenate([table >> 6, table & 63], axis=0)
    out_ref[0, pl.ds(cap, 16), :] = both.astype(jnp.float32).astype(jnp.bfloat16)


def gather_rows(source, slots, counts, lines, first, tiles):
    cap = lines.shape[1]
    rows_spec = pl.BlockSpec((1, cap + 16, NX), lambda t, c: (t, 0, 0))
    rows_shape = hbm((tiles, cap + 16, NX), jnp.bfloat16)
    line_scratch = [pltpu.VMEM(lines.shape, jnp.int32)]
    line_sem = [pltpu.SemaphoreType.DMA]
    whole = pl.BlockSpec(memory_space=pltpu.VMEM)
    if first:
        body = next_gather_kernel
        source = pltpu.with_memory_space_constraint(source, pltpu.VMEM)
        source_spec = whole
        out_specs, out_shape = rows_spec, rows_shape
        scratch = line_scratch + line_sem
    else:
        body = first_gather_kernel
        source = pltpu.with_memory_space_constraint(source, pltpu.HBM)
        source_spec = pl.BlockSpec(memory_space=pltpu.HBM)
        out_specs = [rows_spec, whole]
        out_shape = [rows_shape, pltpu.VMEM((source.shape[0] * 2, 128), jnp.float32)]
        scratch = (
            line_scratch
            + [pltpu.VMEM(source.shape, jnp.bfloat16), pltpu.SemaphoreType.DMA((8,))]
            + line_sem
        )
    return pl.pallas_call(
        functools.partial(body, first=first, cap=cap),
        grid_spec=pltpu.PrefetchScalarGridSpec(
            num_scalar_prefetch=1,
            grid=(tiles,),
            in_specs=[source_spec] + [pl.BlockSpec(memory_space=pltpu.HBM)] * 2,
            out_specs=out_specs,
            scratch_shapes=scratch
            + [pltpu.SMEM((2 * cap,), jnp.int32), pltpu.SemaphoreType.DMA((2,))],
        ),
        out_shape=out_shape,
        compiler_params=params(14),
        cost_estimate=pl.CostEstimate(flops=0, transcendentals=0, bytes_accessed=40_000_000),
        name="gather_rows",
    )(counts, source, in_hbm(lines), in_hbm(slots))


def lines_kernel(
    own_n, peer_n, place_ref, own_hbm, peer_hbm, alias_ref,
    a0_ref, a1_ref, a2_ref, a3_ref, b_ref,
    acc_ref, code_ref, rows_ref, ids_ref, sem, *, first, cap,
):
    step = pl.program_id(0)
    last = pl.num_programs(0) - 1
    most = cap // CHUNK

    def chunks(tile):
        return (own_n[first + tile] + CHUNK - 1) // CHUNK, (peer_n[tile] + CHUNK - 1) // CHUNK

    def for_copies(tile, act):
        slot = lax.rem(tile, 2)
        own, peer = chunks(tile)
        for j, (source, base, count) in enumerate(((own_hbm, 0, own), (peer_hbm, own, peer))):
            for i in range(most):
                copy = pltpu.make_async_copy(
                    source.at[tile, pl.ds(i * CHUNK, CHUNK), :],
                    rows_ref.at[slot, pl.ds(pl.multiple_of((base + i) * CHUNK, CHUNK), CHUNK), :],
                    sem.at[slot, j * (most + 1) + i],
                )

                @pl.when(i < count)
                def _():
                    act(copy)

            act(
                pltpu.make_async_copy(
                    source.at[tile, pl.ds(cap, 16), :],
                    ids_ref.at[slot, j],
                    sem.at[slot, j * (most + 1) + most],
                )
            )

    @pl.when(step == 0)
    def _():
        for_copies(0, lambda copy: copy.start())

    @pl.when(step < last)
    def _():
        for_copies(step + 1, lambda copy: copy.start())

    for_copies(step, lambda copy: copy.wait())

    slot = lax.rem(step, 2)
    own, peer = chunks(step)
    here_core, here_x = place_ref[0], place_ref[1]
    for j in range(2):
        pair = ids_ref[slot, j].astype(jnp.float32).astype(jnp.int32)
        line = pair[0:8] * 64 + pair[8:16] - 1
        cut = line >> 8
        y = line & (NY - 1)
        mine = (line >= 0) & ((cut & 1) == here_core)
        ahead = ((cut >> 1) - here_x) & 3
        target = jnp.where(y < LA, ahead * LA + y, 4 * LA + ahead * LB + y - LA)
        target = jnp.where(mine, target, -1)
        for i in range(most):
            spot = i if j == 0 else own + i
            code_ref[4, pl.ds(spot, 1), :] = target[i : i + 1].astype(jnp.float32)

    acc_ref[...] = jnp.zeros(acc_ref.shape, jnp.float32)
    position = lax.broadcasted_iota(jnp.int32, (CHUNK, CHUNK), 0).astype(jnp.float32)

    def add(start, width):
        rows = rows_ref[slot, pl.ds(pl.multiple_of(start * CHUNK, CHUNK), width * CHUNK), :]
        ids = [code_ref[4, pl.ds(start + i, 1), :] for i in range(width)]
        for m in range(acc_ref.shape[0] // CHUNK):
            hot = [
                jnp.where(position == row - m * CHUNK, 1.0, 0.0).astype(jnp.bfloat16) for row in ids
            ]
            hot = jnp.concatenate(hot, axis=1) if width > 1 else hot[0]
            span = pl.ds(m * CHUNK, CHUNK)
            acc_ref[span, :] += jnp.dot(hot, rows, preferred_element_type=jnp.float32)

    total = own + peer

    def four(i, carry):
        add(i * 4, 4)
        return carry

    lax.fori_loop(0, total // 4, four, 0)
    for width in (1, 2, 3):

        @pl.when(total % 4 == width)
        def _():
            add(total // 4 * 4, width)

    outs = (a0_ref, a1_ref, a2_ref, a3_ref)
    for k in range(4):
        values, code = encode(acc_ref[pl.ds(k * LA, LA), :])
        outs[k][pl.ds(pl.multiple_of(step * LA, LA), LA), :] = values
        code_ref[k, pl.ds(step, 1), :] = pad_row(code)

    codes = []
    for k in range(4):
        values, code = encode(acc_ref[pl.ds(4 * LA + k * LB, LB), :])
        b_ref[0, pl.ds(k * LB, LB), :] = values
        codes.append(pad_row(code))
    b_ref[0, pl.ds(4 * LB, PAD), :] = code_block(codes)

    @pl.when(step == last)
    def _():
        for k in range(4):
            outs[k][pl.ds((last + 1) * LA, PAD), :] = code_ref[k, 0:PAD].astype(jnp.int32).astype(jnp.int16)


def pad_row(row):
    return jnp.concatenate([row, jnp.zeros((1, NX - row.shape[1]), jnp.float32)], axis=1)


def line_blocks(own_rows, peer_rows, own_n, peer_n, place, b_old, first, tiles_all):
    tiles, cap, _ = own_rows.shape
    cap -= 16
    a_shape = (tiles * LA + PAD, NX)
    own_rows = pltpu.with_memory_space_constraint(own_rows, pltpu.HBM)
    peer_rows = pltpu.with_memory_space_constraint(peer_rows, pltpu.HBM)
    args = [own_n, peer_n, place, own_rows, peer_rows]
    aliases = {}
    if b_old is None:
        b_old = jnp.zeros((16, NX), jnp.int16)
    else:
        aliases = {5: 4}
    args.append(b_old)
    return pl.pallas_call(
        functools.partial(lines_kernel, first=first, cap=cap),
        grid_spec=pltpu.PrefetchScalarGridSpec(
            num_scalar_prefetch=3,
            grid=(tiles,),
            in_specs=[pl.BlockSpec(memory_space=pltpu.HBM)] * 2
            + [pl.BlockSpec(memory_space=pl.ANY)],
            out_specs=[pl.BlockSpec(a_shape, lambda t, *_: (0, 0))] * 4
            + [pl.BlockSpec((1, 4 * LB + PAD, NX), lambda t, *_: (t + first, 0, 0))],
            scratch_shapes=[
                pltpu.VMEM((4 * NY, NX), jnp.float32),
                pltpu.VMEM((5, 16, NX), jnp.float32),
                pltpu.VMEM((2, 2 * cap, NX), jnp.bfloat16),
                pltpu.VMEM((2, 2, 16, NX), jnp.bfloat16),
                pltpu.SemaphoreType.DMA((2, 2 * (cap // CHUNK + 1))),
            ],
        ),
        out_shape=[hbm(a_shape, jnp.int16)] * 4
        + [hbm((tiles_all, 4 * LB + PAD, NX), jnp.int16)],
        input_output_aliases=aliases,
        compiler_params=params(16),
        cost_estimate=pl.CostEstimate(
            flops=2 * 1024 * 256 * 20480, transcendentals=0, bytes_accessed=40_000_000
        ),
        name="line_blocks",
    )(*args)


def code_row(block, index, length):
    table = block.astype(jnp.int32).astype(jnp.float32)
    rows = lax.broadcasted_iota(jnp.int32, table.shape, 0)
    row = jnp.sum(jnp.where(rows == index, table, 0.0), axis=0, keepdims=True)
    return row[:, 0:length]


def sum_x_kernel(p0, p1, p2, p3, alias_ref, out_ref, sum_ref, sem, *, first):
    tiles = sum_ref.shape[0]

    def copy_out(i):
        return pltpu.make_async_copy(sum_ref.at[i], out_ref.at[first + i], sem.at[i])

    for i in range(tiles):
        total = jnp.zeros((LA, NX), jnp.float32)
        for part in (p0, p1, p2, p3):
            codes = code_row(part[pl.ds(tiles * LA, PAD), :], i, LA)
            total = total + decode(part[pl.ds(i * LA, LA), :], codes)
        values, code = encode(total)
        sum_ref[i, pl.ds(0, LA), :] = values
        sum_ref[i, pl.ds(LA, PAD), :] = code_block([pad_row(code)])
        copy_out(i).start()
    for i in range(tiles):
        copy_out(i).wait()


def sum_x(parts, old, first, tiles_all):
    tiles = (parts[0].shape[0] - PAD) // LA
    aliases = {}
    if old is None:
        old = jnp.zeros((16, NX), jnp.int16)
    else:
        aliases = {4: 0}
    return pl.pallas_call(
        functools.partial(sum_x_kernel, first=first),
        in_specs=[pl.BlockSpec(memory_space=pltpu.VMEM)] * 4 + [pl.BlockSpec(memory_space=pl.ANY)],
        out_specs=pl.BlockSpec(memory_space=pltpu.HBM),
        out_shape=hbm((tiles_all, LA + PAD, NX), jnp.int16),
        scratch_shapes=[
            pltpu.VMEM((tiles, LA + PAD, NX), jnp.int16),
            pltpu.SemaphoreType.DMA((tiles,)),
        ],
        input_output_aliases=aliases,
        compiler_params=pltpu.CompilerParams(vmem_limit_bytes=12 * 1024 * 1024),
        name="sum_x",
    )(*parts, old)


def sum_tile_kernel(in_hbm_ref, o0, o1, o2, o3, acc_ref, in_ref, sem):
    tiles = in_ref.shape[0]

    def fetch(t):
        return pltpu.make_async_copy(in_hbm_ref.at[t], in_ref.at[t], sem.at[t])

    for t in range(tiles):
        fetch(t).start()
    acc_ref[...] = jnp.zeros(acc_ref.shape, jnp.float32)

    def body(t, carry):
        fetch(t).wait()
        table = in_ref[t, pl.ds(4 * LB, PAD), :].astype(jnp.int32).astype(jnp.float32)
        for k in range(4):
            acc_ref[pl.ds(k * LB, LB), :] += decode(
                in_ref[t, pl.ds(k * LB, LB), :], table[k : k + 1, 0:LB]
            )
        return carry

    lax.fori_loop(0, tiles, body, 0)
    for k, out in enumerate((o0, o1, o2, o3)):
        values, code = encode(acc_ref[pl.ds(k * LB, LB), :])
        out[pl.ds(0, LB), :] = values
        out[pl.ds(LB, PAD), :] = code_block([pad_row(code)])


def sum_tile(arrived):
    out_shape = (LB + PAD, NX)
    return pl.pallas_call(
        sum_tile_kernel,
        in_specs=[pl.BlockSpec(memory_space=pltpu.HBM)],
        out_shape=[jax.ShapeDtypeStruct(out_shape, jnp.int16)] * 4,
        scratch_shapes=[
            pltpu.VMEM((4 * LB, NX), jnp.float32),
            pltpu.VMEM(arrived.shape, jnp.int16),
            pltpu.SemaphoreType.DMA(arrived.shape[:1]),
        ],
        compiler_params=pltpu.CompilerParams(vmem_limit_bytes=12 * 1024 * 1024),
        name="sum_tile",
    )(in_hbm(arrived))


def plane_kernel(a_ref, b0, b1, b2, b3, stencil_ref, plane_ref, send_ref, lines_ref):
    def body(i, carry):
        codes = code_row(a_ref[i, pl.ds(LA, PAD), :], 0, LA)
        lines_ref[pl.ds(0, LA), :] += decode(a_ref[i, pl.ds(0, LA), :], codes)
        return carry

    lines_ref[pl.ds(0, LA), :] = jnp.zeros((LA, NX), jnp.float32)
    lax.fori_loop(0, a_ref.shape[0], body, 0)
    total = jnp.zeros((LB, NX), jnp.float32)
    for b in (b0, b1, b2, b3):
        total = total + decode(b[pl.ds(0, LB), :], code_row(b[pl.ds(LB, PAD), :], 0, LB))
    lines_ref[pl.ds(LA, LB), :] = total

    lines = lines_ref[...]
    high = lines.astype(jnp.bfloat16)
    rest = lines - high.astype(jnp.float32)
    mid = rest.astype(jnp.bfloat16)
    low = (rest - mid.astype(jnp.float32)).astype(jnp.bfloat16)
    plane = jnp.zeros((NY, NX), jnp.float32)
    for k in range(TAPS):
        weights = stencil_ref[:, k * NX : (k + 1) * NX]
        product = jnp.dot(high, weights, preferred_element_type=jnp.float32)
        product += jnp.dot(mid, weights, preferred_element_type=jnp.float32)
        product += jnp.dot(low, weights, preferred_element_type=jnp.float32)
        if k:
            product = pltpu.roll(product, k, 0)
        plane = plane + product
    plane_ref[...] = plane
    rows = []
    for h in range(2):
        values, code = encode(plane[h * 128 : (h + 1) * 128])
        send_ref[pl.ds(h * 128, 128), :] = values
        rows.append(code)
    send_ref[pl.ds(NY, PAD), :] = code_block([jnp.concatenate(rows, axis=1)])


def own_plane(a, bs, stencil):
    return pl.pallas_call(
        plane_kernel,
        out_shape=[
            jax.ShapeDtypeStruct((NY, NX), jnp.float32),
            jax.ShapeDtypeStruct((NY + PAD, NX), jnp.int16),
        ],
        scratch_shapes=[pltpu.VMEM((NY, NX), jnp.float32)],
        compiler_params=pltpu.CompilerParams(vmem_limit_bytes=12 * 1024 * 1024),
        name="own_plane",
    )(a, *bs, stencil)


def smooth_kernel(edge_ref, counts_ref, plane_ref, l1, l2, r1, r2, reads_ref, out_ref, back_ref):
    def halo(ref):
        table = ref[pl.ds(NY, PAD), :].astype(jnp.int32).astype(jnp.float32)
        parts = [
            decode(ref[pl.ds(h * 128, 128), :], table[0:1, h * 128 : (h + 1) * 128])
            for h in range(2)
        ]
        return jnp.concatenate(parts, axis=0)

    row = lax.broadcasted_iota(jnp.int32, (NY, NX), 0)
    col = lax.broadcasted_iota(jnp.int32, (NY, NX), 1)

    def step(below, mid, above):
        near = jnp.where(row == 0, 0.0, pltpu.roll(mid, 1, 0))
        near += jnp.where(row == NY - 1, 0.0, pltpu.roll(mid, NY - 1, 0))
        near += jnp.where(col == 0, 0.0, pltpu.roll(mid, 1, 1))
        near += jnp.where(col == NX - 1, 0.0, pltpu.roll(mid, NX - 1, 1))
        return mid + 0.15 * (near + below + above - 6.0 * mid)

    plane = plane_ref[...]
    left, right = halo(l1), halo(r1)
    lower = step(halo(l2), left, plane)
    upper = step(plane, right, halo(r2))
    lower = jnp.where(edge_ref[0] > 0, lower, 0.0)
    upper = jnp.where(edge_ref[1] > 0, upper, 0.0)
    field = step(lower, step(left, plane, right), upper).astype(jnp.bfloat16)
    out_ref[...] = field

    readers, most = reads_ref.shape
    lane = lax.broadcasted_iota(jnp.int32, (1, most), 1)
    columns = lax.broadcasted_iota(jnp.int32, (most, NY), 1).astype(jnp.float32)
    for t in range(readers):
        ids = jnp.where(lane < counts_ref[t], reads_ref[pl.ds(t, 1), :], -1)
        hot = jnp.where(columns == to_column(ids.astype(jnp.float32)), 1.0, 0.0)
        lines = jnp.dot(hot.astype(jnp.bfloat16), field, preferred_element_type=jnp.float32)
        back_ref[t] = lines.astype(jnp.bfloat16)


def smooth(edges, counts, plane, halos, reads):
    vmem = pl.BlockSpec(memory_space=pltpu.VMEM)
    smem = pl.BlockSpec(memory_space=pltpu.SMEM)
    readers, most = reads.shape
    return pl.pallas_call(
        smooth_kernel,
        in_specs=[smem, smem] + [vmem] * 6,
        out_specs=[vmem, vmem],
        out_shape=[
            jax.ShapeDtypeStruct((NY, NX), jnp.bfloat16),
            jax.ShapeDtypeStruct((readers, most, NX), jnp.bfloat16),
        ],
        compiler_params=pltpu.CompilerParams(vmem_limit_bytes=12 * 1024 * 1024),
        name="smooth",
    )(edges, counts, plane, *halos, reads)


def after_kernel(x_ref, *refs):
    del x_ref, refs


def after(x, others):
    anywhere = pl.BlockSpec(memory_space=pl.ANY)
    return pl.pallas_call(
        after_kernel,
        in_specs=[anywhere] * (1 + len(others)),
        out_specs=anywhere,
        out_shape=hbm(x.shape, x.dtype),
        input_output_aliases={0: 0},
        name="after",
    )(x, *others)


def local(acquired, stencil, send_slots, send_lines, send_counts, return_slots, return_counts):
    tile_count = lax.axis_size("tile")
    cut_count = lax.axis_size("cuts")
    tile_half = tile_count // 2
    here = lax.axis_index("cuts")
    here_x = here // 2
    here_core = here % 2
    place = jnp.stack([here_core, here_x]).astype(jnp.int32)
    counts = send_counts[0]
    swap = [(i, i ^ 1) for i in range(cut_count)]

    places = send_slots[0] + (send_slots[0] & ~7)
    rows, peer_rows = [], []
    for h in range(2):
        source = wide if h else acquired
        made = gather_rows(source, places, counts, send_lines[0], h * tile_half, tile_half)
        if not h:
            made, wide = made
        rows.append(made)
        peer_rows.append(lax.ppermute(rows[h], "cuts", swap))
    cap = send_slots.shape[2]
    peer_counts = [
        (part[:, cap + 7, 0].astype(jnp.float32) * 64 + part[:, cap + 15, 0].astype(jnp.float32))
        .astype(jnp.int32)
        for part in peer_rows
    ]

    def x_send(block, k):
        return lax.ppermute(block, "cuts", [(i, (i + 2 * k) % cut_count) for i in range(cut_count)])

    b_blocks = None
    a_parts = []
    for h in range(2):
        *a_blocks, b_blocks = line_blocks(
            rows[h], peer_rows[h], counts, peer_counts[h], place,
            b_blocks, h * tile_half, tile_count,
        )
        a_parts.append([a_blocks[0]] + [x_send(a_blocks[k], k) for k in (1, 2, 3)])
    near = [a_parts[0][1][:16] | a_parts[0][3][:16]]
    b_blocks = after(b_blocks, near)
    b_arrived = lax.all_to_all(b_blocks, "tile", split_axis=0, concat_axis=0, tiled=True)
    a_sums = None
    for h in range(2):
        a_sums = sum_x(a_parts[h], a_sums, h * tile_half, tile_count)
    a_arrived = lax.all_to_all(a_sums, "tile", split_axis=0, concat_axis=0, tiled=True)
    b_sums = sum_tile(b_arrived)
    b_final = [b_sums[0]] + [x_send(b_sums[k], k) for k in (1, 2, 3)]
    plane, coded = own_plane(a_arrived, b_final, stencil)

    total = cut_count * tile_count

    def plane_send(k):
        pairs = [(i, i + k) for i in range(total) if 0 <= i + k < total]
        return lax.ppermute(coded, ("cuts", "tile"), pairs)

    halos = [plane_send(1), plane_send(2), plane_send(-1), plane_send(-2)]
    spot = here * tile_count + lax.axis_index("tile")
    edges = jnp.stack([spot > 0, spot < total - 1]).astype(jnp.int32)
    field, outgoing = smooth(edges, return_counts[0], plane, halos, return_slots[0])
    returned = lax.all_to_all(outgoing, "tile", split_axis=0, concat_axis=0, tiled=True)
    return field[None], pltpu.with_memory_space_constraint(returned, pltpu.HBM)


def solution(mesh):
    in_specs = (
        P(("cuts", "tile"), None),
        P("tile", None),
        P(("cuts", "tile"), None, None),
        P(("cuts", "tile"), None, None),
        P(("cuts", "tile"), None),
        P(("cuts", "tile"), None, None),
        P(("cuts", "tile"), None),
    )
    out_specs = (P(("cuts", "tile"), None, None), P(("cuts", "tile"), None, None))
    return jax.shard_map(local, mesh=mesh, in_specs=in_specs, out_specs=out_specs, check_vma=False)
```

```python
import functools
import math

import jax
import jax.numpy as jnp
from jax import lax
from jax.experimental import pallas as pl
from jax.experimental.pallas import tpu as pltpu
from jax.sharding import PartitionSpec as P

NX = 256
NY = 256
TAPS = 4
LA = 160
LB = NY - LA
ALPHA = math.log(2.0) / 64.0
TOP = 32700.0
CHUNK = 256
PICK = 64
PAD = 8


def params(mib):
    return pltpu.CompilerParams(
        vmem_limit_bytes=mib * 1024 * 1024, dimension_semantics=("arbitrary",)
    )


def hbm(shape, dtype):
    return pltpu.HBM(shape, dtype)


def in_hbm(x):
    return pltpu.with_memory_space_constraint(x, pltpu.HBM)


def encode(block):
    top = to_row(jnp.max(jnp.abs(block), axis=1, keepdims=True))
    code = jnp.ceil(jnp.log(jnp.maximum(top, 1e-33)) * (1.0 / ALPHA))
    factor = to_column(TOP / jnp.exp(code * ALPHA))
    values = (block * factor + 12582912.0) - 12582912.0
    return values.astype(jnp.int32).astype(jnp.int16), code


def eye(size):
    return lax.broadcasted_iota(jnp.int32, (size, size), 0) == lax.broadcasted_iota(
        jnp.int32, (size, size), 1
    )


def to_row(column):
    return jnp.sum(jnp.where(eye(column.shape[0]), column, 0.0), axis=0, keepdims=True)


def to_column(row):
    return jnp.sum(jnp.where(eye(row.shape[1]), row, 0.0), axis=1, keepdims=True)


def decode(values, code_row):
    scale = jnp.exp(code_row * ALPHA) * (1.0 / TOP)
    return values.astype(jnp.int32).astype(jnp.float32) * to_column(scale)


def code_block(rows):
    block = jnp.zeros((PAD, NX), jnp.float32)
    index = lax.broadcasted_iota(jnp.int32, (PAD, NX), 0)
    for i, row in enumerate(rows):
        block = jnp.where(index == i, row, block)
    return block.astype(jnp.int32).astype(jnp.int16)


def widen_kernel(acq_ref, wide_ref, half_ref, sem, meanwhile):
    pieces = sem.shape[0]
    piece = half_ref.shape[0] // pieces
    copies = []
    for k in range(pieces):
        span = pl.ds(k * piece, piece)
        copies.append(pltpu.make_async_copy(acq_ref.at[span, :], half_ref.at[span, :], sem.at[k]))
        copies[k].start()
    meanwhile()
    for k in range(pieces):
        copies[k].wait()

        def widen(i, carry):
            span = pl.ds(pl.multiple_of(k * piece + i * CHUNK, CHUNK), CHUNK)
            x = half_ref[span, :].astype(jnp.float32)
            for g in range(CHUNK // 8):
                for c in range(2):
                    place = pl.multiple_of((k * piece + i * CHUNK) * 2 + (2 * g + c) * 8, 8)
                    wide_ref[pl.ds(place, 8), :] = x[g * 8 : g * 8 + 8, c * 128 : c * 128 + 128]
            return carry

        lax.fori_loop(0, piece // CHUNK, widen, 0)


def first_gather_kernel(
    counts_ref, acq_ref, lines_hbm, slots_hbm, out_ref, wide_ref, places_ref,
    lines_ref, half_ref, sem, line_sem, slots_ref, slot_sem, **sizes,
):
    fetch = pltpu.make_async_copy(lines_hbm, lines_ref, line_sem)

    @pl.when(pl.program_id(0) == 0)
    def _():
        def slots_meanwhile():
            to_places(slots_hbm, places_ref, slot_sem)
            slots_of(places_ref, slots_ref, slot_sem, 0, **sizes).start()

        fetch.start()
        widen_kernel(acq_ref, wide_ref, half_ref, sem, slots_meanwhile)

    gather_tile(
        fetch, places_ref, slots_ref, slot_sem, counts_ref, lines_ref, out_ref, wide_ref, **sizes
    )


def next_gather_kernel(
    counts_ref, wide_ref, lines_hbm, places_ref, out_ref, lines_ref, line_sem, slots_ref, slot_sem,
    **sizes,
):
    fetch = pltpu.make_async_copy(lines_hbm, lines_ref, line_sem)

    @pl.when(pl.program_id(0) == 0)
    def _():
        fetch.start()
        slots_of(places_ref, slots_ref, slot_sem, 0, **sizes).start()

    gather_tile(
        fetch, places_ref, slots_ref, slot_sem, counts_ref, lines_ref, out_ref, wide_ref, **sizes
    )


def to_places(slots_hbm, places_ref, slot_sem):
    fetch = pltpu.make_async_copy(slots_hbm, places_ref, slot_sem.at[0])
    fetch.start()
    fetch.wait()
    slots = places_ref[...]
    places_ref[...] = slots + (slots & ~7)


def slots_of(places_ref, slots_ref, slot_sem, tile, *, first, cap):
    side = lax.rem(tile, 2)
    return pltpu.make_async_copy(
        places_ref.at[first + tile], slots_ref.at[pl.ds(side * cap, cap)], slot_sem.at[side]
    )


def gather_tile(
    fetch, places_ref, slots_ref, slot_sem, counts_ref, lines_ref, out_ref, wide_ref, *, first, cap
):
    step = pl.program_id(0)

    @pl.when(step + 1 < pl.num_programs(0))
    def _():
        slots_of(places_ref, slots_ref, slot_sem, step + 1, first=first, cap=cap).start()

    slots_of(places_ref, slots_ref, slot_sem, step, first=first, cap=cap).wait()
    count = counts_ref[first + step]
    start = lax.rem(step, 2) * cap

    def pick(i, carry):
        base = pl.multiple_of(i * PICK, PICK)
        places = [slots_ref[start + base + u] for u in range(PICK)]
        for c in range(2):
            rows = [wide_ref[pl.ds(place + 8 * c, 1), :] for place in places]
            rows = jnp.concatenate(rows, axis=0).astype(jnp.bfloat16)
            out_ref[0, pl.ds(base, PICK), c * 128 : c * 128 + 128] = rows
        return carry

    def clear(i, carry):
        base = pl.multiple_of(i * PICK, PICK)
        out_ref[0, pl.ds(base, PICK), :] = jnp.zeros((PICK, NX), jnp.bfloat16)
        return carry

    picks = (count + PICK - 1) // PICK
    lax.fori_loop(0, picks, pick, 0)
    lax.fori_loop(picks, (count + CHUNK - 1) // CHUNK * (CHUNK // PICK), clear, 0)

    @pl.when(step == 0)
    def _():
        fetch.wait()

    ids = lines_ref[pl.ds(first + step, 1), :]
    position = lax.broadcasted_iota(jnp.int32, ids.shape, 1)
    ids = jnp.where(position < count, ids + 1, 0)
    index = lax.broadcasted_iota(jnp.int32, (8, NX), 0)
    table = jnp.where(index == 7, count, 0)
    for i in range(cap // CHUNK):
        table = jnp.where(index == i, ids[:, i * CHUNK : (i + 1) * CHUNK], table)
    both = jnp.concatenate([table >> 6, table & 63], axis=0)
    out_ref[0, pl.ds(cap, 16), :] = both.astype(jnp.float32).astype(jnp.bfloat16)


def gather_rows(source, slots, counts, lines, first, tiles):
    cap = lines.shape[1]
    rows_spec = pl.BlockSpec((1, cap + 16, NX), lambda t, c: (t, 0, 0))
    rows_shape = hbm((tiles, cap + 16, NX), jnp.bfloat16)
    line_scratch = [pltpu.VMEM(lines.shape, jnp.int32)]
    line_sem = [pltpu.SemaphoreType.DMA]
    whole = pl.BlockSpec(memory_space=pltpu.VMEM)
    if first:
        body = next_gather_kernel
        source = pltpu.with_memory_space_constraint(source, pltpu.VMEM)
        slots = pltpu.with_memory_space_constraint(slots, pltpu.VMEM)
        source_spec, slots_spec = whole, whole
        out_specs, out_shape = rows_spec, rows_shape
        scratch = line_scratch + line_sem
    else:
        body = first_gather_kernel
        source = pltpu.with_memory_space_constraint(source, pltpu.HBM)
        slots = in_hbm(slots)
        source_spec = slots_spec = pl.BlockSpec(memory_space=pltpu.HBM)
        out_specs = [rows_spec, whole, whole]
        out_shape = [
            rows_shape,
            pltpu.VMEM((source.shape[0] * 2, 128), jnp.float32),
            pltpu.VMEM(slots.shape, jnp.int32),
        ]
        scratch = (
            line_scratch
            + [pltpu.VMEM(source.shape, jnp.bfloat16), pltpu.SemaphoreType.DMA((8,))]
            + line_sem
        )
    return pl.pallas_call(
        functools.partial(body, first=first, cap=cap),
        grid_spec=pltpu.PrefetchScalarGridSpec(
            num_scalar_prefetch=1,
            grid=(tiles,),
            in_specs=[source_spec, pl.BlockSpec(memory_space=pltpu.HBM), slots_spec],
            out_specs=out_specs,
            scratch_shapes=scratch
            + [
                pltpu.SMEM((2 * cap,), jnp.int32),
                pltpu.SemaphoreType.DMA((2,)),
            ],
        ),
        out_shape=out_shape,
        compiler_params=params(14),
        cost_estimate=pl.CostEstimate(flops=0, transcendentals=0, bytes_accessed=40_000_000),
        name="gather_rows",
    )(counts, source, in_hbm(lines), slots)


def lines_kernel(
    own_n, peer_n, place_ref, own_hbm, peer_hbm, alias_ref,
    a0_ref, a1_ref, a2_ref, a3_ref, b_ref,
    acc_ref, code_ref, rows_ref, ids_ref, sem, *, first, cap,
):
    step = pl.program_id(0)
    last = pl.num_programs(0) - 1
    most = cap // CHUNK

    def chunks(tile):
        return (own_n[first + tile] + CHUNK - 1) // CHUNK, (peer_n[tile] + CHUNK - 1) // CHUNK

    def for_copies(tile, act):
        slot = lax.rem(tile, 2)
        own, peer = chunks(tile)
        for j, (source, base, count) in enumerate(((own_hbm, 0, own), (peer_hbm, own, peer))):
            for i in range(most):
                copy = pltpu.make_async_copy(
                    source.at[tile, pl.ds(i * CHUNK, CHUNK), :],
                    rows_ref.at[slot, pl.ds(pl.multiple_of((base + i) * CHUNK, CHUNK), CHUNK), :],
                    sem.at[slot, j * (most + 1) + i],
                )

                @pl.when(i < count)
                def _():
                    act(copy)

            act(
                pltpu.make_async_copy(
                    source.at[tile, pl.ds(cap, 16), :],
                    ids_ref.at[slot, j],
                    sem.at[slot, j * (most + 1) + most],
                )
            )

    @pl.when(step == 0)
    def _():
        for_copies(0, lambda copy: copy.start())

    @pl.when(step < last)
    def _():
        for_copies(step + 1, lambda copy: copy.start())

    for_copies(step, lambda copy: copy.wait())

    slot = lax.rem(step, 2)
    own, peer = chunks(step)
    here_core, here_x = place_ref[0], place_ref[1]
    for j in range(2):
        pair = ids_ref[slot, j].astype(jnp.float32).astype(jnp.int32)
        line = pair[0:8] * 64 + pair[8:16] - 1
        cut = line >> 8
        y = line & (NY - 1)
        mine = (line >= 0) & ((cut & 1) == here_core)
        ahead = ((cut >> 1) - here_x) & 3
        target = jnp.where(y < LA, ahead * LA + y, 4 * LA + ahead * LB + y - LA)
        target = jnp.where(mine, target, -1)
        for i in range(most):
            spot = i if j == 0 else own + i
            code_ref[4, pl.ds(spot, 1), :] = target[i : i + 1].astype(jnp.float32)

    position = lax.broadcasted_iota(jnp.int32, (CHUNK, CHUNK), 0).astype(jnp.float32)

    def add(start, width, first_group=False):
        rows = rows_ref[slot, pl.ds(pl.multiple_of(start * CHUNK, CHUNK), width * CHUNK), :]
        ids = [code_ref[4, pl.ds(start + i, 1), :] for i in range(width)]
        for m in range(acc_ref.shape[0] // CHUNK):
            hot = [
                jnp.where(position == row - m * CHUNK, 1.0, 0.0).astype(jnp.bfloat16) for row in ids
            ]
            hot = jnp.concatenate(hot, axis=1) if width > 1 else hot[0]
            span = pl.ds(m * CHUNK, CHUNK)
            product = jnp.dot(hot, rows, preferred_element_type=jnp.float32)
            acc_ref[span, :] = product if first_group else acc_ref[span, :] + product

    total = own + peer
    head = lax.rem(total - 1, 4) + 1
    for width in (1, 2, 3, 4):

        @pl.when(head == width)
        def _():
            add(0, width, first_group=True)

    def four(i, carry):
        add(head + i * 4, 4)
        return carry

    lax.fori_loop(0, (total - head) // 4, four, 0)

    outs = (a0_ref, a1_ref, a2_ref, a3_ref)
    for k in range(4):
        values, code = encode(acc_ref[pl.ds(k * LA, LA), :])
        outs[k][pl.ds(pl.multiple_of(step * LA, LA), LA), :] = values
        code_ref[k, pl.ds(step, 1), :] = pad_row(code)

    codes = []
    for k in range(4):
        values, code = encode(acc_ref[pl.ds(4 * LA + k * LB, LB), :])
        b_ref[0, pl.ds(k * LB, LB), :] = values
        codes.append(pad_row(code))
    b_ref[0, pl.ds(4 * LB, PAD), :] = code_block(codes)

    @pl.when(step == last)
    def _():
        for k in range(4):
            outs[k][pl.ds((last + 1) * LA, PAD), :] = code_ref[k, 0:PAD].astype(jnp.int32).astype(jnp.int16)


def pad_row(row):
    return jnp.concatenate([row, jnp.zeros((1, NX - row.shape[1]), jnp.float32)], axis=1)


def line_blocks(own_rows, peer_rows, own_n, peer_n, place, b_old, first, tiles_all):
    tiles, cap, _ = own_rows.shape
    cap -= 16
    a_shape = (tiles * LA + PAD, NX)
    own_rows = pltpu.with_memory_space_constraint(own_rows, pltpu.HBM)
    peer_rows = pltpu.with_memory_space_constraint(peer_rows, pltpu.HBM)
    args = [own_n, peer_n, place, own_rows, peer_rows]
    aliases = {}
    if b_old is None:
        b_old = jnp.zeros((16, NX), jnp.int16)
    else:
        aliases = {5: 4}
    args.append(b_old)
    return pl.pallas_call(
        functools.partial(lines_kernel, first=first, cap=cap),
        grid_spec=pltpu.PrefetchScalarGridSpec(
            num_scalar_prefetch=3,
            grid=(tiles,),
            in_specs=[pl.BlockSpec(memory_space=pltpu.HBM)] * 2
            + [pl.BlockSpec(memory_space=pl.ANY)],
            out_specs=[pl.BlockSpec(a_shape, lambda t, *_: (0, 0))] * 4
            + [pl.BlockSpec((1, 4 * LB + PAD, NX), lambda t, *_: (t + first, 0, 0))],
            scratch_shapes=[
                pltpu.VMEM((4 * NY, NX), jnp.float32),
                pltpu.VMEM((5, 16, NX), jnp.float32),
                pltpu.VMEM((2, 2 * cap, NX), jnp.bfloat16),
                pltpu.VMEM((2, 2, 16, NX), jnp.bfloat16),
                pltpu.SemaphoreType.DMA((2, 2 * (cap // CHUNK + 1))),
            ],
        ),
        out_shape=[hbm(a_shape, jnp.int16)] * 4
        + [hbm((tiles_all, 4 * LB + PAD, NX), jnp.int16)],
        input_output_aliases=aliases,
        compiler_params=params(16),
        cost_estimate=pl.CostEstimate(
            flops=2 * 1024 * 256 * 20480, transcendentals=0, bytes_accessed=40_000_000
        ),
        name="line_blocks",
    )(*args)


def code_row(block, index, length):
    table = block.astype(jnp.int32).astype(jnp.float32)
    rows = lax.broadcasted_iota(jnp.int32, table.shape, 0)
    row = jnp.sum(jnp.where(rows == index, table, 0.0), axis=0, keepdims=True)
    return row[:, 0:length]


def sum_x_kernel(p0, p1, p2, p3, alias_ref, out_ref, sum_ref, sem, *, first):
    tiles = sum_ref.shape[0]

    def copy_out(i):
        return pltpu.make_async_copy(sum_ref.at[i], out_ref.at[first + i], sem.at[i])

    for i in range(tiles):
        total = jnp.zeros((LA, NX), jnp.float32)
        for part in (p0, p1, p2, p3):
            codes = code_row(part[pl.ds(tiles * LA, PAD), :], i, LA)
            total = total + decode(part[pl.ds(i * LA, LA), :], codes)
        values, code = encode(total)
        sum_ref[i, pl.ds(0, LA), :] = values
        sum_ref[i, pl.ds(LA, PAD), :] = code_block([pad_row(code)])
        copy_out(i).start()
    for i in range(tiles):
        copy_out(i).wait()


def sum_x(parts, old, first, tiles_all):
    tiles = (parts[0].shape[0] - PAD) // LA
    aliases = {}
    if old is None:
        old = jnp.zeros((16, NX), jnp.int16)
    else:
        aliases = {4: 0}
    return pl.pallas_call(
        functools.partial(sum_x_kernel, first=first),
        in_specs=[pl.BlockSpec(memory_space=pltpu.VMEM)] * 4 + [pl.BlockSpec(memory_space=pl.ANY)],
        out_specs=pl.BlockSpec(memory_space=pltpu.HBM),
        out_shape=hbm((tiles_all, LA + PAD, NX), jnp.int16),
        scratch_shapes=[
            pltpu.VMEM((tiles, LA + PAD, NX), jnp.int16),
            pltpu.SemaphoreType.DMA((tiles,)),
        ],
        input_output_aliases=aliases,
        compiler_params=pltpu.CompilerParams(vmem_limit_bytes=12 * 1024 * 1024),
        name="sum_x",
    )(*parts, old)


def sum_tile_kernel(in_hbm_ref, o0, o1, o2, o3, acc_ref, in_ref, sem):
    tiles = in_ref.shape[0]

    def fetch(t):
        return pltpu.make_async_copy(in_hbm_ref.at[t], in_ref.at[t], sem.at[t])

    for t in range(tiles):
        fetch(t).start()
    acc_ref[...] = jnp.zeros(acc_ref.shape, jnp.float32)

    def body(t, carry):
        fetch(t).wait()
        table = in_ref[t, pl.ds(4 * LB, PAD), :].astype(jnp.int32).astype(jnp.float32)
        for k in range(4):
            acc_ref[pl.ds(k * LB, LB), :] += decode(
                in_ref[t, pl.ds(k * LB, LB), :], table[k : k + 1, 0:LB]
            )
        return carry

    lax.fori_loop(0, tiles, body, 0)
    for k, out in enumerate((o0, o1, o2, o3)):
        values, code = encode(acc_ref[pl.ds(k * LB, LB), :])
        out[pl.ds(0, LB), :] = values
        out[pl.ds(LB, PAD), :] = code_block([pad_row(code)])


def sum_tile(arrived):
    out_shape = (LB + PAD, NX)
    return pl.pallas_call(
        sum_tile_kernel,
        in_specs=[pl.BlockSpec(memory_space=pltpu.HBM)],
        out_shape=[jax.ShapeDtypeStruct(out_shape, jnp.int16)] * 4,
        scratch_shapes=[
            pltpu.VMEM((4 * LB, NX), jnp.float32),
            pltpu.VMEM(arrived.shape, jnp.int16),
            pltpu.SemaphoreType.DMA(arrived.shape[:1]),
        ],
        compiler_params=pltpu.CompilerParams(vmem_limit_bytes=12 * 1024 * 1024),
        name="sum_tile",
    )(in_hbm(arrived))


def plane_kernel(a_ref, b0, b1, b2, b3, stencil_ref, plane_ref, send_ref, lines_ref):
    def body(i, carry):
        codes = code_row(a_ref[i, pl.ds(LA, PAD), :], 0, LA)
        lines_ref[pl.ds(0, LA), :] += decode(a_ref[i, pl.ds(0, LA), :], codes)
        return carry

    lines_ref[pl.ds(0, LA), :] = jnp.zeros((LA, NX), jnp.float32)
    lax.fori_loop(0, a_ref.shape[0], body, 0)
    total = jnp.zeros((LB, NX), jnp.float32)
    for b in (b0, b1, b2, b3):
        total = total + decode(b[pl.ds(0, LB), :], code_row(b[pl.ds(LB, PAD), :], 0, LB))
    lines_ref[pl.ds(LA, LB), :] = total

    lines = lines_ref[...]
    high = lines.astype(jnp.bfloat16)
    rest = lines - high.astype(jnp.float32)
    mid = rest.astype(jnp.bfloat16)
    low = (rest - mid.astype(jnp.float32)).astype(jnp.bfloat16)
    plane = jnp.zeros((NY, NX), jnp.float32)
    for k in range(TAPS):
        weights = stencil_ref[:, k * NX : (k + 1) * NX]
        product = jnp.dot(high, weights, preferred_element_type=jnp.float32)
        product += jnp.dot(mid, weights, preferred_element_type=jnp.float32)
        product += jnp.dot(low, weights, preferred_element_type=jnp.float32)
        if k:
            product = pltpu.roll(product, k, 0)
        plane = plane + product
    plane_ref[...] = plane
    rows = []
    for h in range(2):
        values, code = encode(plane[h * 128 : (h + 1) * 128])
        send_ref[pl.ds(h * 128, 128), :] = values
        rows.append(code)
    send_ref[pl.ds(NY, PAD), :] = code_block([jnp.concatenate(rows, axis=1)])


def own_plane(a, bs, stencil):
    return pl.pallas_call(
        plane_kernel,
        out_shape=[
            jax.ShapeDtypeStruct((NY, NX), jnp.float32),
            jax.ShapeDtypeStruct((NY + PAD, NX), jnp.int16),
        ],
        scratch_shapes=[pltpu.VMEM((NY, NX), jnp.float32)],
        compiler_params=pltpu.CompilerParams(vmem_limit_bytes=12 * 1024 * 1024),
        name="own_plane",
    )(a, *bs, stencil)


def smooth_kernel(edge_ref, counts_ref, plane_ref, l1, l2, r1, r2, reads_ref, out_ref, back_ref):
    def halo(ref):
        table = ref[pl.ds(NY, PAD), :].astype(jnp.int32).astype(jnp.float32)
        parts = [
            decode(ref[pl.ds(h * 128, 128), :], table[0:1, h * 128 : (h + 1) * 128])
            for h in range(2)
        ]
        return jnp.concatenate(parts, axis=0)

    row = lax.broadcasted_iota(jnp.int32, (NY, NX), 0)
    col = lax.broadcasted_iota(jnp.int32, (NY, NX), 1)

    def step(below, mid, above):
        near = jnp.where(row == 0, 0.0, pltpu.roll(mid, 1, 0))
        near += jnp.where(row == NY - 1, 0.0, pltpu.roll(mid, NY - 1, 0))
        near += jnp.where(col == 0, 0.0, pltpu.roll(mid, 1, 1))
        near += jnp.where(col == NX - 1, 0.0, pltpu.roll(mid, NX - 1, 1))
        return mid + 0.15 * (near + below + above - 6.0 * mid)

    plane = plane_ref[...]
    left, right = halo(l1), halo(r1)
    lower = step(halo(l2), left, plane)
    upper = step(plane, right, halo(r2))
    lower = jnp.where(edge_ref[0] > 0, lower, 0.0)
    upper = jnp.where(edge_ref[1] > 0, upper, 0.0)
    field = step(lower, step(left, plane, right), upper).astype(jnp.bfloat16)
    out_ref[...] = field

    readers, most = reads_ref.shape
    lane = lax.broadcasted_iota(jnp.int32, (1, most), 1)
    columns = lax.broadcasted_iota(jnp.int32, (most, NY), 1).astype(jnp.float32)
    for t in range(readers):
        ids = jnp.where(lane < counts_ref[t], reads_ref[pl.ds(t, 1), :], -1)
        hot = jnp.where(columns == to_column(ids.astype(jnp.float32)), 1.0, 0.0)
        lines = jnp.dot(hot.astype(jnp.bfloat16), field, preferred_element_type=jnp.float32)
        back_ref[t] = lines.astype(jnp.bfloat16)


def smooth(edges, counts, plane, halos, reads):
    vmem = pl.BlockSpec(memory_space=pltpu.VMEM)
    smem = pl.BlockSpec(memory_space=pltpu.SMEM)
    readers, most = reads.shape
    return pl.pallas_call(
        smooth_kernel,
        in_specs=[smem, smem] + [vmem] * 6,
        out_specs=[vmem, vmem],
        out_shape=[
            jax.ShapeDtypeStruct((NY, NX), jnp.bfloat16),
            jax.ShapeDtypeStruct((readers, most, NX), jnp.bfloat16),
        ],
        compiler_params=pltpu.CompilerParams(vmem_limit_bytes=12 * 1024 * 1024),
        name="smooth",
    )(edges, counts, plane, *halos, reads)


def after_kernel(x_ref, *refs):
    del x_ref, refs


def after(x, others):
    anywhere = pl.BlockSpec(memory_space=pl.ANY)
    return pl.pallas_call(
        after_kernel,
        in_specs=[anywhere] * (1 + len(others)),
        out_specs=anywhere,
        out_shape=hbm(x.shape, x.dtype),
        input_output_aliases={0: 0},
        name="after",
    )(x, *others)


def local(acquired, stencil, send_slots, send_lines, send_counts, return_slots, return_counts):
    tile_count = lax.axis_size("tile")
    cut_count = lax.axis_size("cuts")
    tile_half = tile_count // 2
    here = lax.axis_index("cuts")
    here_x = here // 2
    here_core = here % 2
    place = jnp.stack([here_core, here_x]).astype(jnp.int32)
    counts = send_counts[0]
    swap = [(i, i ^ 1) for i in range(cut_count)]

    rows, peer_rows = [], []
    for h in range(2):
        source, slots = (wide, places) if h else (acquired, send_slots[0])
        made = gather_rows(source, slots, counts, send_lines[0], h * tile_half, tile_half)
        if not h:
            made, wide, places = made
        rows.append(made)
        peer_rows.append(lax.ppermute(rows[h], "cuts", swap))
    cap = send_slots.shape[2]
    peer_counts = [
        (part[:, cap + 7, 0].astype(jnp.float32) * 64 + part[:, cap + 15, 0].astype(jnp.float32))
        .astype(jnp.int32)
        for part in peer_rows
    ]

    def x_send(block, k):
        return lax.ppermute(block, "cuts", [(i, (i + 2 * k) % cut_count) for i in range(cut_count)])

    b_blocks = None
    a_parts = []
    for h in range(2):
        *a_blocks, b_blocks = line_blocks(
            rows[h], peer_rows[h], counts, peer_counts[h], place,
            b_blocks, h * tile_half, tile_count,
        )
        a_parts.append([a_blocks[0]] + [x_send(a_blocks[k], k) for k in (1, 2, 3)])
    near = [a_parts[0][1][:16] | a_parts[0][3][:16]]
    b_blocks = after(b_blocks, near)
    b_arrived = lax.all_to_all(b_blocks, "tile", split_axis=0, concat_axis=0, tiled=True)
    a_sums = None
    for h in range(2):
        a_sums = sum_x(a_parts[h], a_sums, h * tile_half, tile_count)
    a_arrived = lax.all_to_all(a_sums, "tile", split_axis=0, concat_axis=0, tiled=True)
    b_sums = sum_tile(b_arrived)
    b_final = [b_sums[0]] + [x_send(b_sums[k], k) for k in (1, 2, 3)]
    plane, coded = own_plane(a_arrived, b_final, stencil)

    total = cut_count * tile_count

    def plane_send(k):
        pairs = [(i, i + k) for i in range(total) if 0 <= i + k < total]
        return lax.ppermute(coded, ("cuts", "tile"), pairs)

    halos = [plane_send(1), plane_send(2), plane_send(-1), plane_send(-2)]
    spot = here * tile_count + lax.axis_index("tile")
    edges = jnp.stack([spot > 0, spot < total - 1]).astype(jnp.int32)
    field, outgoing = smooth(edges, return_counts[0], plane, halos, return_slots[0])
    returned = lax.all_to_all(outgoing, "tile", split_axis=0, concat_axis=0, tiled=True)
    return field[None], pltpu.with_memory_space_constraint(returned, pltpu.HBM)


def solution(mesh):
    in_specs = (
        P(("cuts", "tile"), None),
        P("tile", None),
        P(("cuts", "tile"), None, None),
        P(("cuts", "tile"), None, None),
        P(("cuts", "tile"), None),
        P(("cuts", "tile"), None, None),
        P(("cuts", "tile"), None),
    )
    out_specs = (P(("cuts", "tile"), None, None), P(("cuts", "tile"), None, None))
    return jax.shard_map(local, mesh=mesh, in_specs=in_specs, out_specs=out_specs, check_vma=False)
```

```python
import functools
import math

import jax
import jax.numpy as jnp
from jax import lax
from jax.experimental import pallas as pl
from jax.experimental.pallas import tpu as pltpu
from jax.sharding import PartitionSpec as P

NX = 256
NY = 256
TAPS = 4
LA = 144
LB = NY - LA
ALPHA = math.log(2.0) / 64.0
TOP = 32700.0
CHUNK = 256
PICK = 64
PAD = 8


def params(mib):
    return pltpu.CompilerParams(
        vmem_limit_bytes=mib * 1024 * 1024, dimension_semantics=("arbitrary",)
    )


def hbm(shape, dtype):
    return pltpu.HBM(shape, dtype)


def in_hbm(x):
    return pltpu.with_memory_space_constraint(x, pltpu.HBM)


def encode(block):
    top = to_row(jnp.max(jnp.abs(block), axis=1, keepdims=True))
    code = jnp.ceil(jnp.log(jnp.maximum(top, 1e-33)) * (1.0 / ALPHA))
    factor = to_column(TOP / jnp.exp(code * ALPHA))
    values = (block * factor + 12582912.0) - 12582912.0
    return values.astype(jnp.int32).astype(jnp.int16), code


def eye(size):
    return lax.broadcasted_iota(jnp.int32, (size, size), 0) == lax.broadcasted_iota(
        jnp.int32, (size, size), 1
    )


def to_row(column):
    return jnp.sum(jnp.where(eye(column.shape[0]), column, 0.0), axis=0, keepdims=True)


def to_column(row):
    return jnp.sum(jnp.where(eye(row.shape[1]), row, 0.0), axis=1, keepdims=True)


def decode(values, code_row):
    scale = jnp.exp(code_row * ALPHA) * (1.0 / TOP)
    return values.astype(jnp.int32).astype(jnp.float32) * to_column(scale)


def code_block(rows):
    block = jnp.zeros((PAD, NX), jnp.float32)
    index = lax.broadcasted_iota(jnp.int32, (PAD, NX), 0)
    for i, row in enumerate(rows):
        block = jnp.where(index == i, row, block)
    return block.astype(jnp.int32).astype(jnp.int16)


def widen_kernel(acq_ref, wide_ref, half_ref, sem, meanwhile):
    pieces = sem.shape[0]
    piece = half_ref.shape[0] // pieces
    copies = []
    for k in range(pieces):
        span = pl.ds(k * piece, piece)
        copies.append(pltpu.make_async_copy(acq_ref.at[span, :], half_ref.at[span, :], sem.at[k]))
        copies[k].start()
    meanwhile()
    for k in range(pieces):
        copies[k].wait()

        def widen(i, carry):
            span = pl.ds(pl.multiple_of(k * piece + i * CHUNK, CHUNK), CHUNK)
            x = half_ref[span, :].astype(jnp.float32)
            for g in range(CHUNK // 8):
                for c in range(2):
                    place = pl.multiple_of((k * piece + i * CHUNK) * 2 + (2 * g + c) * 8, 8)
                    wide_ref[pl.ds(place, 8), :] = x[g * 8 : g * 8 + 8, c * 128 : c * 128 + 128]
            return carry

        lax.fori_loop(0, piece // CHUNK, widen, 0)


def first_gather_kernel(
    counts_ref, acq_ref, lines_hbm, slots_hbm, out_ref, wide_ref, places_ref,
    lines_ref, half_ref, sem, line_sem, slots_ref, slot_sem, **sizes,
):
    fetch = pltpu.make_async_copy(lines_hbm, lines_ref, line_sem)

    @pl.when(pl.program_id(0) == 0)
    def _():
        def slots_meanwhile():
            to_places(slots_hbm, places_ref, slot_sem)
            slots_of(places_ref, slots_ref, slot_sem, 0, **sizes).start()

        fetch.start()
        widen_kernel(acq_ref, wide_ref, half_ref, sem, slots_meanwhile)

    gather_tile(
        fetch, places_ref, slots_ref, slot_sem, counts_ref, lines_ref, out_ref, wide_ref, **sizes
    )


def next_gather_kernel(
    counts_ref, wide_ref, lines_hbm, places_ref, out_ref, lines_ref, line_sem, slots_ref, slot_sem,
    **sizes,
):
    fetch = pltpu.make_async_copy(lines_hbm, lines_ref, line_sem)

    @pl.when(pl.program_id(0) == 0)
    def _():
        fetch.start()
        slots_of(places_ref, slots_ref, slot_sem, 0, **sizes).start()

    gather_tile(
        fetch, places_ref, slots_ref, slot_sem, counts_ref, lines_ref, out_ref, wide_ref, **sizes
    )


def to_places(slots_hbm, places_ref, slot_sem):
    fetch = pltpu.make_async_copy(slots_hbm, places_ref, slot_sem.at[0])
    fetch.start()
    fetch.wait()
    slots = places_ref[...]
    places_ref[...] = slots + (slots & ~7)


def slots_of(places_ref, slots_ref, slot_sem, tile, *, first, cap):
    side = lax.rem(tile, 2)
    return pltpu.make_async_copy(
        places_ref.at[first + tile], slots_ref.at[pl.ds(side * cap, cap)], slot_sem.at[side]
    )


def gather_tile(
    fetch, places_ref, slots_ref, slot_sem, counts_ref, lines_ref, out_ref, wide_ref, *, first, cap
):
    step = pl.program_id(0)

    @pl.when(step + 1 < pl.num_programs(0))
    def _():
        slots_of(places_ref, slots_ref, slot_sem, step + 1, first=first, cap=cap).start()

    slots_of(places_ref, slots_ref, slot_sem, step, first=first, cap=cap).wait()
    count = counts_ref[first + step]
    start = lax.rem(step, 2) * cap

    def pick(i, carry):
        base = pl.multiple_of(i * PICK, PICK)
        places = [slots_ref[start + base + u] for u in range(PICK)]
        for c in range(2):
            rows = [wide_ref[pl.ds(place + 8 * c, 1), :] for place in places]
            rows = jnp.concatenate(rows, axis=0).astype(jnp.bfloat16)
            out_ref[0, pl.ds(base, PICK), c * 128 : c * 128 + 128] = rows
        return carry

    def clear(i, carry):
        base = pl.multiple_of(i * PICK, PICK)
        out_ref[0, pl.ds(base, PICK), :] = jnp.zeros((PICK, NX), jnp.bfloat16)
        return carry

    picks = (count + PICK - 1) // PICK
    lax.fori_loop(0, picks, pick, 0)
    lax.fori_loop(picks, (count + CHUNK - 1) // CHUNK * (CHUNK // PICK), clear, 0)

    @pl.when(step == 0)
    def _():
        fetch.wait()

    ids = lines_ref[pl.ds(first + step, 1), :]
    position = lax.broadcasted_iota(jnp.int32, ids.shape, 1)
    ids = jnp.where(position < count, ids + 1, 0)
    index = lax.broadcasted_iota(jnp.int32, (8, NX), 0)
    table = jnp.where(index == 7, count, 0)
    for i in range(cap // CHUNK):
        table = jnp.where(index == i, ids[:, i * CHUNK : (i + 1) * CHUNK], table)
    both = jnp.concatenate([table >> 6, table & 63], axis=0)
    out_ref[0, pl.ds(cap, 16), :] = both.astype(jnp.float32).astype(jnp.bfloat16)


def gather_rows(source, slots, counts, lines, first, tiles):
    cap = lines.shape[1]
    rows_spec = pl.BlockSpec((1, cap + 16, NX), lambda t, c: (t, 0, 0))
    rows_shape = hbm((tiles, cap + 16, NX), jnp.bfloat16)
    line_scratch = [pltpu.VMEM(lines.shape, jnp.int32)]
    line_sem = [pltpu.SemaphoreType.DMA]
    whole = pl.BlockSpec(memory_space=pltpu.VMEM)
    if first:
        body = next_gather_kernel
        source = pltpu.with_memory_space_constraint(source, pltpu.VMEM)
        slots = pltpu.with_memory_space_constraint(slots, pltpu.VMEM)
        source_spec, slots_spec = whole, whole
        out_specs, out_shape = rows_spec, rows_shape
        scratch = line_scratch + line_sem
    else:
        body = first_gather_kernel
        source = pltpu.with_memory_space_constraint(source, pltpu.HBM)
        slots = in_hbm(slots)
        source_spec = slots_spec = pl.BlockSpec(memory_space=pltpu.HBM)
        out_specs = [rows_spec, whole, whole]
        out_shape = [
            rows_shape,
            pltpu.VMEM((source.shape[0] * 2, 128), jnp.float32),
            pltpu.VMEM(slots.shape, jnp.int32),
        ]
        scratch = (
            line_scratch
            + [pltpu.VMEM(source.shape, jnp.bfloat16), pltpu.SemaphoreType.DMA((8,))]
            + line_sem
        )
    return pl.pallas_call(
        functools.partial(body, first=first, cap=cap),
        grid_spec=pltpu.PrefetchScalarGridSpec(
            num_scalar_prefetch=1,
            grid=(tiles,),
            in_specs=[source_spec, pl.BlockSpec(memory_space=pltpu.HBM), slots_spec],
            out_specs=out_specs,
            scratch_shapes=scratch
            + [
                pltpu.SMEM((2 * cap,), jnp.int32),
                pltpu.SemaphoreType.DMA((2,)),
            ],
        ),
        out_shape=out_shape,
        compiler_params=params(14),
        cost_estimate=pl.CostEstimate(flops=0, transcendentals=0, bytes_accessed=40_000_000),
        name="gather_rows",
    )(counts, source, in_hbm(lines), slots)


def lines_kernel(
    own_n, peer_n, place_ref, own_hbm, peer_hbm, alias_ref,
    a0_ref, a1_ref, a2_ref, a3_ref, b_ref,
    acc_ref, code_ref, rows_ref, ids_ref, sem, *, first, cap,
):
    step = pl.program_id(0)
    last = pl.num_programs(0) - 1
    most = cap // CHUNK

    def chunks(tile):
        return (own_n[first + tile] + CHUNK - 1) // CHUNK, (peer_n[tile] + CHUNK - 1) // CHUNK

    def for_copies(tile, act):
        slot = lax.rem(tile, 2)
        own, peer = chunks(tile)
        for j, (source, base, count) in enumerate(((own_hbm, 0, own), (peer_hbm, own, peer))):
            for i in range(most):
                copy = pltpu.make_async_copy(
                    source.at[tile, pl.ds(i * CHUNK, CHUNK), :],
                    rows_ref.at[slot, pl.ds(pl.multiple_of((base + i) * CHUNK, CHUNK), CHUNK), :],
                    sem.at[slot, j * (most + 1) + i],
                )

                @pl.when(i < count)
                def _():
                    act(copy)

            act(
                pltpu.make_async_copy(
                    source.at[tile, pl.ds(cap, 16), :],
                    ids_ref.at[slot, j],
                    sem.at[slot, j * (most + 1) + most],
                )
            )

    @pl.when(step == 0)
    def _():
        for_copies(0, lambda copy: copy.start())

    @pl.when(step < last)
    def _():
        for_copies(step + 1, lambda copy: copy.start())

    for_copies(step, lambda copy: copy.wait())

    slot = lax.rem(step, 2)
    own, peer = chunks(step)
    here_core, here_x = place_ref[0], place_ref[1]
    for j in range(2):
        pair = ids_ref[slot, j].astype(jnp.float32).astype(jnp.int32)
        line = pair[0:8] * 64 + pair[8:16] - 1
        cut = line >> 8
        y = line & (NY - 1)
        mine = (line >= 0) & ((cut & 1) == here_core)
        ahead = ((cut >> 1) - here_x) & 3
        target = jnp.where(y < LA, ahead * LA + y, 4 * LA + ahead * LB + y - LA)
        target = jnp.where(mine, target, -1)
        for i in range(most):
            spot = i if j == 0 else own + i
            code_ref[4, pl.ds(spot, 1), :] = target[i : i + 1].astype(jnp.float32)

    position = lax.broadcasted_iota(jnp.int32, (CHUNK, CHUNK), 0).astype(jnp.float32)

    def add(start, width, first_group=False):
        rows = rows_ref[slot, pl.ds(pl.multiple_of(start * CHUNK, CHUNK), width * CHUNK), :]
        ids = [code_ref[4, pl.ds(start + i, 1), :] for i in range(width)]
        for m in range(acc_ref.shape[0] // CHUNK):
            hot = [
                jnp.where(position == row - m * CHUNK, 1.0, 0.0).astype(jnp.bfloat16) for row in ids
            ]
            hot = jnp.concatenate(hot, axis=1) if width > 1 else hot[0]
            span = pl.ds(m * CHUNK, CHUNK)
            product = jnp.dot(hot, rows, preferred_element_type=jnp.float32)
            acc_ref[span, :] = product if first_group else acc_ref[span, :] + product

    total = own + peer
    head = lax.rem(total - 1, 4) + 1
    for width in (1, 2, 3, 4):

        @pl.when(head == width)
        def _():
            add(0, width, first_group=True)

    def four(i, carry):
        add(head + i * 4, 4)
        return carry

    lax.fori_loop(0, (total - head) // 4, four, 0)

    outs = (a0_ref, a1_ref, a2_ref, a3_ref)
    for k in range(4):
        values, code = encode(acc_ref[pl.ds(k * LA, LA), :])
        outs[k][pl.ds(pl.multiple_of(step * LA, LA), LA), :] = values
        code_ref[k, pl.ds(step, 1), :] = pad_row(code)

    codes = []
    for k in range(4):
        values, code = encode(acc_ref[pl.ds(4 * LA + k * LB, LB), :])
        b_ref[0, pl.ds(k * LB, LB), :] = values
        codes.append(pad_row(code))
    b_ref[0, pl.ds(4 * LB, PAD), :] = code_block(codes)

    @pl.when(step == last)
    def _():
        for k in range(4):
            outs[k][pl.ds((last + 1) * LA, PAD), :] = code_ref[k, 0:PAD].astype(jnp.int32).astype(jnp.int16)


def pad_row(row):
    return jnp.concatenate([row, jnp.zeros((1, NX - row.shape[1]), jnp.float32)], axis=1)


def line_blocks(own_rows, peer_rows, own_n, peer_n, place, b_old, first, tiles_all):
    tiles, cap, _ = own_rows.shape
    cap -= 16
    a_shape = (tiles * LA + PAD, NX)
    own_rows = pltpu.with_memory_space_constraint(own_rows, pltpu.HBM)
    peer_rows = pltpu.with_memory_space_constraint(peer_rows, pltpu.HBM)
    args = [own_n, peer_n, place, own_rows, peer_rows]
    aliases = {}
    if b_old is None:
        b_old = jnp.zeros((16, NX), jnp.int16)
    else:
        aliases = {5: 4}
    args.append(b_old)
    return pl.pallas_call(
        functools.partial(lines_kernel, first=first, cap=cap),
        grid_spec=pltpu.PrefetchScalarGridSpec(
            num_scalar_prefetch=3,
            grid=(tiles,),
            in_specs=[pl.BlockSpec(memory_space=pltpu.HBM)] * 2
            + [pl.BlockSpec(memory_space=pl.ANY)],
            out_specs=[pl.BlockSpec(a_shape, lambda t, *_: (0, 0))] * 4
            + [pl.BlockSpec((1, 4 * LB + PAD, NX), lambda t, *_: (t + first, 0, 0))],
            scratch_shapes=[
                pltpu.VMEM((4 * NY, NX), jnp.float32),
                pltpu.VMEM((5, 16, NX), jnp.float32),
                pltpu.VMEM((2, 2 * cap, NX), jnp.bfloat16),
                pltpu.VMEM((2, 2, 16, NX), jnp.bfloat16),
                pltpu.SemaphoreType.DMA((2, 2 * (cap // CHUNK + 1))),
            ],
        ),
        out_shape=[hbm(a_shape, jnp.int16)] * 4
        + [hbm((tiles_all, 4 * LB + PAD, NX), jnp.int16)],
        input_output_aliases=aliases,
        compiler_params=params(16),
        cost_estimate=pl.CostEstimate(
            flops=2 * 1024 * 256 * 20480, transcendentals=0, bytes_accessed=40_000_000
        ),
        name="line_blocks",
    )(*args)


def code_row(block, index, length):
    table = block.astype(jnp.int32).astype(jnp.float32)
    rows = lax.broadcasted_iota(jnp.int32, table.shape, 0)
    row = jnp.sum(jnp.where(rows == index, table, 0.0), axis=0, keepdims=True)
    return row[:, 0:length]


def sum_x_kernel(p0, p1, p2, p3, alias_ref, out_ref, sum_ref, sem, *, first):
    tiles = sum_ref.shape[0]

    def copy_out(i):
        return pltpu.make_async_copy(sum_ref.at[i], out_ref.at[first + i], sem.at[i])

    for i in range(tiles):
        total = jnp.zeros((LA, NX), jnp.float32)
        for part in (p0, p1, p2, p3):
            codes = code_row(part[pl.ds(tiles * LA, PAD), :], i, LA)
            total = total + decode(part[pl.ds(i * LA, LA), :], codes)
        values, code = encode(total)
        sum_ref[i, pl.ds(0, LA), :] = values
        sum_ref[i, pl.ds(LA, PAD), :] = code_block([pad_row(code)])
        copy_out(i).start()
    for i in range(tiles):
        copy_out(i).wait()


def sum_x(parts, old, first, tiles_all):
    tiles = (parts[0].shape[0] - PAD) // LA
    aliases = {}
    if old is None:
        old = jnp.zeros((16, NX), jnp.int16)
    else:
        aliases = {4: 0}
    return pl.pallas_call(
        functools.partial(sum_x_kernel, first=first),
        in_specs=[pl.BlockSpec(memory_space=pltpu.VMEM)] * 4 + [pl.BlockSpec(memory_space=pl.ANY)],
        out_specs=pl.BlockSpec(memory_space=pltpu.HBM),
        out_shape=hbm((tiles_all, LA + PAD, NX), jnp.int16),
        scratch_shapes=[
            pltpu.VMEM((tiles, LA + PAD, NX), jnp.int16),
            pltpu.SemaphoreType.DMA((tiles,)),
        ],
        input_output_aliases=aliases,
        compiler_params=pltpu.CompilerParams(vmem_limit_bytes=12 * 1024 * 1024),
        name="sum_x",
    )(*parts, old)


def sum_tile_kernel(in_hbm_ref, o0, o1, o2, o3, acc_ref, in_ref, sem):
    tiles = in_ref.shape[0]

    def fetch(t):
        return pltpu.make_async_copy(in_hbm_ref.at[t], in_ref.at[t], sem.at[t])

    for t in range(tiles):
        fetch(t).start()
    acc_ref[...] = jnp.zeros(acc_ref.shape, jnp.float32)

    def body(t, carry):
        fetch(t).wait()
        table = in_ref[t, pl.ds(4 * LB, PAD), :].astype(jnp.int32).astype(jnp.float32)
        for k in range(4):
            acc_ref[pl.ds(k * LB, LB), :] += decode(
                in_ref[t, pl.ds(k * LB, LB), :], table[k : k + 1, 0:LB]
            )
        return carry

    lax.fori_loop(0, tiles, body, 0)
    for k, out in enumerate((o0, o1, o2, o3)):
        values, code = encode(acc_ref[pl.ds(k * LB, LB), :])
        out[pl.ds(0, LB), :] = values
        out[pl.ds(LB, PAD), :] = code_block([pad_row(code)])


def sum_tile(arrived):
    out_shape = (LB + PAD, NX)
    return pl.pallas_call(
        sum_tile_kernel,
        in_specs=[pl.BlockSpec(memory_space=pltpu.HBM)],
        out_shape=[jax.ShapeDtypeStruct(out_shape, jnp.int16)] * 4,
        scratch_shapes=[
            pltpu.VMEM((4 * LB, NX), jnp.float32),
            pltpu.VMEM(arrived.shape, jnp.int16),
            pltpu.SemaphoreType.DMA(arrived.shape[:1]),
        ],
        compiler_params=pltpu.CompilerParams(vmem_limit_bytes=12 * 1024 * 1024),
        name="sum_tile",
    )(in_hbm(arrived))


def plane_kernel(a_ref, b0, b1, b2, b3, stencil_ref, plane_ref, send_ref, lines_ref):
    def body(i, carry):
        codes = code_row(a_ref[i, pl.ds(LA, PAD), :], 0, LA)
        lines_ref[pl.ds(0, LA), :] += decode(a_ref[i, pl.ds(0, LA), :], codes)
        return carry

    lines_ref[pl.ds(0, LA), :] = jnp.zeros((LA, NX), jnp.float32)
    lax.fori_loop(0, a_ref.shape[0], body, 0)
    total = jnp.zeros((LB, NX), jnp.float32)
    for b in (b0, b1, b2, b3):
        total = total + decode(b[pl.ds(0, LB), :], code_row(b[pl.ds(LB, PAD), :], 0, LB))
    lines_ref[pl.ds(LA, LB), :] = total

    lines = lines_ref[...]
    high = lines.astype(jnp.bfloat16)
    rest = lines - high.astype(jnp.float32)
    mid = rest.astype(jnp.bfloat16)
    low = (rest - mid.astype(jnp.float32)).astype(jnp.bfloat16)
    plane = jnp.zeros((NY, NX), jnp.float32)
    for k in range(TAPS):
        weights = stencil_ref[:, k * NX : (k + 1) * NX]
        product = jnp.dot(high, weights, preferred_element_type=jnp.float32)
        product += jnp.dot(mid, weights, preferred_element_type=jnp.float32)
        product += jnp.dot(low, weights, preferred_element_type=jnp.float32)
        if k:
            product = pltpu.roll(product, k, 0)
        plane = plane + product
    plane_ref[...] = plane
    rows = []
    for h in range(2):
        values, code = encode(plane[h * 128 : (h + 1) * 128])
        send_ref[pl.ds(h * 128, 128), :] = values
        rows.append(code)
    send_ref[pl.ds(NY, PAD), :] = code_block([jnp.concatenate(rows, axis=1)])


def own_plane(a, bs, stencil):
    return pl.pallas_call(
        plane_kernel,
        out_shape=[
            jax.ShapeDtypeStruct((NY, NX), jnp.float32),
            jax.ShapeDtypeStruct((NY + PAD, NX), jnp.int16),
        ],
        scratch_shapes=[pltpu.VMEM((NY, NX), jnp.float32)],
        compiler_params=pltpu.CompilerParams(vmem_limit_bytes=12 * 1024 * 1024),
        name="own_plane",
    )(a, *bs, stencil)


def smooth_kernel(edge_ref, counts_ref, plane_ref, l1, l2, r1, r2, reads_ref, out_ref, back_ref):
    def halo(ref):
        table = ref[pl.ds(NY, PAD), :].astype(jnp.int32).astype(jnp.float32)
        parts = [
            decode(ref[pl.ds(h * 128, 128), :], table[0:1, h * 128 : (h + 1) * 128])
            for h in range(2)
        ]
        return jnp.concatenate(parts, axis=0)

    row = lax.broadcasted_iota(jnp.int32, (NY, NX), 0)
    col = lax.broadcasted_iota(jnp.int32, (NY, NX), 1)

    def step(below, mid, above):
        near = jnp.where(row == 0, 0.0, pltpu.roll(mid, 1, 0))
        near += jnp.where(row == NY - 1, 0.0, pltpu.roll(mid, NY - 1, 0))
        near += jnp.where(col == 0, 0.0, pltpu.roll(mid, 1, 1))
        near += jnp.where(col == NX - 1, 0.0, pltpu.roll(mid, NX - 1, 1))
        return mid + 0.15 * (near + below + above - 6.0 * mid)

    plane = plane_ref[...]
    left, right = halo(l1), halo(r1)
    lower = step(halo(l2), left, plane)
    upper = step(plane, right, halo(r2))
    lower = jnp.where(edge_ref[0] > 0, lower, 0.0)
    upper = jnp.where(edge_ref[1] > 0, upper, 0.0)
    field = step(lower, step(left, plane, right), upper).astype(jnp.bfloat16)
    out_ref[...] = field

    readers, most = reads_ref.shape
    lane = lax.broadcasted_iota(jnp.int32, (1, most), 1)
    columns = lax.broadcasted_iota(jnp.int32, (most, NY), 1).astype(jnp.float32)
    for t in range(readers):
        ids = jnp.where(lane < counts_ref[t], reads_ref[pl.ds(t, 1), :], -1)
        hot = jnp.where(columns == to_column(ids.astype(jnp.float32)), 1.0, 0.0)
        lines = jnp.dot(hot.astype(jnp.bfloat16), field, preferred_element_type=jnp.float32)
        back_ref[t] = lines.astype(jnp.bfloat16)


def smooth(edges, counts, plane, halos, reads):
    vmem = pl.BlockSpec(memory_space=pltpu.VMEM)
    smem = pl.BlockSpec(memory_space=pltpu.SMEM)
    readers, most = reads.shape
    return pl.pallas_call(
        smooth_kernel,
        in_specs=[smem, smem] + [vmem] * 6,
        out_specs=[vmem, vmem],
        out_shape=[
            jax.ShapeDtypeStruct((NY, NX), jnp.bfloat16),
            jax.ShapeDtypeStruct((readers, most, NX), jnp.bfloat16),
        ],
        compiler_params=pltpu.CompilerParams(vmem_limit_bytes=12 * 1024 * 1024),
        name="smooth",
    )(edges, counts, plane, *halos, reads)


def after_kernel(x_ref, *refs):
    del x_ref, refs


def after(x, others):
    anywhere = pl.BlockSpec(memory_space=pl.ANY)
    return pl.pallas_call(
        after_kernel,
        in_specs=[anywhere] * (1 + len(others)),
        out_specs=anywhere,
        out_shape=hbm(x.shape, x.dtype),
        input_output_aliases={0: 0},
        name="after",
    )(x, *others)


def local(acquired, stencil, send_slots, send_lines, send_counts, return_slots, return_counts):
    tile_count = lax.axis_size("tile")
    cut_count = lax.axis_size("cuts")
    tile_half = tile_count // 2
    here = lax.axis_index("cuts")
    here_x = here // 2
    here_core = here % 2
    place = jnp.stack([here_core, here_x]).astype(jnp.int32)
    counts = send_counts[0]
    swap = [(i, i ^ 1) for i in range(cut_count)]

    rows, peer_rows = [], []
    for h in range(2):
        source, slots = (wide, places) if h else (acquired, send_slots[0])
        made = gather_rows(source, slots, counts, send_lines[0], h * tile_half, tile_half)
        if not h:
            made, wide, places = made
        rows.append(made)
        peer_rows.append(lax.ppermute(rows[h], "cuts", swap))
    cap = send_slots.shape[2]
    peer_counts = [
        (part[:, cap + 7, 0].astype(jnp.float32) * 64 + part[:, cap + 15, 0].astype(jnp.float32))
        .astype(jnp.int32)
        for part in peer_rows
    ]

    def x_send(block, k):
        return lax.ppermute(block, "cuts", [(i, (i + 2 * k) % cut_count) for i in range(cut_count)])

    b_blocks = None
    a_parts = []
    for h in range(2):
        *a_blocks, b_blocks = line_blocks(
            rows[h], peer_rows[h], counts, peer_counts[h], place,
            b_blocks, h * tile_half, tile_count,
        )
        a_parts.append([a_blocks[0]] + [x_send(a_blocks[k], k) for k in (1, 2, 3)])
    near = [a_parts[0][1][:16] | a_parts[0][3][:16]]
    b_blocks = after(b_blocks, near)
    b_arrived = lax.all_to_all(b_blocks, "tile", split_axis=0, concat_axis=0, tiled=True)
    a_sums = None
    for h in range(2):
        a_sums = sum_x(a_parts[h], a_sums, h * tile_half, tile_count)
    a_arrived = lax.all_to_all(a_sums, "tile", split_axis=0, concat_axis=0, tiled=True)
    b_sums = sum_tile(b_arrived)
    b_final = [b_sums[0]] + [x_send(b_sums[k], k) for k in (1, 2, 3)]
    plane, coded = own_plane(a_arrived, b_final, stencil)

    total = cut_count * tile_count

    def plane_send(k):
        pairs = [(i, i + k) for i in range(total) if 0 <= i + k < total]
        return lax.ppermute(coded, ("cuts", "tile"), pairs)

    halos = [plane_send(1), plane_send(2), plane_send(-1), plane_send(-2)]
    spot = here * tile_count + lax.axis_index("tile")
    edges = jnp.stack([spot > 0, spot < total - 1]).astype(jnp.int32)
    field, outgoing = smooth(edges, return_counts[0], plane, halos, return_slots[0])
    returned = lax.all_to_all(outgoing, "tile", split_axis=0, concat_axis=0, tiled=True)
    return field[None], pltpu.with_memory_space_constraint(returned, pltpu.HBM)


def solution(mesh):
    in_specs = (
        P(("cuts", "tile"), None),
        P("tile", None),
        P(("cuts", "tile"), None, None),
        P(("cuts", "tile"), None, None),
        P(("cuts", "tile"), None),
        P(("cuts", "tile"), None, None),
        P(("cuts", "tile"), None),
    )
    out_specs = (P(("cuts", "tile"), None, None), P(("cuts", "tile"), None, None))
    return jax.shard_map(local, mesh=mesh, in_specs=in_specs, out_specs=out_specs, check_vma=False)
```

```python
import functools
import math

import jax
import jax.numpy as jnp
from jax import lax
from jax.experimental import pallas as pl
from jax.experimental.pallas import tpu as pltpu
from jax.sharding import PartitionSpec as P

NX = 256
NY = 256
TAPS = 4
LA = 160
LB = NY - LA
ALPHA = math.log(2.0) / 64.0
TOP = 32700.0
CHUNK = 256
PICK = 64
PAD = 8


def params(mib):
    return pltpu.CompilerParams(
        vmem_limit_bytes=mib * 1024 * 1024, dimension_semantics=("arbitrary",)
    )


def hbm(shape, dtype):
    return pltpu.HBM(shape, dtype)


def in_hbm(x):
    return pltpu.with_memory_space_constraint(x, pltpu.HBM)


def encode(block):
    top = to_row(jnp.max(jnp.abs(block), axis=1, keepdims=True))
    code = jnp.ceil(jnp.log(jnp.maximum(top, 1e-33)) * (1.0 / ALPHA))
    factor = to_column(TOP / jnp.exp(code * ALPHA))
    values = (block * factor + 12582912.0) - 12582912.0
    return values.astype(jnp.int32).astype(jnp.int16), code


def eye(size):
    return lax.broadcasted_iota(jnp.int32, (size, size), 0) == lax.broadcasted_iota(
        jnp.int32, (size, size), 1
    )


def to_row(column):
    return jnp.sum(jnp.where(eye(column.shape[0]), column, 0.0), axis=0, keepdims=True)


def to_column(row):
    return jnp.sum(jnp.where(eye(row.shape[1]), row, 0.0), axis=1, keepdims=True)


def decode(values, code_row):
    scale = jnp.exp(code_row * ALPHA) * (1.0 / TOP)
    return values.astype(jnp.int32).astype(jnp.float32) * to_column(scale)


def code_block(rows):
    block = jnp.zeros((PAD, NX), jnp.float32)
    index = lax.broadcasted_iota(jnp.int32, (PAD, NX), 0)
    for i, row in enumerate(rows):
        block = jnp.where(index == i, row, block)
    return block.astype(jnp.int32).astype(jnp.int16)


def widen_kernel(acq_ref, wide_ref, half_ref, sem, meanwhile):
    pieces = sem.shape[0]
    piece = half_ref.shape[0] // pieces
    copies = []
    for k in range(pieces):
        span = pl.ds(k * piece, piece)
        copies.append(pltpu.make_async_copy(acq_ref.at[span, :], half_ref.at[span, :], sem.at[k]))
        copies[k].start()
    meanwhile()
    for k in range(pieces):
        copies[k].wait()

        def widen(i, carry):
            span = pl.ds(pl.multiple_of(k * piece + i * CHUNK, CHUNK), CHUNK)
            x = half_ref[span, :].astype(jnp.float32)
            for g in range(CHUNK // 8):
                for c in range(2):
                    place = pl.multiple_of((k * piece + i * CHUNK) * 2 + (2 * g + c) * 8, 8)
                    wide_ref[pl.ds(place, 8), :] = x[g * 8 : g * 8 + 8, c * 128 : c * 128 + 128]
            return carry

        lax.fori_loop(0, piece // CHUNK, widen, 0)


def first_gather_kernel(
    counts_ref, acq_ref, lines_hbm, slots_hbm, out_ref, wide_ref, places_ref,
    lines_ref, half_ref, sem, line_sem, slots_ref, slot_sem, **sizes,
):
    fetch = pltpu.make_async_copy(lines_hbm, lines_ref, line_sem)

    @pl.when(pl.program_id(0) == 0)
    def _():
        def slots_meanwhile():
            to_places(slots_hbm, places_ref, slot_sem)
            slots_of(places_ref, slots_ref, slot_sem, 0, **sizes).start()

        fetch.start()
        widen_kernel(acq_ref, wide_ref, half_ref, sem, slots_meanwhile)

    gather_tile(
        fetch, places_ref, slots_ref, slot_sem, counts_ref, lines_ref, out_ref, wide_ref, **sizes
    )


def next_gather_kernel(
    counts_ref, wide_ref, lines_hbm, places_ref, out_ref, lines_ref, line_sem, slots_ref, slot_sem,
    **sizes,
):
    fetch = pltpu.make_async_copy(lines_hbm, lines_ref, line_sem)

    @pl.when(pl.program_id(0) == 0)
    def _():
        fetch.start()
        slots_of(places_ref, slots_ref, slot_sem, 0, **sizes).start()

    gather_tile(
        fetch, places_ref, slots_ref, slot_sem, counts_ref, lines_ref, out_ref, wide_ref, **sizes
    )


def to_places(slots_hbm, places_ref, slot_sem):
    fetch = pltpu.make_async_copy(slots_hbm, places_ref, slot_sem.at[0])
    fetch.start()
    fetch.wait()
    slots = places_ref[...]
    places_ref[...] = slots + (slots & ~7)


def slots_of(places_ref, slots_ref, slot_sem, tile, *, first, cap):
    side = lax.rem(tile, 2)
    return pltpu.make_async_copy(
        places_ref.at[first + tile], slots_ref.at[pl.ds(side * cap, cap)], slot_sem.at[side]
    )


def gather_tile(
    fetch, places_ref, slots_ref, slot_sem, counts_ref, lines_ref, out_ref, wide_ref, *, first, cap
):
    step = pl.program_id(0)

    @pl.when(step + 1 < pl.num_programs(0))
    def _():
        slots_of(places_ref, slots_ref, slot_sem, step + 1, first=first, cap=cap).start()

    slots_of(places_ref, slots_ref, slot_sem, step, first=first, cap=cap).wait()
    count = counts_ref[first + step]
    start = lax.rem(step, 2) * cap

    def pick(i, carry):
        base = pl.multiple_of(i * PICK, PICK)
        places = [slots_ref[start + base + u] for u in range(PICK)]
        for c in range(2):
            rows = [wide_ref[pl.ds(place + 8 * c, 1), :] for place in places]
            rows = jnp.concatenate(rows, axis=0).astype(jnp.bfloat16)
            out_ref[0, pl.ds(base, PICK), c * 128 : c * 128 + 128] = rows
        return carry

    def clear(i, carry):
        base = pl.multiple_of(i * PICK, PICK)
        out_ref[0, pl.ds(base, PICK), :] = jnp.zeros((PICK, NX), jnp.bfloat16)
        return carry

    picks = (count + PICK - 1) // PICK
    lax.fori_loop(0, picks, pick, 0)
    lax.fori_loop(picks, (count + CHUNK - 1) // CHUNK * (CHUNK // PICK), clear, 0)

    @pl.when(step == 0)
    def _():
        fetch.wait()

    ids = lines_ref[pl.ds(first + step, 1), :]
    position = lax.broadcasted_iota(jnp.int32, ids.shape, 1)
    ids = jnp.where(position < count, ids + 1, 0)
    index = lax.broadcasted_iota(jnp.int32, (8, NX), 0)
    table = jnp.where(index == 7, count, 0)
    for i in range(cap // CHUNK):
        table = jnp.where(index == i, ids[:, i * CHUNK : (i + 1) * CHUNK], table)
    both = jnp.concatenate([table >> 6, table & 63], axis=0)
    out_ref[0, pl.ds(cap, 16), :] = both.astype(jnp.float32).astype(jnp.bfloat16)


def gather_rows(source, slots, counts, lines, first, tiles):
    cap = lines.shape[1]
    rows_spec = pl.BlockSpec((1, cap + 16, NX), lambda t, c: (t, 0, 0))
    rows_shape = hbm((tiles, cap + 16, NX), jnp.bfloat16)
    line_scratch = [pltpu.VMEM(lines.shape, jnp.int32)]
    line_sem = [pltpu.SemaphoreType.DMA]
    whole = pl.BlockSpec(memory_space=pltpu.VMEM)
    if first:
        body = next_gather_kernel
        source = pltpu.with_memory_space_constraint(source, pltpu.VMEM)
        slots = pltpu.with_memory_space_constraint(slots, pltpu.VMEM)
        source_spec, slots_spec = whole, whole
        out_specs, out_shape = rows_spec, rows_shape
        scratch = line_scratch + line_sem
    else:
        body = first_gather_kernel
        source = pltpu.with_memory_space_constraint(source, pltpu.HBM)
        slots = in_hbm(slots)
        source_spec = slots_spec = pl.BlockSpec(memory_space=pltpu.HBM)
        out_specs = [rows_spec, whole, whole]
        out_shape = [
            rows_shape,
            pltpu.VMEM((source.shape[0] * 2, 128), jnp.float32),
            pltpu.VMEM(slots.shape, jnp.int32),
        ]
        scratch = (
            line_scratch
            + [pltpu.VMEM(source.shape, jnp.bfloat16), pltpu.SemaphoreType.DMA((8,))]
            + line_sem
        )
    return pl.pallas_call(
        functools.partial(body, first=first, cap=cap),
        grid_spec=pltpu.PrefetchScalarGridSpec(
            num_scalar_prefetch=1,
            grid=(tiles,),
            in_specs=[source_spec, pl.BlockSpec(memory_space=pltpu.HBM), slots_spec],
            out_specs=out_specs,
            scratch_shapes=scratch
            + [
                pltpu.SMEM((2 * cap,), jnp.int32),
                pltpu.SemaphoreType.DMA((2,)),
            ],
        ),
        out_shape=out_shape,
        compiler_params=params(14),
        cost_estimate=pl.CostEstimate(flops=0, transcendentals=0, bytes_accessed=40_000_000),
        name="gather_rows",
    )(counts, source, in_hbm(lines), slots)


def lines_kernel(
    own_n, peer_n, place_ref, own_hbm, peer_hbm, alias_ref,
    a0_ref, a1_ref, a2_ref, a3_ref, b_ref,
    acc_ref, code_ref, rows_ref, ids_ref, sem, *, first, cap,
):
    step = pl.program_id(0)
    last = pl.num_programs(0) - 1
    most = cap // CHUNK

    def chunks(tile):
        return (own_n[first + tile] + CHUNK - 1) // CHUNK, (peer_n[tile] + CHUNK - 1) // CHUNK

    def for_copies(tile, act):
        slot = lax.rem(tile, 2)
        own, peer = chunks(tile)
        for j, (source, base, count) in enumerate(((own_hbm, 0, own), (peer_hbm, own, peer))):
            for i in range(most):
                copy = pltpu.make_async_copy(
                    source.at[tile, pl.ds(i * CHUNK, CHUNK), :],
                    rows_ref.at[slot, pl.ds(pl.multiple_of((base + i) * CHUNK, CHUNK), CHUNK), :],
                    sem.at[slot, j * (most + 1) + i],
                )

                @pl.when(i < count)
                def _():
                    act(copy)

            act(
                pltpu.make_async_copy(
                    source.at[tile, pl.ds(cap, 16), :],
                    ids_ref.at[slot, j],
                    sem.at[slot, j * (most + 1) + most],
                )
            )

    @pl.when(step == 0)
    def _():
        for_copies(0, lambda copy: copy.start())

    @pl.when(step < last)
    def _():
        for_copies(step + 1, lambda copy: copy.start())

    for_copies(step, lambda copy: copy.wait())

    slot = lax.rem(step, 2)
    own, peer = chunks(step)
    here_core, here_x = place_ref[0], place_ref[1]
    for j in range(2):
        pair = ids_ref[slot, j].astype(jnp.float32).astype(jnp.int32)
        line = pair[0:8] * 64 + pair[8:16] - 1
        cut = line >> 8
        y = line & (NY - 1)
        mine = (line >= 0) & ((cut & 1) == here_core)
        ahead = ((cut >> 1) - here_x) & 3
        target = jnp.where(y < LA, ahead * LA + y, 4 * LA + ahead * LB + y - LA)
        target = jnp.where(mine, target, -1)
        for i in range(most):
            spot = i if j == 0 else own + i
            code_ref[4, pl.ds(spot, 1), :] = target[i : i + 1].astype(jnp.float32)

    position = lax.broadcasted_iota(jnp.int32, (CHUNK, CHUNK), 0).astype(jnp.float32)

    def add(start, width, first_group=False):
        rows = rows_ref[slot, pl.ds(pl.multiple_of(start * CHUNK, CHUNK), width * CHUNK), :]
        ids = [code_ref[4, pl.ds(start + i, 1), :] for i in range(width)]
        for m in range(acc_ref.shape[0] // CHUNK):
            hot = [
                jnp.where(position == row - m * CHUNK, 1.0, 0.0).astype(jnp.bfloat16) for row in ids
            ]
            hot = jnp.concatenate(hot, axis=1) if width > 1 else hot[0]
            span = pl.ds(m * CHUNK, CHUNK)
            product = jnp.dot(hot, rows, preferred_element_type=jnp.float32)
            acc_ref[span, :] = product if first_group else acc_ref[span, :] + product

    total = own + peer
    head = lax.rem(total - 1, 4) + 1
    for width in (1, 2, 3, 4):

        @pl.when(head == width)
        def _():
            add(0, width, first_group=True)

    def four(i, carry):
        add(head + i * 4, 4)
        return carry

    lax.fori_loop(0, (total - head) // 4, four, 0)

    outs = (a0_ref, a1_ref, a2_ref, a3_ref)
    for k in range(4):
        values, code = encode(acc_ref[pl.ds(k * LA, LA), :])
        outs[k][pl.ds(pl.multiple_of(step * LA, LA), LA), :] = values
        code_ref[k, pl.ds(step, 1), :] = pad_row(code)

    codes = []
    for k in range(4):
        values, code = encode(acc_ref[pl.ds(4 * LA + k * LB, LB), :])
        b_ref[0, pl.ds(k * LB, LB), :] = values
        codes.append(pad_row(code))
    b_ref[0, pl.ds(4 * LB, PAD), :] = code_block(codes)

    @pl.when(step == last)
    def _():
        for k in range(4):
            outs[k][pl.ds((last + 1) * LA, PAD), :] = code_ref[k, 0:PAD].astype(jnp.int32).astype(jnp.int16)


def pad_row(row):
    return jnp.concatenate([row, jnp.zeros((1, NX - row.shape[1]), jnp.float32)], axis=1)


def line_blocks(own_rows, peer_rows, own_n, peer_n, place, b_old, first, tiles_all):
    tiles, cap, _ = own_rows.shape
    cap -= 16
    a_shape = (tiles * LA + PAD, NX)
    own_rows = pltpu.with_memory_space_constraint(own_rows, pltpu.HBM)
    peer_rows = pltpu.with_memory_space_constraint(peer_rows, pltpu.HBM)
    args = [own_n, peer_n, place, own_rows, peer_rows]
    aliases = {}
    if b_old is None:
        b_old = jnp.zeros((16, NX), jnp.int16)
    else:
        aliases = {5: 4}
    args.append(b_old)
    return pl.pallas_call(
        functools.partial(lines_kernel, first=first, cap=cap),
        grid_spec=pltpu.PrefetchScalarGridSpec(
            num_scalar_prefetch=3,
            grid=(tiles,),
            in_specs=[pl.BlockSpec(memory_space=pltpu.HBM)] * 2
            + [pl.BlockSpec(memory_space=pl.ANY)],
            out_specs=[pl.BlockSpec(a_shape, lambda t, *_: (0, 0))] * 4
            + [pl.BlockSpec((1, 4 * LB + PAD, NX), lambda t, *_: (t + first, 0, 0))],
            scratch_shapes=[
                pltpu.VMEM((4 * NY, NX), jnp.float32),
                pltpu.VMEM((5, 16, NX), jnp.float32),
                pltpu.VMEM((2, 2 * cap, NX), jnp.bfloat16),
                pltpu.VMEM((2, 2, 16, NX), jnp.bfloat16),
                pltpu.SemaphoreType.DMA((2, 2 * (cap // CHUNK + 1))),
            ],
        ),
        out_shape=[hbm(a_shape, jnp.int16)] * 4
        + [hbm((tiles_all, 4 * LB + PAD, NX), jnp.int16)],
        input_output_aliases=aliases,
        compiler_params=params(16),
        cost_estimate=pl.CostEstimate(
            flops=2 * 1024 * 256 * 20480, transcendentals=0, bytes_accessed=40_000_000
        ),
        name="line_blocks",
    )(*args)


def code_row(block, index, length):
    table = block.astype(jnp.int32).astype(jnp.float32)
    rows = lax.broadcasted_iota(jnp.int32, table.shape, 0)
    row = jnp.sum(jnp.where(rows == index, table, 0.0), axis=0, keepdims=True)
    return row[:, 0:length]


def sum_x_kernel(*refs, first, parts, early):
    part_refs, early_ref = refs[:parts], refs[parts]
    out_ref, sum_ref, sem = refs[parts + 1 + early :]
    tiles = sum_ref.shape[0]

    def copy_out(i):
        return pltpu.make_async_copy(sum_ref.at[i], out_ref.at[first + i], sem.at[i])

    for i in range(tiles):
        total = early_ref[i] if early else jnp.zeros((LA, NX), jnp.float32)
        for part in part_refs:
            codes = code_row(part[pl.ds(tiles * LA, PAD), :], i, LA)
            total = total + decode(part[pl.ds(i * LA, LA), :], codes)
        values, code = encode(total)
        sum_ref[i, pl.ds(0, LA), :] = values
        sum_ref[i, pl.ds(LA, PAD), :] = code_block([pad_row(code)])
        copy_out(i).start()
    for i in range(tiles):
        copy_out(i).wait()


def sum_x(parts, old, first, tiles_all, early=None):
    tiles = (parts[0].shape[0] - PAD) // LA
    args = list(parts) + ([] if early is None else [early])
    aliases = {} if old is None else {len(args): 0}
    if old is None:
        old = jnp.zeros((16, NX), jnp.int16)
    return pl.pallas_call(
        functools.partial(
            sum_x_kernel, first=first, parts=len(parts), early=int(early is not None)
        ),
        in_specs=[pl.BlockSpec(memory_space=pltpu.VMEM)] * len(args)
        + [pl.BlockSpec(memory_space=pl.ANY)],
        out_specs=pl.BlockSpec(memory_space=pltpu.HBM),
        out_shape=hbm((tiles_all, LA + PAD, NX), jnp.int16),
        scratch_shapes=[
            pltpu.VMEM((tiles, LA + PAD, NX), jnp.int16),
            pltpu.SemaphoreType.DMA((tiles,)),
        ],
        input_output_aliases=aliases,
        compiler_params=pltpu.CompilerParams(vmem_limit_bytes=12 * 1024 * 1024),
        name="sum_x",
    )(*args, old)


def add_x_kernel(p0, p1, p2, out_ref):
    tiles = out_ref.shape[0]
    for i in range(tiles):
        total = jnp.zeros((LA, NX), jnp.float32)
        for part in (p0, p1, p2):
            codes = code_row(part[pl.ds(tiles * LA, PAD), :], i, LA)
            total = total + decode(part[pl.ds(i * LA, LA), :], codes)
        out_ref[i] = total


def add_x(parts):
    tiles = (parts[0].shape[0] - PAD) // LA
    return pl.pallas_call(
        add_x_kernel,
        out_shape=jax.ShapeDtypeStruct((tiles, LA, NX), jnp.float32),
        compiler_params=pltpu.CompilerParams(vmem_limit_bytes=12 * 1024 * 1024),
        name="add_x",
    )(*parts)


def sum_tile_kernel(in_hbm_ref, o0, o1, o2, o3, acc_ref, in_ref, sem):
    tiles = in_ref.shape[0]

    def fetch(t):
        return pltpu.make_async_copy(in_hbm_ref.at[t], in_ref.at[t], sem.at[t])

    for t in range(tiles):
        fetch(t).start()
    acc_ref[...] = jnp.zeros(acc_ref.shape, jnp.float32)

    def body(t, carry):
        fetch(t).wait()
        table = in_ref[t, pl.ds(4 * LB, PAD), :].astype(jnp.int32).astype(jnp.float32)
        for k in range(4):
            acc_ref[pl.ds(k * LB, LB), :] += decode(
                in_ref[t, pl.ds(k * LB, LB), :], table[k : k + 1, 0:LB]
            )
        return carry

    lax.fori_loop(0, tiles, body, 0)
    for k, out in enumerate((o0, o1, o2, o3)):
        values, code = encode(acc_ref[pl.ds(k * LB, LB), :])
        out[pl.ds(0, LB), :] = values
        out[pl.ds(LB, PAD), :] = code_block([pad_row(code)])


def sum_tile(arrived):
    out_shape = (LB + PAD, NX)
    return pl.pallas_call(
        sum_tile_kernel,
        in_specs=[pl.BlockSpec(memory_space=pltpu.HBM)],
        out_shape=[jax.ShapeDtypeStruct(out_shape, jnp.int16)] * 4,
        scratch_shapes=[
            pltpu.VMEM((4 * LB, NX), jnp.float32),
            pltpu.VMEM(arrived.shape, jnp.int16),
            pltpu.SemaphoreType.DMA(arrived.shape[:1]),
        ],
        compiler_params=pltpu.CompilerParams(vmem_limit_bytes=12 * 1024 * 1024),
        name="sum_tile",
    )(in_hbm(arrived))


def plane_kernel(a_ref, b0, b1, b2, b3, stencil_ref, plane_ref, send_ref, lines_ref):
    def body(i, carry):
        codes = code_row(a_ref[i, pl.ds(LA, PAD), :], 0, LA)
        lines_ref[pl.ds(0, LA), :] += decode(a_ref[i, pl.ds(0, LA), :], codes)
        return carry

    lines_ref[pl.ds(0, LA), :] = jnp.zeros((LA, NX), jnp.float32)
    lax.fori_loop(0, a_ref.shape[0], body, 0)
    total = jnp.zeros((LB, NX), jnp.float32)
    for b in (b0, b1, b2, b3):
        total = total + decode(b[pl.ds(0, LB), :], code_row(b[pl.ds(LB, PAD), :], 0, LB))
    lines_ref[pl.ds(LA, LB), :] = total

    lines = lines_ref[...]
    high = lines.astype(jnp.bfloat16)
    rest = lines - high.astype(jnp.float32)
    mid = rest.astype(jnp.bfloat16)
    low = (rest - mid.astype(jnp.float32)).astype(jnp.bfloat16)
    plane = jnp.zeros((NY, NX), jnp.float32)
    for k in range(TAPS):
        weights = stencil_ref[:, k * NX : (k + 1) * NX]
        product = jnp.dot(high, weights, preferred_element_type=jnp.float32)
        product += jnp.dot(mid, weights, preferred_element_type=jnp.float32)
        product += jnp.dot(low, weights, preferred_element_type=jnp.float32)
        if k:
            product = pltpu.roll(product, k, 0)
        plane = plane + product
    plane_ref[...] = plane
    rows = []
    for h in range(2):
        values, code = encode(plane[h * 128 : (h + 1) * 128])
        send_ref[pl.ds(h * 128, 128), :] = values
        rows.append(code)
    send_ref[pl.ds(NY, PAD), :] = code_block([jnp.concatenate(rows, axis=1)])


def own_plane(a, bs, stencil):
    return pl.pallas_call(
        plane_kernel,
        out_shape=[
            jax.ShapeDtypeStruct((NY, NX), jnp.float32),
            jax.ShapeDtypeStruct((NY + PAD, NX), jnp.int16),
        ],
        scratch_shapes=[pltpu.VMEM((NY, NX), jnp.float32)],
        compiler_params=pltpu.CompilerParams(vmem_limit_bytes=12 * 1024 * 1024),
        name="own_plane",
    )(a, *bs, stencil)


def smooth_kernel(edge_ref, counts_ref, plane_ref, l1, l2, r1, r2, reads_ref, out_ref, back_ref):
    def halo(ref):
        table = ref[pl.ds(NY, PAD), :].astype(jnp.int32).astype(jnp.float32)
        parts = [
            decode(ref[pl.ds(h * 128, 128), :], table[0:1, h * 128 : (h + 1) * 128])
            for h in range(2)
        ]
        return jnp.concatenate(parts, axis=0)

    row = lax.broadcasted_iota(jnp.int32, (NY, NX), 0)
    col = lax.broadcasted_iota(jnp.int32, (NY, NX), 1)

    def step(below, mid, above):
        near = jnp.where(row == 0, 0.0, pltpu.roll(mid, 1, 0))
        near += jnp.where(row == NY - 1, 0.0, pltpu.roll(mid, NY - 1, 0))
        near += jnp.where(col == 0, 0.0, pltpu.roll(mid, 1, 1))
        near += jnp.where(col == NX - 1, 0.0, pltpu.roll(mid, NX - 1, 1))
        return mid + 0.15 * (near + below + above - 6.0 * mid)

    plane = plane_ref[...]
    left, right = halo(l1), halo(r1)
    lower = step(halo(l2), left, plane)
    upper = step(plane, right, halo(r2))
    lower = jnp.where(edge_ref[0] > 0, lower, 0.0)
    upper = jnp.where(edge_ref[1] > 0, upper, 0.0)
    field = step(lower, step(left, plane, right), upper).astype(jnp.bfloat16)
    out_ref[...] = field

    readers, most = reads_ref.shape
    lane = lax.broadcasted_iota(jnp.int32, (1, most), 1)
    columns = lax.broadcasted_iota(jnp.int32, (most, NY), 1).astype(jnp.float32)
    for t in range(readers):
        ids = jnp.where(lane < counts_ref[t], reads_ref[pl.ds(t, 1), :], -1)
        hot = jnp.where(columns == to_column(ids.astype(jnp.float32)), 1.0, 0.0)
        lines = jnp.dot(hot.astype(jnp.bfloat16), field, preferred_element_type=jnp.float32)
        back_ref[t] = lines.astype(jnp.bfloat16)


def smooth(edges, counts, plane, halos, reads):
    vmem = pl.BlockSpec(memory_space=pltpu.VMEM)
    smem = pl.BlockSpec(memory_space=pltpu.SMEM)
    readers, most = reads.shape
    return pl.pallas_call(
        smooth_kernel,
        in_specs=[smem, smem] + [vmem] * 6,
        out_specs=[vmem, vmem],
        out_shape=[
            jax.ShapeDtypeStruct((NY, NX), jnp.bfloat16),
            jax.ShapeDtypeStruct((readers, most, NX), jnp.bfloat16),
        ],
        compiler_params=pltpu.CompilerParams(vmem_limit_bytes=12 * 1024 * 1024),
        name="smooth",
    )(edges, counts, plane, *halos, reads)


def after_kernel(x_ref, *refs):
    del x_ref, refs


def after(x, others):
    anywhere = pl.BlockSpec(memory_space=pl.ANY)
    return pl.pallas_call(
        after_kernel,
        in_specs=[anywhere] * (1 + len(others)),
        out_specs=anywhere,
        out_shape=hbm(x.shape, x.dtype),
        input_output_aliases={0: 0},
        name="after",
    )(x, *others)


def local(acquired, stencil, send_slots, send_lines, send_counts, return_slots, return_counts):
    tile_count = lax.axis_size("tile")
    cut_count = lax.axis_size("cuts")
    tile_half = tile_count // 2
    here = lax.axis_index("cuts")
    here_x = here // 2
    here_core = here % 2
    place = jnp.stack([here_core, here_x]).astype(jnp.int32)
    counts = send_counts[0]
    swap = [(i, i ^ 1) for i in range(cut_count)]

    rows, peer_rows = [], []
    for h in range(2):
        source, slots = (wide, places) if h else (acquired, send_slots[0])
        made = gather_rows(source, slots, counts, send_lines[0], h * tile_half, tile_half)
        if not h:
            made, wide, places = made
        rows.append(made)
        peer_rows.append(lax.ppermute(rows[h], "cuts", swap))
    cap = send_slots.shape[2]
    peer_counts = [
        (part[:, cap + 7, 0].astype(jnp.float32) * 64 + part[:, cap + 15, 0].astype(jnp.float32))
        .astype(jnp.int32)
        for part in peer_rows
    ]

    def x_send(block, k):
        return lax.ppermute(block, "cuts", [(i, (i + 2 * k) % cut_count) for i in range(cut_count)])

    b_blocks = None
    a_parts = []
    for h in range(2):
        *a_blocks, b_blocks = line_blocks(
            rows[h], peer_rows[h], counts, peer_counts[h], place,
            b_blocks, h * tile_half, tile_count,
        )
        a_parts.append([a_blocks[0]] + [x_send(a_blocks[k], k) for k in (1, 2, 3)])
    near = [a_parts[0][1][:16] | a_parts[0][3][:16]]
    b_blocks = after(b_blocks, near)
    b_arrived = lax.all_to_all(b_blocks, "tile", split_axis=0, concat_axis=0, tiled=True)
    a_sums = sum_x(a_parts[0], None, 0, tile_count)
    own_block, ahead, far, behind = a_parts[1]
    early = add_x([own_block, ahead, behind])
    a_sums = sum_x([far], a_sums, tile_half, tile_count, early)
    a_arrived = lax.all_to_all(a_sums, "tile", split_axis=0, concat_axis=0, tiled=True)
    b_sums = sum_tile(b_arrived)
    b_final = [b_sums[0]] + [x_send(b_sums[k], k) for k in (1, 2, 3)]
    plane, coded = own_plane(a_arrived, b_final, stencil)

    total = cut_count * tile_count

    def plane_send(k):
        pairs = [(i, i + k) for i in range(total) if 0 <= i + k < total]
        return lax.ppermute(coded, ("cuts", "tile"), pairs)

    halos = [plane_send(1), plane_send(2), plane_send(-1), plane_send(-2)]
    spot = here * tile_count + lax.axis_index("tile")
    edges = jnp.stack([spot > 0, spot < total - 1]).astype(jnp.int32)
    field, outgoing = smooth(edges, return_counts[0], plane, halos, return_slots[0])
    returned = lax.all_to_all(outgoing, "tile", split_axis=0, concat_axis=0, tiled=True)
    return field[None], returned


def solution(mesh):
    in_specs = (
        P(("cuts", "tile"), None),
        P("tile", None),
        P(("cuts", "tile"), None, None),
        P(("cuts", "tile"), None, None),
        P(("cuts", "tile"), None),
        P(("cuts", "tile"), None, None),
        P(("cuts", "tile"), None),
    )
    out_specs = (P(("cuts", "tile"), None, None), P(("cuts", "tile"), None, None))
    return jax.shard_map(local, mesh=mesh, in_specs=in_specs, out_specs=out_specs, check_vma=False)
```

```python
import functools
import math

import jax
import jax.numpy as jnp
from jax import lax
from jax.experimental import pallas as pl
from jax.experimental.pallas import tpu as pltpu
from jax.sharding import PartitionSpec as P

NX = 256
NY = 256
TAPS = 4
LA = 160
LB = NY - LA
ALPHA = math.log(2.0) / 64.0
TOP = 32700.0
CHUNK = 256
PICK = 64
PAD = 8


def params(mib):
    return pltpu.CompilerParams(
        vmem_limit_bytes=mib * 1024 * 1024, dimension_semantics=("arbitrary",)
    )


def hbm(shape, dtype):
    return pltpu.HBM(shape, dtype)


def in_hbm(x):
    return pltpu.with_memory_space_constraint(x, pltpu.HBM)


def encode(block):
    top = to_row(jnp.max(jnp.abs(block), axis=1, keepdims=True))
    code = jnp.ceil(jnp.log(jnp.maximum(top, 1e-33)) * (1.0 / ALPHA))
    factor = to_column(TOP / jnp.exp(code * ALPHA))
    values = (block * factor + 12582912.0) - 12582912.0
    return values.astype(jnp.int32).astype(jnp.int16), code


def eye(size):
    return lax.broadcasted_iota(jnp.int32, (size, size), 0) == lax.broadcasted_iota(
        jnp.int32, (size, size), 1
    )


def to_row(column):
    return jnp.sum(jnp.where(eye(column.shape[0]), column, 0.0), axis=0, keepdims=True)


def to_column(row):
    return jnp.sum(jnp.where(eye(row.shape[1]), row, 0.0), axis=1, keepdims=True)


def decode(values, code_row):
    scale = jnp.exp(code_row * ALPHA) * (1.0 / TOP)
    return values.astype(jnp.int32).astype(jnp.float32) * to_column(scale)


def code_block(rows):
    block = jnp.zeros((PAD, NX), jnp.float32)
    index = lax.broadcasted_iota(jnp.int32, (PAD, NX), 0)
    for i, row in enumerate(rows):
        block = jnp.where(index == i, row, block)
    return block.astype(jnp.int32).astype(jnp.int16)


def widen_kernel(acq_ref, wide_ref, half_ref, sem, meanwhile):
    pieces = sem.shape[0]
    piece = half_ref.shape[0] // pieces
    copies = []
    for k in range(pieces):
        span = pl.ds(k * piece, piece)
        copies.append(pltpu.make_async_copy(acq_ref.at[span, :], half_ref.at[span, :], sem.at[k]))
        copies[k].start()
    meanwhile()
    for k in range(pieces):
        copies[k].wait()

        def widen(i, carry):
            span = pl.ds(pl.multiple_of(k * piece + i * CHUNK, CHUNK), CHUNK)
            x = half_ref[span, :].astype(jnp.float32)
            for g in range(CHUNK // 8):
                for c in range(2):
                    place = pl.multiple_of((k * piece + i * CHUNK) * 2 + (2 * g + c) * 8, 8)
                    wide_ref[pl.ds(place, 8), :] = x[g * 8 : g * 8 + 8, c * 128 : c * 128 + 128]
            return carry

        lax.fori_loop(0, piece // CHUNK, widen, 0)


def first_gather_kernel(
    counts_ref, acq_ref, lines_hbm, slots_hbm, out_ref, wide_ref, places_ref,
    lines_ref, half_ref, sem, line_sem, slots_ref, slot_sem, **sizes,
):
    fetch = pltpu.make_async_copy(lines_hbm, lines_ref, line_sem)

    @pl.when(pl.program_id(0) == 0)
    def _():
        def slots_meanwhile():
            to_places(slots_hbm, places_ref, slot_sem)
            slots_of(places_ref, slots_ref, slot_sem, 0, **sizes).start()

        fetch.start()
        widen_kernel(acq_ref, wide_ref, half_ref, sem, slots_meanwhile)

    gather_tile(
        fetch, places_ref, slots_ref, slot_sem, counts_ref, lines_ref, out_ref, wide_ref, **sizes
    )


def next_gather_kernel(
    counts_ref, wide_ref, lines_hbm, places_ref, out_ref, lines_ref, line_sem, slots_ref, slot_sem,
    **sizes,
):
    fetch = pltpu.make_async_copy(lines_hbm, lines_ref, line_sem)

    @pl.when(pl.program_id(0) == 0)
    def _():
        fetch.start()
        slots_of(places_ref, slots_ref, slot_sem, 0, **sizes).start()

    gather_tile(
        fetch, places_ref, slots_ref, slot_sem, counts_ref, lines_ref, out_ref, wide_ref, **sizes
    )


def to_places(slots_hbm, places_ref, slot_sem):
    fetch = pltpu.make_async_copy(slots_hbm, places_ref, slot_sem.at[0])
    fetch.start()
    fetch.wait()
    slots = places_ref[...]
    places_ref[...] = slots + (slots & ~7)


def slots_of(places_ref, slots_ref, slot_sem, tile, *, first, cap):
    side = lax.rem(tile, 2)
    return pltpu.make_async_copy(
        places_ref.at[first + tile], slots_ref.at[pl.ds(side * cap, cap)], slot_sem.at[side]
    )


def gather_tile(
    fetch, places_ref, slots_ref, slot_sem, counts_ref, lines_ref, out_ref, wide_ref, *, first, cap
):
    step = pl.program_id(0)

    @pl.when(step + 1 < pl.num_programs(0))
    def _():
        slots_of(places_ref, slots_ref, slot_sem, step + 1, first=first, cap=cap).start()

    slots_of(places_ref, slots_ref, slot_sem, step, first=first, cap=cap).wait()
    count = counts_ref[first + step]
    start = lax.rem(step, 2) * cap

    def pick(i, carry):
        base = pl.multiple_of(i * PICK, PICK)
        places = [slots_ref[start + base + u] for u in range(PICK)]
        for c in range(2):
            rows = [wide_ref[pl.ds(place + 8 * c, 1), :] for place in places]
            rows = jnp.concatenate(rows, axis=0).astype(jnp.bfloat16)
            out_ref[0, pl.ds(base, PICK), c * 128 : c * 128 + 128] = rows
        return carry

    def clear(i, carry):
        base = pl.multiple_of(i * PICK, PICK)
        out_ref[0, pl.ds(base, PICK), :] = jnp.zeros((PICK, NX), jnp.bfloat16)
        return carry

    picks = (count + PICK - 1) // PICK
    lax.fori_loop(0, picks, pick, 0)
    lax.fori_loop(picks, (count + CHUNK - 1) // CHUNK * (CHUNK // PICK), clear, 0)

    @pl.when(step == 0)
    def _():
        fetch.wait()

    ids = lines_ref[pl.ds(first + step, 1), :]
    position = lax.broadcasted_iota(jnp.int32, ids.shape, 1)
    ids = jnp.where(position < count, ids + 1, 0)
    index = lax.broadcasted_iota(jnp.int32, (8, NX), 0)
    table = jnp.where(index == 7, count, 0)
    for i in range(cap // CHUNK):
        table = jnp.where(index == i, ids[:, i * CHUNK : (i + 1) * CHUNK], table)
    both = jnp.concatenate([table >> 6, table & 63], axis=0)
    out_ref[0, pl.ds(cap, 16), :] = both.astype(jnp.float32).astype(jnp.bfloat16)


def gather_rows(source, slots, counts, lines, first, tiles):
    cap = lines.shape[1]
    rows_spec = pl.BlockSpec((1, cap + 16, NX), lambda t, c: (t, 0, 0))
    rows_shape = hbm((tiles, cap + 16, NX), jnp.bfloat16)
    line_scratch = [pltpu.VMEM(lines.shape, jnp.int32)]
    line_sem = [pltpu.SemaphoreType.DMA]
    whole = pl.BlockSpec(memory_space=pltpu.VMEM)
    if first:
        body = next_gather_kernel
        source = pltpu.with_memory_space_constraint(source, pltpu.VMEM)
        slots = pltpu.with_memory_space_constraint(slots, pltpu.VMEM)
        source_spec, slots_spec = whole, whole
        out_specs, out_shape = rows_spec, rows_shape
        scratch = line_scratch + line_sem
    else:
        body = first_gather_kernel
        source = pltpu.with_memory_space_constraint(source, pltpu.HBM)
        slots = in_hbm(slots)
        source_spec = slots_spec = pl.BlockSpec(memory_space=pltpu.HBM)
        out_specs = [rows_spec, whole, whole]
        out_shape = [
            rows_shape,
            pltpu.VMEM((source.shape[0] * 2, 128), jnp.float32),
            pltpu.VMEM(slots.shape, jnp.int32),
        ]
        scratch = (
            line_scratch
            + [pltpu.VMEM(source.shape, jnp.bfloat16), pltpu.SemaphoreType.DMA((8,))]
            + line_sem
        )
    return pl.pallas_call(
        functools.partial(body, first=first, cap=cap),
        grid_spec=pltpu.PrefetchScalarGridSpec(
            num_scalar_prefetch=1,
            grid=(tiles,),
            in_specs=[source_spec, pl.BlockSpec(memory_space=pltpu.HBM), slots_spec],
            out_specs=out_specs,
            scratch_shapes=scratch
            + [
                pltpu.SMEM((2 * cap,), jnp.int32),
                pltpu.SemaphoreType.DMA((2,)),
            ],
        ),
        out_shape=out_shape,
        compiler_params=params(14),
        cost_estimate=pl.CostEstimate(flops=0, transcendentals=0, bytes_accessed=40_000_000),
        name="gather_rows",
    )(counts, source, in_hbm(lines), slots)


def lines_kernel(
    own_n, peer_n, place_ref, own_hbm, peer_hbm, alias_ref,
    a0_ref, a1_ref, a2_ref, a3_ref, b_ref,
    acc_ref, code_ref, rows_ref, ids_ref, sem, *, first, cap,
):
    step = pl.program_id(0)
    last = pl.num_programs(0) - 1
    most = cap // CHUNK

    def chunks(tile):
        return (own_n[first + tile] + CHUNK - 1) // CHUNK, (peer_n[tile] + CHUNK - 1) // CHUNK

    def for_copies(tile, act):
        slot = lax.rem(tile, 2)
        own, peer = chunks(tile)
        for j, (source, base, count) in enumerate(((own_hbm, 0, own), (peer_hbm, own, peer))):
            for i in range(most):
                copy = pltpu.make_async_copy(
                    source.at[tile, pl.ds(i * CHUNK, CHUNK), :],
                    rows_ref.at[slot, pl.ds(pl.multiple_of((base + i) * CHUNK, CHUNK), CHUNK), :],
                    sem.at[slot, j * (most + 1) + i],
                )

                @pl.when(i < count)
                def _():
                    act(copy)

            act(
                pltpu.make_async_copy(
                    source.at[tile, pl.ds(cap, 16), :],
                    ids_ref.at[slot, j],
                    sem.at[slot, j * (most + 1) + most],
                )
            )

    @pl.when(step == 0)
    def _():
        for_copies(0, lambda copy: copy.start())

    @pl.when(step < last)
    def _():
        for_copies(step + 1, lambda copy: copy.start())

    for_copies(step, lambda copy: copy.wait())

    slot = lax.rem(step, 2)
    own, peer = chunks(step)
    here_core, here_x = place_ref[0], place_ref[1]
    for j in range(2):
        pair = ids_ref[slot, j].astype(jnp.float32).astype(jnp.int32)
        line = pair[0:8] * 64 + pair[8:16] - 1
        cut = line >> 8
        y = line & (NY - 1)
        mine = (line >= 0) & ((cut & 1) == here_core)
        ahead = ((cut >> 1) - here_x) & 3
        target = jnp.where(y < LA, ahead * LA + y, 4 * LA + ahead * LB + y - LA)
        target = jnp.where(mine, target, -1)
        for i in range(most):
            spot = i if j == 0 else own + i
            code_ref[4, pl.ds(spot, 1), :] = target[i : i + 1].astype(jnp.float32)

    position = lax.broadcasted_iota(jnp.int32, (CHUNK, CHUNK), 0).astype(jnp.float32)

    def add(start, width, first_group=False):
        rows = rows_ref[slot, pl.ds(pl.multiple_of(start * CHUNK, CHUNK), width * CHUNK), :]
        ids = [code_ref[4, pl.ds(start + i, 1), :] for i in range(width)]
        for m in range(acc_ref.shape[0] // CHUNK):
            hot = [
                jnp.where(position == row - m * CHUNK, 1.0, 0.0).astype(jnp.bfloat16) for row in ids
            ]
            hot = jnp.concatenate(hot, axis=1) if width > 1 else hot[0]
            span = pl.ds(m * CHUNK, CHUNK)
            product = jnp.dot(hot, rows, preferred_element_type=jnp.float32)
            acc_ref[span, :] = product if first_group else acc_ref[span, :] + product

    total = own + peer
    head = lax.rem(total - 1, 4) + 1
    for width in (1, 2, 3, 4):

        @pl.when(head == width)
        def _():
            add(0, width, first_group=True)

    def four(i, carry):
        add(head + i * 4, 4)
        return carry

    lax.fori_loop(0, (total - head) // 4, four, 0)

    outs = (a0_ref, a1_ref, a2_ref, a3_ref)
    for k in range(4):
        values, code = encode(acc_ref[pl.ds(k * LA, LA), :])
        outs[k][pl.ds(pl.multiple_of(step * LA, LA), LA), :] = values
        code_ref[k, pl.ds(step, 1), :] = pad_row(code)

    codes = []
    for k in range(4):
        values, code = encode(acc_ref[pl.ds(4 * LA + k * LB, LB), :])
        b_ref[0, pl.ds(k * LB, LB), :] = values
        codes.append(pad_row(code))
    b_ref[0, pl.ds(4 * LB, PAD), :] = code_block(codes)

    @pl.when(step == last)
    def _():
        for k in range(4):
            outs[k][pl.ds((last + 1) * LA, PAD), :] = code_ref[k, 0:PAD].astype(jnp.int32).astype(jnp.int16)


def pad_row(row):
    return jnp.concatenate([row, jnp.zeros((1, NX - row.shape[1]), jnp.float32)], axis=1)


def line_blocks(own_rows, peer_rows, own_n, peer_n, place, b_old, first, tiles_all):
    tiles, cap, _ = own_rows.shape
    cap -= 16
    a_shape = (tiles * LA + PAD, NX)
    own_rows = pltpu.with_memory_space_constraint(own_rows, pltpu.HBM)
    peer_rows = pltpu.with_memory_space_constraint(peer_rows, pltpu.HBM)
    args = [own_n, peer_n, place, own_rows, peer_rows]
    aliases = {}
    if b_old is None:
        b_old = jnp.zeros((16, NX), jnp.int16)
    else:
        aliases = {5: 4}
    args.append(b_old)
    return pl.pallas_call(
        functools.partial(lines_kernel, first=first, cap=cap),
        grid_spec=pltpu.PrefetchScalarGridSpec(
            num_scalar_prefetch=3,
            grid=(tiles,),
            in_specs=[pl.BlockSpec(memory_space=pltpu.HBM)] * 2
            + [pl.BlockSpec(memory_space=pl.ANY)],
            out_specs=[pl.BlockSpec(a_shape, lambda t, *_: (0, 0))] * 4
            + [pl.BlockSpec((1, 4 * LB + PAD, NX), lambda t, *_: (t + first, 0, 0))],
            scratch_shapes=[
                pltpu.VMEM((4 * NY, NX), jnp.float32),
                pltpu.VMEM((5, 16, NX), jnp.float32),
                pltpu.VMEM((2, 2 * cap, NX), jnp.bfloat16),
                pltpu.VMEM((2, 2, 16, NX), jnp.bfloat16),
                pltpu.SemaphoreType.DMA((2, 2 * (cap // CHUNK + 1))),
            ],
        ),
        out_shape=[hbm(a_shape, jnp.int16)] * 4
        + [hbm((tiles_all, 4 * LB + PAD, NX), jnp.int16)],
        input_output_aliases=aliases,
        compiler_params=params(16),
        cost_estimate=pl.CostEstimate(
            flops=2 * 1024 * 256 * 20480, transcendentals=0, bytes_accessed=40_000_000
        ),
        name="line_blocks",
    )(*args)


def code_row(block, index, length):
    table = block.astype(jnp.int32).astype(jnp.float32)
    rows = lax.broadcasted_iota(jnp.int32, table.shape, 0)
    row = jnp.sum(jnp.where(rows == index, table, 0.0), axis=0, keepdims=True)
    return row[:, 0:length]


def sum_x_kernel(*refs, first, parts, early):
    part_refs, early_ref = refs[:parts], refs[parts]
    out_ref, sum_ref, sem = refs[parts + 1 + early :]
    tiles = sum_ref.shape[0]

    def copy_out(i):
        return pltpu.make_async_copy(sum_ref.at[i], out_ref.at[first + i], sem.at[i])

    for i in range(tiles):
        total = early_ref[i] if early else jnp.zeros((LA, NX), jnp.float32)
        for part in part_refs:
            codes = code_row(part[pl.ds(tiles * LA, PAD), :], i, LA)
            total = total + decode(part[pl.ds(i * LA, LA), :], codes)
        values, code = encode(total)
        sum_ref[i, pl.ds(0, LA), :] = values
        sum_ref[i, pl.ds(LA, PAD), :] = code_block([pad_row(code)])
        copy_out(i).start()
    for i in range(tiles):
        copy_out(i).wait()


def sum_x(parts, old, first, tiles_all, early=None):
    tiles = (parts[0].shape[0] - PAD) // LA
    args = list(parts) + ([] if early is None else [early])
    aliases = {} if old is None else {len(args): 0}
    if old is None:
        old = jnp.zeros((16, NX), jnp.int16)
    return pl.pallas_call(
        functools.partial(
            sum_x_kernel, first=first, parts=len(parts), early=int(early is not None)
        ),
        in_specs=[pl.BlockSpec(memory_space=pltpu.VMEM)] * len(args)
        + [pl.BlockSpec(memory_space=pl.ANY)],
        out_specs=pl.BlockSpec(memory_space=pltpu.HBM),
        out_shape=hbm((tiles_all, LA + PAD, NX), jnp.int16),
        scratch_shapes=[
            pltpu.VMEM((tiles, LA + PAD, NX), jnp.int16),
            pltpu.SemaphoreType.DMA((tiles,)),
        ],
        input_output_aliases=aliases,
        compiler_params=pltpu.CompilerParams(vmem_limit_bytes=12 * 1024 * 1024),
        name="sum_x",
    )(*args, old)


def add_x_kernel(p0, p1, p2, out_ref):
    tiles = out_ref.shape[0]
    for i in range(tiles):
        total = jnp.zeros((LA, NX), jnp.float32)
        for part in (p0, p1, p2):
            codes = code_row(part[pl.ds(tiles * LA, PAD), :], i, LA)
            total = total + decode(part[pl.ds(i * LA, LA), :], codes)
        out_ref[i] = total


def add_x(parts):
    tiles = (parts[0].shape[0] - PAD) // LA
    return pl.pallas_call(
        add_x_kernel,
        out_shape=jax.ShapeDtypeStruct((tiles, LA, NX), jnp.float32),
        compiler_params=pltpu.CompilerParams(vmem_limit_bytes=12 * 1024 * 1024),
        name="add_x",
    )(*parts)


def sum_tile_kernel(in_hbm_ref, o0, o1, o2, o3, acc_ref, in_ref, sem):
    tiles = in_ref.shape[0]

    def fetch(t):
        return pltpu.make_async_copy(in_hbm_ref.at[t], in_ref.at[t], sem.at[t])

    for t in range(tiles):
        fetch(t).start()
    acc_ref[...] = jnp.zeros(acc_ref.shape, jnp.float32)

    def body(t, carry):
        fetch(t).wait()
        table = in_ref[t, pl.ds(4 * LB, PAD), :].astype(jnp.int32).astype(jnp.float32)
        for k in range(4):
            acc_ref[pl.ds(k * LB, LB), :] += decode(
                in_ref[t, pl.ds(k * LB, LB), :], table[k : k + 1, 0:LB]
            )
        return carry

    lax.fori_loop(0, tiles, body, 0)
    for k, out in enumerate((o0, o1, o2, o3)):
        values, code = encode(acc_ref[pl.ds(k * LB, LB), :])
        out[pl.ds(0, LB), :] = values
        out[pl.ds(LB, PAD), :] = code_block([pad_row(code)])


def sum_tile(arrived):
    out_shape = (LB + PAD, NX)
    return pl.pallas_call(
        sum_tile_kernel,
        in_specs=[pl.BlockSpec(memory_space=pltpu.HBM)],
        out_shape=[jax.ShapeDtypeStruct(out_shape, jnp.int16)] * 4,
        scratch_shapes=[
            pltpu.VMEM((4 * LB, NX), jnp.float32),
            pltpu.VMEM(arrived.shape, jnp.int16),
            pltpu.SemaphoreType.DMA(arrived.shape[:1]),
        ],
        compiler_params=pltpu.CompilerParams(vmem_limit_bytes=12 * 1024 * 1024),
        name="sum_tile",
    )(in_hbm(arrived))


def plane_kernel(a_ref, b0, b1, b2, b3, stencil_ref, plane_ref, send_ref, lines_ref):
    def body(i, carry):
        codes = code_row(a_ref[i, pl.ds(LA, PAD), :], 0, LA)
        lines_ref[pl.ds(0, LA), :] += decode(a_ref[i, pl.ds(0, LA), :], codes)
        return carry

    lines_ref[pl.ds(0, LA), :] = jnp.zeros((LA, NX), jnp.float32)
    lax.fori_loop(0, a_ref.shape[0], body, 0)
    total = jnp.zeros((LB, NX), jnp.float32)
    for b in (b0, b1, b2, b3):
        total = total + decode(b[pl.ds(0, LB), :], code_row(b[pl.ds(LB, PAD), :], 0, LB))
    lines_ref[pl.ds(LA, LB), :] = total

    lines = lines_ref[...]
    high = lines.astype(jnp.bfloat16)
    rest = lines - high.astype(jnp.float32)
    mid = rest.astype(jnp.bfloat16)
    low = (rest - mid.astype(jnp.float32)).astype(jnp.bfloat16)
    plane = jnp.zeros((NY, NX), jnp.float32)
    for k in range(TAPS):
        weights = stencil_ref[:, k * NX : (k + 1) * NX]
        product = jnp.dot(high, weights, preferred_element_type=jnp.float32)
        product += jnp.dot(mid, weights, preferred_element_type=jnp.float32)
        product += jnp.dot(low, weights, preferred_element_type=jnp.float32)
        if k:
            product = pltpu.roll(product, k, 0)
        plane = plane + product
    plane_ref[...] = plane
    rows = []
    for h in range(2):
        values, code = encode(plane[h * 128 : (h + 1) * 128])
        send_ref[pl.ds(h * 128, 128), :] = values
        rows.append(code)
    send_ref[pl.ds(NY, PAD), :] = code_block([jnp.concatenate(rows, axis=1)])


def own_plane(a, bs, stencil):
    return pl.pallas_call(
        plane_kernel,
        out_shape=[
            jax.ShapeDtypeStruct((NY, NX), jnp.float32),
            jax.ShapeDtypeStruct((NY + PAD, NX), jnp.int16),
        ],
        scratch_shapes=[pltpu.VMEM((NY, NX), jnp.float32)],
        compiler_params=pltpu.CompilerParams(vmem_limit_bytes=12 * 1024 * 1024),
        name="own_plane",
    )(a, *bs, stencil)


def smooth_kernel(edge_ref, counts_ref, plane_ref, l2, r2, l1, r1, reads_ref, out_ref, back_ref):
    def halo(ref):
        table = ref[pl.ds(NY, PAD), :].astype(jnp.int32).astype(jnp.float32)
        parts = [
            decode(ref[pl.ds(h * 128, 128), :], table[0:1, h * 128 : (h + 1) * 128])
            for h in range(2)
        ]
        return jnp.concatenate(parts, axis=0)

    row = lax.broadcasted_iota(jnp.int32, (NY, NX), 0)
    col = lax.broadcasted_iota(jnp.int32, (NY, NX), 1)

    def step(below, mid, above):
        near = jnp.where(row == 0, 0.0, pltpu.roll(mid, 1, 0))
        near += jnp.where(row == NY - 1, 0.0, pltpu.roll(mid, NY - 1, 0))
        near += jnp.where(col == 0, 0.0, pltpu.roll(mid, 1, 1))
        near += jnp.where(col == NX - 1, 0.0, pltpu.roll(mid, NX - 1, 1))
        return mid + 0.15 * (near + below + above - 6.0 * mid)

    plane = plane_ref[...]
    left, right = halo(l1), halo(r1)
    lower = step(halo(l2), left, plane)
    upper = step(plane, right, halo(r2))
    lower = jnp.where(edge_ref[0] > 0, lower, 0.0)
    upper = jnp.where(edge_ref[1] > 0, upper, 0.0)
    field = step(lower, step(left, plane, right), upper).astype(jnp.bfloat16)
    out_ref[...] = field

    readers, most = reads_ref.shape
    lane = lax.broadcasted_iota(jnp.int32, (1, most), 1)
    columns = lax.broadcasted_iota(jnp.int32, (most, NY), 1).astype(jnp.float32)
    for t in range(readers):
        ids = jnp.where(lane < counts_ref[t], reads_ref[pl.ds(t, 1), :], -1)
        hot = jnp.where(columns == to_column(ids.astype(jnp.float32)), 1.0, 0.0)
        lines = jnp.dot(hot.astype(jnp.bfloat16), field, preferred_element_type=jnp.float32)
        back_ref[t] = lines.astype(jnp.bfloat16)


def smooth(edges, counts, plane, halos, reads):
    vmem = pl.BlockSpec(memory_space=pltpu.VMEM)
    smem = pl.BlockSpec(memory_space=pltpu.SMEM)
    readers, most = reads.shape
    return pl.pallas_call(
        smooth_kernel,
        in_specs=[smem, smem] + [vmem] * 6,
        out_specs=[vmem, vmem],
        out_shape=[
            jax.ShapeDtypeStruct((NY, NX), jnp.bfloat16),
            jax.ShapeDtypeStruct((readers, most, NX), jnp.bfloat16),
        ],
        compiler_params=pltpu.CompilerParams(vmem_limit_bytes=12 * 1024 * 1024),
        name="smooth",
    )(edges, counts, plane, *halos, reads)


def after_kernel(x_ref, *refs):
    del x_ref, refs


def after(x, others):
    anywhere = pl.BlockSpec(memory_space=pl.ANY)
    return pl.pallas_call(
        after_kernel,
        in_specs=[anywhere] * (1 + len(others)),
        out_specs=anywhere,
        out_shape=hbm(x.shape, x.dtype),
        input_output_aliases={0: 0},
        name="after",
    )(x, *others)


def local(acquired, stencil, send_slots, send_lines, send_counts, return_slots, return_counts):
    tile_count = lax.axis_size("tile")
    cut_count = lax.axis_size("cuts")
    tile_half = tile_count // 2
    here = lax.axis_index("cuts")
    here_x = here // 2
    here_core = here % 2
    place = jnp.stack([here_core, here_x]).astype(jnp.int32)
    counts = send_counts[0]
    swap = [(i, i ^ 1) for i in range(cut_count)]

    rows, peer_rows = [], []
    for h in range(2):
        source, slots = (wide, places) if h else (acquired, send_slots[0])
        made = gather_rows(source, slots, counts, send_lines[0], h * tile_half, tile_half)
        if not h:
            made, wide, places = made
        rows.append(made)
        peer_rows.append(lax.ppermute(rows[h], "cuts", swap))
    cap = send_slots.shape[2]
    peer_counts = [
        (part[:, cap + 7, 0].astype(jnp.float32) * 64 + part[:, cap + 15, 0].astype(jnp.float32))
        .astype(jnp.int32)
        for part in peer_rows
    ]

    def x_send(block, k):
        return lax.ppermute(block, "cuts", [(i, (i + 2 * k) % cut_count) for i in range(cut_count)])

    b_blocks = None
    a_parts = []
    for h in range(2):
        *a_blocks, b_blocks = line_blocks(
            rows[h], peer_rows[h], counts, peer_counts[h], place,
            b_blocks, h * tile_half, tile_count,
        )
        a_parts.append([a_blocks[0]] + [x_send(a_blocks[k], k) for k in (1, 2, 3)])
    near = [a_parts[0][1][:16] | a_parts[0][3][:16]]
    b_blocks = after(b_blocks, near)
    b_arrived = lax.all_to_all(b_blocks, "tile", split_axis=0, concat_axis=0, tiled=True)
    a_sums = sum_x(a_parts[0], None, 0, tile_count)
    own_block, ahead, across, behind = a_parts[1]
    early = add_x([own_block, ahead, behind])
    a_sums = sum_x([across], a_sums, tile_half, tile_count, early)
    a_arrived = lax.all_to_all(a_sums, "tile", split_axis=0, concat_axis=0, tiled=True)
    b_sums = sum_tile(b_arrived)
    b_final = [b_sums[0]] + [x_send(b_sums[k], k) for k in (1, 2, 3)]
    plane, coded = own_plane(a_arrived, b_final, stencil)

    total = cut_count * tile_count

    def plane_send(k):
        pairs = [(i, i + k) for i in range(total) if 0 <= i + k < total]
        return lax.ppermute(coded, ("cuts", "tile"), pairs)

    far = [plane_send(2), plane_send(-2)]
    near = [plane_send(1), plane_send(-1)]
    halos = far + near
    spot = here * tile_count + lax.axis_index("tile")
    edges = jnp.stack([spot > 0, spot < total - 1]).astype(jnp.int32)
    field, outgoing = smooth(edges, return_counts[0], plane, halos, return_slots[0])
    returned = lax.all_to_all(outgoing, "tile", split_axis=0, concat_axis=0, tiled=True)
    return field[None], returned


def solution(mesh):
    in_specs = (
        P(("cuts", "tile"), None),
        P("tile", None),
        P(("cuts", "tile"), None, None),
        P(("cuts", "tile"), None, None),
        P(("cuts", "tile"), None),
        P(("cuts", "tile"), None, None),
        P(("cuts", "tile"), None),
    )
    out_specs = (P(("cuts", "tile"), None, None), P(("cuts", "tile"), None, None))
    return jax.shard_map(local, mesh=mesh, in_specs=in_specs, out_specs=out_specs, check_vma=False)
```
